256 devices in a mesh: dp: 16 (over x, z_hi, core), seq: 16 (over y, z_lo).
Axes of the slice: x: 4, y: 4, z: 8 (z_hi: 2, z_lo: 4; z = z_hi * 4 + z_lo), core: 2. Of those that a mesh axis runs over, the one named last changes fastest.
Arguments:
- tokens: bfloat16 [16, 2048, 1024], P('dp', 'seq'), may hold values from -6 to 6
- in_gain: float32 [1024], replicated, may hold values from 0.1 to 1.9
- w_proj: bfloat16 [1024, 4096], replicated, may hold values from -0.1875 to 0.1875
- out_gain: float32 [1024], replicated, may hold values from 0.1 to 1.9
- w_out: bfloat16 [1024, 1024], replicated, may hold values from -0.1875 to 0.1875
- rab_slope: float32 [8], replicated, may hold values from -1 to 0.2
- hist_blocks: int32 [16, 3], P('dp'), may hold values from 1 to 10, 16 in all within a row
- hist_tail: int32 [16, 3], P('dp'), may hold values from 1 to 128
- node_table: bfloat16 [4096, 1024], P('dp'), may hold values from -0.1875 to 0.1875
- subtree_map: int32 [64], replicated, may hold values from 0 to 63, each once
- beam_nodes: int32 [48, 1024], P('dp', 'seq'), may hold values from 0 to 4095
Outputs:
- layer_out: bfloat16 [16, 2048, 1024], P('dp', 'seq')
- beam_scores: float32 [48, 1024], P('dp', 'seq')
The draws below stay inside these ranges and needn't reach their ends.
Inputs may be any that keep to these rules, and one draw needn't show every extreme that they name: `hist_blocks`: each row sums to 16; its largest entry is exactly 10. `subtree_map`: a permutation of 0 to 63.
All inputs are finite; a program needn't handle non-finite values.
Results may differ from the reference program's by a relative error of at most 0.0059.
Values may be sent and summed in bfloat16 or wider, within the bound.
No kernel may reach another device: no remote copies, remote signals or barrier semaphores. Data moves between devices by JAX's collectives and lax.ppermute only.
A program may use at most 128 MiB of HBM per device.

```python
import math
import jax
import jax.numpy as jnp
import numpy as np
from jax import lax

D = 1024
HEADS = 8
HD = 128
BLK = 128
SUBT = 64
USERS = 3
BEAM = 1024
TOK_DP = 2048
NBLK = 16
MOST = 10
USERS_ALL = 48
NODES = 4096
SUBTREES = 64
N_DP = 16


def draw_w_proj(key, part):
    entries = jax.random.truncated_normal(key, -6.0, 6.0, (D, 4 * D), jnp.float32)
    return (entries * D ** (-0.5)).astype(jnp.bfloat16)


def draw_rab_slope(key, part):
    return jax.random.uniform(key, (HEADS,), jnp.float32, -0.4, 0.2)


def place_ends(array, stream_key, least, top_value):
    shape = array.shape
    spot = [jax.random.randint(jax.random.fold_in(stream_key, axis), (), 0, shape[axis]) for axis in range(len(shape))]
    array = array.at[tuple(spot)].set(least)
    longest = shape.index(max(shape))
    spot[longest] = (spot[longest] + 1) % shape[longest]
    return array.at[tuple(spot)].set(top_value)


def block_scale(stream_key, shape, shards, least, top_value):
    level = 1.0
    for axis_at, parts in shards:
        steps = jax.random.uniform(jax.random.fold_in(jax.random.fold_in(stream_key, 6), axis_at), (parts,), jnp.float32, least / len(shards), top_value / len(shards))
        level = level * jnp.repeat(jnp.exp(steps), shape[axis_at] // parts).reshape((-1,) + (1,) * (len(shape) - 1 - axis_at))
    return level


def cumulative_ranks(amount, slope):
    portions = [(1 << 20) // math.isqrt(standing ** slope) + 1 for standing in range(1, amount + 1)]
    scale = 1 + sum(portions) // (1 << 30)
    return np.cumsum(np.array([max(1, weight // scale) for weight in portions]))


def ranked(key, dims, count, skew):
    listing = cumulative_ranks(count, skew)
    ticket = jax.random.randint(jax.random.fold_in(key, 1), dims, 0, int(listing[count - 1]))
    grade = jnp.searchsorted(jnp.asarray(listing, jnp.int32), ticket, side="right")
    return jax.random.permutation(jax.random.fold_in(key, 2), count)[grade].astype(jnp.int32)


def split_up(count, total, limit, skew):
    loads = [(1 << 20) // math.isqrt(standing ** skew) + 1 for standing in range(2, count + 1)]
    surplus, holding = total - limit - (count - 1), [1] * (count - 1)
    while surplus > 0:
        movable = [i for i in range(count - 1) if holding[i] < limit]
        pool, remaining = sum([loads[i] for i in movable]), surplus
        for i in movable:
            more = min(limit - holding[i], max(1, remaining * loads[i] // pool), surplus)
            holding[i] = holding[i] + more
            surplus = surplus - more
    return np.array([limit] + holding)


def uneven(stream_key, amount, total, limit, slope):
    if amount == 2:
        one = jax.random.randint(stream_key, (), max(1, total - limit), min(limit, total - 1) + 1)
        return jnp.stack([one, total - one])
    sizes = jnp.asarray(split_up(amount, total, limit, slope), jnp.int32)
    pairs = (amount - 1) // 2
    source_of, receiver = sizes[1:1 + 2 * pairs:2], sizes[2:2 + 2 * pairs:2]
    slack = jnp.minimum(source_of - 1, limit - receiver)
    shifted = jax.random.randint(jax.random.fold_in(stream_key, 1), (pairs,), 0, 1 << 20) % (slack + 1)
    sizes = sizes.at[1:1 + 2 * pairs:2].set(source_of - shifted).at[2:2 + 2 * pairs:2].set(receiver + shifted)
    return sizes[jax.random.permutation(jax.random.fold_in(stream_key, 2), amount)]


def scatter_about(rng, shape, width, reach, split=(), held_as=jnp.bfloat16):
    level = block_scale(rng, shape, split, -0.22, 0.18) if split else 1.0
    values = jax.random.normal(rng, shape, jnp.float32) * width * level
    return jnp.minimum(jnp.maximum(values, -reach), reach).astype(held_as)


def setup_inputs(seed: int = 0) -> dict:
    key_list = jax.random.split(jax.random.key(seed), 12)
    tokens = scatter_about(key_list[0], (N_DP, TOK_DP, D), 1.0, 6.0, ((0, 16), (1, 16)))
    in_gain = jnp.clip(1.0 + 0.18 * jax.random.normal(key_list[1], (D,), jnp.float32), 0.1, 1.9)
    w_proj = draw_w_proj(jax.random.fold_in(key_list[11], 71), 0)
    out_gain = jnp.clip(1.0 + 0.18 * jax.random.normal(key_list[3], (D,), jnp.float32), 0.1, 1.9)
    w_out = scatter_about(key_list[4], (D, D), D ** -0.5, 0.1875)
    rab_slope = draw_rab_slope(jax.random.fold_in(key_list[11], 71), 0)
    hist_blocks = jax.vmap(lambda own: uneven(own, USERS, NBLK, MOST, 0))(jax.random.split(key_list[6], N_DP)).reshape((N_DP, USERS)).astype(jnp.int32)
    hist_tail = place_ends(jax.random.randint(key_list[7], (N_DP, USERS), 1, BLK + 1), jax.random.fold_in(key_list[7], 1), 1, BLK).astype(jnp.int32)
    node_table = scatter_about(key_list[8], (NODES, D), D ** -0.5, 0.1875, ((0, 16),))
    subtree_map = jax.random.permutation(key_list[9], SUBTREES).astype(jnp.int32)
    beam_nodes = place_ends(ranked(key_list[10], (USERS_ALL, BEAM), NODES, 1), jax.random.fold_in(key_list[10], 3), 0, NODES - 1).astype(jnp.int32)
    return {"tokens": tokens, "in_gain": in_gain, "w_proj": w_proj, "out_gain": out_gain, "w_out": w_out, "rab_slope": rab_slope, "hist_blocks": hist_blocks, "hist_tail": hist_tail, "node_table": node_table, "subtree_map": subtree_map, "beam_nodes": beam_nodes}


def layer_norm(rows):
    centred = rows - lax.optimization_barrier(jnp.mean(rows, axis=-1, keepdims=True))
    spread = lax.optimization_barrier(jnp.mean(centred * centred, axis=-1, keepdims=True))
    return centred * lax.rsqrt(spread + 1e-05)

def user_table(blocks, tail_len):
    blocks = blocks.astype(jnp.int32)
    starts = (jnp.cumsum(blocks) - blocks).astype(jnp.int32)
    lengths = ((blocks - 1) * BLK + tail_len.astype(jnp.int32)).astype(jnp.int32)
    return (starts, lengths)

def segments(blocks, tail_len, positions):
    starts, lengths = user_table(blocks, tail_len)
    block_of = jnp.floor_divide(positions, BLK).astype(jnp.int32)
    owning = lax.optimization_barrier(jnp.sum((block_of[:, None] >= starts[None, :]).astype(jnp.int32), axis=1)) - 1
    onehot = (owning[:, None] == jnp.arange(USERS, dtype=jnp.int32)[None, :]).astype(jnp.int32)
    first_pos = lax.optimization_barrier(jnp.sum(onehot * starts[None, :], axis=1)) * BLK
    user_len = lax.optimization_barrier(jnp.sum(onehot * lengths[None, :], axis=1))
    is_live = (owning >= 0) & (positions - first_pos < user_len)
    return jnp.where(is_live, owning, -1).astype(jnp.int32)

def attend(query_rows, query_pos, query_seg, key_rows, value_rows, key_pos, key_seg, rab_slope):
    scores = jnp.einsum('qhd,khd->hqk', query_rows.astype(jnp.float32), key_rows.astype(jnp.float32))
    scores = scores * query_rows.shape[-1] ** (-0.5)
    gap = query_pos[:, None] - key_pos[None, :]
    allowed = (query_seg[:, None] == key_seg[None, :]) & (query_seg[:, None] >= 0) & (gap >= 0)
    bias = rab_slope[:, None, None] * jnp.log1p(jnp.maximum(gap, 0).astype(jnp.float32))[None]
    weights = jnp.where(allowed[None], jax.nn.silu(scores + bias), 0.0).astype(jnp.bfloat16)
    return jnp.einsum('hqk,khd->qhd', weights.astype(jnp.float32), value_rows.astype(jnp.float32))

def reference(tokens, in_gain, w_proj, out_gain, w_out, rab_slope, hist_blocks, hist_tail, node_table, subtree_map, beam_nodes):
    back = MOST * BLK
    qblock = math.gcd(512, TOK_DP)

    def one_group(item):
        x_rows, blocks, tail_len = item
        normed = (layer_norm(x_rows.astype(jnp.float32)) * in_gain).astype(jnp.bfloat16)
        proj = jax.nn.silu(jnp.dot(normed, w_proj, preferred_element_type=jnp.float32)).astype(jnp.bfloat16)
        gate_rows = proj[:, :D]
        query_rows = proj[:, D:2 * D]
        key_rows = proj[:, 2 * D:3 * D]
        value_rows = proj[:, 3 * D:]
        positions = jnp.arange(TOK_DP, dtype=jnp.int32)
        seg_all = segments(blocks, tail_len, positions)
        key_pad = jnp.concatenate([jnp.zeros((back, D), jnp.bfloat16), key_rows], axis=0)
        value_pad = jnp.concatenate([jnp.zeros((back, D), jnp.bfloat16), value_rows], axis=0)
        pos_pad = jnp.arange(-back, TOK_DP, dtype=jnp.int32)
        seg_pad = jnp.concatenate([jnp.full((back,), -1, jnp.int32), seg_all], axis=0)

        def per_block(index):
            start = (index * qblock).astype(jnp.int32)
            span = back + qblock
            queries = lax.dynamic_slice_in_dim(query_rows, start, qblock, 0).reshape(qblock, HEADS, HD)
            query_pos = lax.dynamic_slice_in_dim(positions, start, qblock, 0)
            query_seg = lax.dynamic_slice_in_dim(seg_all, start, qblock, 0)
            keys_here = lax.dynamic_slice_in_dim(key_pad, start, span, 0).reshape(span, HEADS, HD)
            values_here = lax.dynamic_slice_in_dim(value_pad, start, span, 0).reshape(span, HEADS, HD)
            key_pos = lax.dynamic_slice_in_dim(pos_pad, start, span, 0)
            key_seg = lax.dynamic_slice_in_dim(seg_pad, start, span, 0)
            return attend(queries, query_pos, query_seg, keys_here, values_here, key_pos, key_seg, rab_slope)
        mixed = lax.map(per_block, jnp.arange(TOK_DP // qblock, dtype=jnp.int32)).reshape(TOK_DP, D)
        gated = (layer_norm(mixed) * out_gain * gate_rows.astype(jnp.float32)).astype(jnp.bfloat16)
        layer_rows = (x_rows.astype(jnp.float32) + jnp.dot(gated, w_out, preferred_element_type=jnp.float32)).astype(jnp.bfloat16)
        starts, lengths = user_table(blocks, tail_len)
        last_slot = (starts * BLK + lengths - 1).astype(jnp.int32)
        states = jnp.take(layer_rows, last_slot, axis=0)
        return (layer_rows, states)
    layer_out, states = lax.map(one_group, (tokens, hist_blocks, hist_tail))
    all_states = states.reshape(USERS_ALL, D)
    stored = (jnp.take(subtree_map, beam_nodes // SUBT) * SUBT + beam_nodes % SUBT).astype(jnp.int32)

    def score_user(item):
        state_row, row_ids = item
        return jnp.dot(jnp.take(node_table, row_ids, axis=0), state_row, preferred_element_type=jnp.float32)
    beam_scores = lax.map(score_user, (all_states, stored))
    return (layer_out, beam_scores)
```

```python
import jax
import jax.numpy as jnp
from jax import lax
from jax.experimental import pallas as pl
from jax.experimental.pallas import tpu as pltpu
from jax.sharding import PartitionSpec as P

BLK = 128
SUBT = 64
USERS = 3
D = 1024
HEADS = 8
HD = 128
NSEQ = 16
HALF = BLK // 2
ROW_K, ROW_V, ROW_Q, ROW_X, ROWS_A = 0, 128, 256, 320, 336
ROWS_B = HALF + 16
MAXD = 10
UNROLL = 4
MASKED = -1e30


def silu(x):
    half = 0.5 * x
    return half + half * jnp.tanh(half)


def layer_norm(rows):
    centred = rows - jnp.mean(rows, axis=-1, keepdims=True)
    spread = jnp.mean(centred * centred, axis=-1, keepdims=True)
    return centred * lax.rsqrt(spread + 1e-05)


def user_starts(blocks_ref):
    one = blocks_ref[0, 0]
    return (0, one, one + blocks_ref[0, 1])


def project_kernel(blocks_ref, tail_ref, x_ref, gain_ref, wg_ref, wq_ref, wk_ref, wv_ref, send_ref, gate_ref, normed):
    step = pl.program_id(0)

    @pl.when(step == 0)
    def _():
        normed[...] = (layer_norm(x_ref[...].astype(jnp.float32)) * gain_ref[...]).astype(jnp.bfloat16)

    rows = normed[...]

    def part(w_ref):
        return silu(jnp.dot(rows, w_ref[...], preferred_element_type=jnp.float32)).astype(jnp.bfloat16)

    queries, keys, values = part(wq_ref), part(wk_ref), part(wv_ref)
    for head in range(2):
        cols = slice(head * HD, (head + 1) * HD)
        for half in range(2):
            to = step * 4 + head * 2 + half
            send_ref[to, ROW_K:ROW_V, :] = keys[:, cols]
            send_ref[to, ROW_V:ROW_Q, :] = values[:, cols]
            send_ref[to, ROW_Q:ROW_X, :] = queries[half * HALF : (half + 1) * HALF, cols]
    gate_ref[:, pl.ds(pl.multiple_of(step * 256, 256), 256)] = part(wg_ref)

    @pl.when(step == pl.num_programs(0) - 1)
    def _():
        me = lax.axis_index("seq")
        starts = user_starts(blocks_ref)
        last = jnp.int32(-1)
        for user in range(USERS):
            ends = starts[user] + blocks_ref[0, user] - 1 == me
            last = jnp.where(ends, tail_ref[0, user] - 1, last)
        pick = (lax.broadcasted_iota(jnp.int32, (16, BLK), 1) == last).astype(jnp.bfloat16)
        gate_row = jnp.dot(pick, gate_ref[...], preferred_element_type=jnp.float32)[0:1]
        token_row = jnp.dot(pick, x_ref[...], preferred_element_type=jnp.float32)[0:1]
        pieces = [gate_row[:, h * HD : (h + 1) * HD] for h in range(HEADS)]
        pieces += [token_row[:, h * HD : (h + 1) * HD] for h in range(HEADS)]
        extra = jnp.concatenate(pieces, axis=0).astype(jnp.bfloat16)
        for to in range(NSEQ):
            send_ref[to, ROW_X:ROWS_A, :] = extra


def attend_kernel(blocks_ref, tail_ref, slope_ref, got_ref, out_ref, acc, bias, list_b, list_j):
    me = lax.axis_index("seq")
    head, half = me // 2, me % 2
    starts = user_starts(blocks_ref)
    slope = slope_ref[head]

    def start_of(b):
        return jnp.where(b >= starts[2], starts[2], jnp.where(b >= starts[1], starts[1], 0))

    def fill(b, count):
        begin = start_of(b)

        def put(j, at):
            list_b[at] = b
            list_j[at] = j
            return at + 1

        return lax.fori_loop(begin, b + 1, put, count)

    count = lax.fori_loop(0, NSEQ, fill, jnp.int32(0))
    for pad in range(UNROLL - 1):
        list_b[count + pad] = NSEQ
        list_j[count + pad] = NSEQ - 1

    offset = (
        lax.broadcasted_iota(jnp.int32, (HALF, BLK), 0) - lax.broadcasted_iota(jnp.int32, (HALF, BLK), 1) + half * HALF
    )
    for d in range(MAXD):
        gap = offset + d * BLK
        table = slope * jnp.log1p(jnp.maximum(gap, 0).astype(jnp.float32))
        bias[d] = jnp.where(gap >= 0, table, MASKED)
    acc[...] = jnp.zeros_like(acc)
    scale = HD ** (-0.5)

    def some(step, carry):
        products, targets = [], []
        for t in range(UNROLL):
            b, j = list_b[step * UNROLL + t], list_j[step * UNROLL + t]
            queries = got_ref[jnp.minimum(b, NSEQ - 1), ROW_Q:ROW_X, :]
            scores = lax.dot_general(
                queries, got_ref[j, ROW_K:ROW_V, :], (((1,), (1,)), ((), ())), preferred_element_type=jnp.float32
            )
            weights = silu(scores * scale + bias[b - j]).astype(jnp.bfloat16)
            products.append(jnp.dot(weights, got_ref[j, ROW_V:ROW_Q, :], preferred_element_type=jnp.float32))
            targets.append(b)
        for b, product in zip(targets, products):
            acc[b] += product
        return carry

    lax.fori_loop(0, (count + UNROLL - 1) // UNROLL, some, 0)

    live = []
    for user in range(USERS):
        end = starts[user] + blocks_ref[0, user] - 1
        row = tail_ref[0, user] - 1 - half * HALF
        here = (row >= 0) & (row < HALF)
        value = acc[end, pl.ds(jnp.clip(row, 0, HALF - 1), 1), :]
        live.append(jnp.where(here, value, 0.0))
    extra = jnp.concatenate(live + [jnp.zeros((16 - USERS, HD), jnp.float32)], axis=0).astype(jnp.bfloat16)
    row_at = lax.broadcasted_iota(jnp.int32, (HALF, HD), 0) + half * HALF
    for b in range(NSEQ):
        valid = jnp.int32(BLK)
        for user in range(USERS):
            valid = jnp.where(starts[user] + blocks_ref[0, user] - 1 == b, tail_ref[0, user], valid)
        out_ref[b, 0:HALF, :] = jnp.where(row_at < valid, acc[b], 0.0).astype(jnp.bfloat16)
        out_ref[b, HALF:ROWS_B, :] = extra


def finish_kernel(
    blocks_ref, mixed_ref, extra_ref, gate_ref, x_ref, gain_ref, w_ref, ta_ref, tb_ref, tc_ref, td_ref, out_ref, score_ref
):
    starts = user_starts(blocks_ref)
    columns, tails = [], []
    for h in range(HEADS):
        low, high = mixed_ref[2 * h], mixed_ref[2 * h + 1]
        columns.append(jnp.concatenate([low[:HALF], high[:HALF]], axis=0).astype(jnp.float32))
        tails.append(low[HALF:].astype(jnp.float32) + high[HALF:].astype(jnp.float32))
    body = jnp.concatenate(columns, axis=1)
    tail = jnp.concatenate(tails, axis=1)
    gates, tokens = [], []
    for user in range(USERS):
        rows = extra_ref[starts[user] + blocks_ref[0, user] - 1].astype(jnp.float32)
        gates.append(jnp.concatenate([rows[h : h + 1] for h in range(HEADS)], axis=1))
        tokens.append(jnp.concatenate([rows[HEADS + h : HEADS + h + 1] for h in range(HEADS)], axis=1))
    zeros = jnp.zeros((16 - USERS, D), jnp.float32)
    gate_tail = jnp.concatenate(gates + [zeros], axis=0)
    token_tail = jnp.concatenate(tokens + [zeros], axis=0)
    gain = gain_ref[...]
    gated = (layer_norm(body) * gain * gate_ref[...].astype(jnp.float32)).astype(jnp.bfloat16)
    gated_tail = (layer_norm(tail) * gain * gate_tail).astype(jnp.bfloat16)
    both = jnp.concatenate([gated, gated_tail], axis=0)
    mixed_out = jnp.dot(both, w_ref[...], preferred_element_type=jnp.float32)
    out_ref[...] = (x_ref[...].astype(jnp.float32) + mixed_out[:BLK]).astype(jnp.bfloat16)
    states = (token_tail + mixed_out[BLK:]).astype(jnp.bfloat16)
    parts = [
        lax.dot_general(states, t_ref[...], (((1,), (1,)), ((), ())), preferred_element_type=jnp.float32)
        for t_ref in (ta_ref, tb_ref, tc_ref, td_ref)
    ]
    sides = [jnp.concatenate(parts[2 * side : 2 * side + 2], axis=1) for side in range(2)]
    rows = [sides[side][user : user + 1] for user in range(USERS) for side in range(2)]
    score_ref[...] = jnp.concatenate(rows + [jnp.zeros((2, 128), jnp.float32)], axis=0)


def pick_kernel(ids_ref, map_ref, s0_ref, s1_ref, s2_ref, s3_ref, out_ref):
    seq, dp = lax.axis_index("seq"), lax.axis_index("dp")
    my_y, my_z = seq // 4, seq % 4
    my_x, my_zh, my_c = dp // 4, (dp // 2) % 2, dp % 2
    subtree = lax.broadcasted_iota(jnp.int32, (64, 64), 0)
    for user in range(USERS):
        ids = ids_ref[user : user + 1, :]
        block = jnp.sum(jnp.where(subtree == ids // SUBT, map_ref[...], 0), axis=0, keepdims=True)
        row = block * SUBT + ids % SUBT
        owner, inside = row // 256, row % 256
        s_of, at = inside // 16, inside % 16
        x_rel = (my_x - owner // 4 + 4) % 4
        zh_rel = (my_zh - (owner // 2) % 2 + 2) % 2
        c_rel = (my_c - owner % 2 + 2) % 2
        column = x_rel * 64 + zh_rel * 32 + c_rel * 16 + at
        y_rel = (my_y - s_of // 4 + 4) % 4
        z_rel = (my_z - s_of % 4 + 4) % 4
        lane = column % 128
        side = column // 128
        hot = (lax.broadcasted_iota(jnp.int32, (128, 64), 0) == lane).astype(jnp.float32)
        total = jnp.zeros((1, 64), jnp.float32)
        for z, s_ref in enumerate((s0_ref, s1_ref, s2_ref, s3_ref)):
            found = jnp.dot(
                s_ref[...], hot, preferred_element_type=jnp.float32, precision=lax.Precision.HIGHEST
            )
            wanted = y_rel * 8 + user * 2 + side
            hit = (lax.broadcasted_iota(jnp.int32, (32, 64), 0) == wanted) & (z_rel == z)
            total = total + jnp.sum(jnp.where(hit, found, 0.0), axis=0, keepdims=True)
        out_ref[user : user + 1, :] = total


def vmem():
    return pl.BlockSpec(memory_space=pltpu.VMEM)


def smem():
    return pl.BlockSpec(memory_space=pltpu.SMEM)


def dp_shift(value, move):
    return lax.ppermute(value, "dp", [(i, move(i)) for i in range(16)])


def seq_shift(value, move):
    return lax.ppermute(value, "seq", [(i, move(i)) for i in range(16)])


def body(
    tokens,
    in_gain,
    w_proj,
    out_gain,
    w_out,
    rab_slope,
    hist_blocks,
    hist_tail,
    node_table,
    subtree_map,
    beam_nodes,
):
    x_rows = tokens[0]
    seq = lax.axis_index("seq")
    own = lax.dynamic_slice_in_dim(node_table, seq * 16, 16, 0)
    pair = jnp.concatenate([own, dp_shift(own, lambda i: i ^ 1)], axis=0)
    quad = jnp.concatenate([pair, dp_shift(pair, lambda i: i ^ 2)], axis=0)
    table = [quad] + [dp_shift(quad, lambda i, n=n: (i + 4 * n) % 16) for n in (1, 2, 3)]

    send, gate = pl.pallas_call(
        project_kernel,
        grid=(4,),
        in_specs=[
            smem(),
            smem(),
            pl.BlockSpec((BLK, D), lambda i: (0, 0)),
            pl.BlockSpec((1, D), lambda i: (0, 0)),
        ]
        + [pl.BlockSpec((D, 256), lambda i, p=p: (0, 4 * p + i)) for p in range(4)],
        out_specs=[
            pl.BlockSpec((NSEQ, ROWS_A, HD), lambda i: (0, 0, 0)),
            pl.BlockSpec((BLK, D), lambda i: (0, 0)),
        ],
        out_shape=[
            jax.ShapeDtypeStruct((NSEQ, ROWS_A, HD), jnp.bfloat16),
            jax.ShapeDtypeStruct((BLK, D), jnp.bfloat16),
        ],
        scratch_shapes=[pltpu.VMEM((BLK, D), jnp.bfloat16)],
        name="project",
        cost_estimate=pl.CostEstimate(flops=2 * BLK * D * 4 * D, bytes_accessed=10 << 20, transcendentals=BLK * 4 * D),
    )(hist_blocks, hist_tail, x_rows, in_gain[None, :], w_proj, w_proj, w_proj, w_proj)

    got = lax.all_to_all(send, "seq", 0, 0, tiled=True)

    back = pl.pallas_call(
        attend_kernel,
        in_specs=[smem(), smem(), smem(), vmem()],
        out_specs=vmem(),
        out_shape=jax.ShapeDtypeStruct((NSEQ, ROWS_B, HD), jnp.bfloat16),
        scratch_shapes=[
            pltpu.VMEM((NSEQ + 1, HALF, HD), jnp.float32),
            pltpu.VMEM((MAXD, HALF, BLK), jnp.float32),
            pltpu.SMEM((96,), jnp.int32),
            pltpu.SMEM((96,), jnp.int32),
        ],
        name="attend",
        cost_estimate=pl.CostEstimate(flops=1 << 28, bytes_accessed=2 << 20, transcendentals=1 << 20),
    )(hist_blocks, hist_tail, rab_slope, got)

    mixed = lax.all_to_all(back, "seq", 0, 0, tiled=True)

    layer_rows, scores = pl.pallas_call(
        finish_kernel,
        grid=(1,),
        in_specs=[
            smem(),
            pl.BlockSpec((NSEQ, ROWS_B, HD), lambda i: (0, 0, 0)),
            pl.BlockSpec((NSEQ, 16, HD), lambda i: (0, ROW_X // 16, 0)),
            pl.BlockSpec((BLK, D), lambda i: (0, 0)),
            pl.BlockSpec((BLK, D), lambda i: (0, 0)),
            pl.BlockSpec((1, D), lambda i: (0, 0)),
            pl.BlockSpec((D, D), lambda i: (0, 0)),
        ]
        + [pl.BlockSpec((64, D), lambda i: (0, 0))] * 4,
        out_specs=[pl.BlockSpec((BLK, D), lambda i: (0, 0)), pl.BlockSpec((8, 128), lambda i: (0, 0))],
        out_shape=[jax.ShapeDtypeStruct((BLK, D), jnp.bfloat16), jax.ShapeDtypeStruct((8, 128), jnp.float32)],
        name="finish",
        cost_estimate=pl.CostEstimate(flops=2 * 144 * D * D, bytes_accessed=4 << 20, transcendentals=0),
    )(hist_blocks, mixed, got, gate, x_rows, out_gain[None, :], w_out, *table)

    along_y = jnp.concatenate(
        [scores] + [seq_shift(scores, lambda i, n=n: (i + 4 * n) % 16) for n in (1, 2, 3)], axis=0
    )
    along_z = [along_y] + [seq_shift(along_y, lambda i, n=n: i // 4 * 4 + (i + n) % 4) for n in (1, 2, 3)]
    beam_scores = pl.pallas_call(
        pick_kernel,
        in_specs=[vmem()] * 6,
        out_specs=vmem(),
        out_shape=jax.ShapeDtypeStruct((USERS, 64), jnp.float32),
        name="pick",
    )(beam_nodes, subtree_map[:, None], *along_z)
    return (layer_rows[None], beam_scores)


def solution(mesh):
    placed = (
        P("dp", "seq", None),
        P(),
        P(),
        P(),
        P(),
        P(),
        P("dp", None),
        P("dp", None),
        P("dp", None),
        P(),
        P("dp", "seq"),
    )
    return jax.shard_map(
        body,
        mesh=mesh,
        in_specs=placed,
        out_specs=(P("dp", "seq", None), P("dp", "seq")),
        check_vma=False,
    )
```

```python
import jax
import jax.numpy as jnp
from jax import lax
from jax.experimental import pallas as pl
from jax.experimental.pallas import tpu as pltpu
from jax.sharding import PartitionSpec as P

BLK = 128
SUBT = 64
USERS = 3
D = 1024
HEADS = 8
HD = 128
NSEQ = 16
MAXD = 10
UNROLL = 4
MASKED = -1e30
ROW_K, ROW_V, ROW_Q, ROWS_A = 0, 128, 256, 384
ROW_E, ROW_X, ROWS_B = 128, 144, 160
FAR = (2, 3, 6, 7)
NEAR = (0, 1, 4, 5)
SETS = [[0, 1, 2, 3, 8, 9, 10, 11], [4, 5, 6, 7, 12, 13, 14, 15]]
LIST = 128


def head_of(seq):
    return (seq // 8) * 4 + seq % 4


def set_of(seq):
    return (seq // 4) % 2


def spread(q):
    return (q // 4) * 8 + q % 4


def silu(x):
    half = 0.5 * x
    return half + half * jnp.tanh(half)


def layer_norm(rows):
    centred = rows - jnp.mean(rows, axis=-1, keepdims=True)
    spread_ = jnp.mean(centred * centred, axis=-1, keepdims=True)
    return centred * lax.rsqrt(spread_ + 1e-05)


def user_starts(blocks_ref):
    one = blocks_ref[0, 0]
    return (0, one, one + blocks_ref[0, 1])


def message(rows, wq_ref, wk_ref, wv_ref, out_ref):
    def part(w_ref):
        return silu(jnp.dot(rows, w_ref[...], preferred_element_type=jnp.float32))

    out_ref[ROW_K:ROW_V, :] = part(wk_ref).T.astype(jnp.bfloat16)
    out_ref[ROW_V:ROW_Q, :] = part(wv_ref).astype(jnp.bfloat16)
    out_ref[ROW_Q:ROWS_A, :] = part(wq_ref).astype(jnp.bfloat16)


def project_far_kernel(heads_ref, x_ref, gain_ref, wq_ref, wk_ref, wv_ref, normed_ref, *out_refs):
    step = pl.program_id(0)

    @pl.when(step == 0)
    def _():
        normed_ref[...] = (layer_norm(x_ref[...].astype(jnp.float32)) * gain_ref[...]).astype(jnp.bfloat16)

    for at, out_ref in enumerate(out_refs):

        @pl.when(step == at)
        def _(out_ref=out_ref):
            message(normed_ref[...], wq_ref, wk_ref, wv_ref, out_ref)


def project_near_kernel(heads_ref, normed_ref, wq_ref, wk_ref, wv_ref, wg_ref, gate_ref, *out_refs):
    step = pl.program_id(0)
    for at, out_ref in enumerate(out_refs):

        @pl.when(step == at)
        def _(at=at, out_ref=out_ref):
            message(normed_ref[...], wq_ref, wk_ref, wv_ref, out_ref)
            gate_ref[:, at * 256 : (at + 1) * 256] = silu(
                jnp.dot(normed_ref[...], wg_ref[...], preferred_element_type=jnp.float32)
            ).astype(jnp.bfloat16)


def prepare_kernel(
    blocks_ref, tail_ref, slope_ref, ids_ref, map_ref, x_ref, gate_ref, bias_ref, list_ref, hot_ref, row_ref, extra_ref
):
    me, dp = lax.axis_index("seq"), lax.axis_index("dp")
    starts = user_starts(blocks_ref)
    slope = slope_ref[head_of(me)]
    offset = lax.broadcasted_iota(jnp.int32, (BLK, BLK), 0) - lax.broadcasted_iota(jnp.int32, (BLK, BLK), 1)
    for d in range(MAXD):
        gap = offset + d * BLK
        table = slope * jnp.log1p(jnp.maximum(gap, 0).astype(jnp.float32))
        bias_ref[d] = jnp.where(gap >= 0, table, MASKED) if d == 0 else table

    def fill(t, counts):
        b = (t // 4) * 8 + set_of(me) * 4 + t % 4
        begin = jnp.where(b >= starts[2], starts[2], jnp.where(b >= starts[1], starts[1], 0))

        def put(j, counts):
            apart = j ^ me
            cross = (apart // 4) % 2
            q = (apart // 8) * 4 + apart % 4
            late = cross * ((q // 2) % 2)
            code = ((t ^ head_of(me)) * 16 + cross * 8 + q) * 16 + b - j
            first, second = counts
            list_ref[jnp.where(late == 1, LIST + second, first)] = code
            return (first + 1 - late, second + late)

        return lax.fori_loop(begin, b + 1, put, counts)

    counts = lax.fori_loop(0, 8, fill, (jnp.int32(0), jnp.int32(0)))
    for which, count in enumerate(counts):
        for pad in range(UNROLL - 1):
            list_ref[which * LIST + count + pad] = 8 * 256
        list_ref[which * LIST + LIST - 1] = (count + UNROLL - 1) // UNROLL

    my_x, my_zh, my_c = dp // 4, (dp // 2) % 2, dp % 2
    subtree = lax.broadcasted_iota(jnp.int32, (64, 64), 0)
    for user in range(USERS):
        end = starts[user] + blocks_ref[0, user] - 1
        ids = ids_ref[user : user + 1, :]
        block = jnp.sum(jnp.where(subtree == ids // SUBT, map_ref[...], 0), axis=0, keepdims=True)
        row = block * SUBT + ids % SUBT
        owner, inside = row // 256, row % 256
        shard, at = inside // 32, inside % 32
        x_rel = (my_x - owner // 4 + 4) % 4
        zh_rel = (my_zh - (owner // 2) % 2 + 2) % 2
        c_rel = (my_c - owner % 2 + 2) % 2
        lane = zh_rel * 64 + c_rel * 32 + at
        source = (shard // 4) * 8 + set_of(end) * 4 + shard % 4
        hot_ref[user] = (lax.broadcasted_iota(jnp.int32, (BLK, 64), 0) == lane).astype(jnp.float32)
        row_ref[user] = jnp.broadcast_to(source * 16 + user * 4 + x_rel, (8, 64))

    last = jnp.int32(-1)
    for user in range(USERS):
        last = jnp.where(starts[user] + blocks_ref[0, user] - 1 == me, tail_ref[0, user] - 1, last)
    pick = (lax.broadcasted_iota(jnp.int32, (16, BLK), 1) == last).astype(jnp.bfloat16)
    gate_row = jnp.dot(pick, gate_ref[...], preferred_element_type=jnp.float32)[0:1]
    token_row = jnp.dot(pick, x_ref[...], preferred_element_type=jnp.float32)[0:1]
    pieces = [row[:, h * HD : (h + 1) * HD] for row in (gate_row, token_row) for h in range(HEADS)]
    extra_ref[...] = jnp.concatenate(pieces, axis=0).astype(jnp.bfloat16)


def run_pairs(list_ref, which, query, keys, values, bias_ref, acc):
    scale = HD ** (-0.5)

    def some(step, carry):
        products, targets = [], []
        for t in range(UNROLL):
            code = list_ref[which * LIST + step * UNROLL + t]
            mine, slot, d = code // 256, (code // 16) % 16, code % 16
            scores = jnp.dot(query(jnp.minimum(mine, 7)), keys(slot), preferred_element_type=jnp.float32)
            weights = silu(scores * scale + bias_ref[d]).astype(jnp.bfloat16)
            products.append(jnp.dot(weights, values(slot), preferred_element_type=jnp.float32))
            targets.append(mine)
        for mine, product in zip(targets, products):
            acc[mine] += product
        return carry

    lax.fori_loop(0, list_ref[which * LIST + LIST - 1], some, 0)


def attend_first_kernel(list_ref, bias_ref, *refs):
    got_refs, cross_ref, acc_ref, queries_ref, keep, acc = refs[:8], refs[8], refs[9], refs[10], refs[11], refs[12]
    for q, got_ref in enumerate(got_refs):
        keep[q] = got_ref[ROW_K:ROW_Q, :]
        queries_ref[q] = got_ref[ROW_Q:ROWS_A, :]
    for at, q in enumerate(NEAR):
        keep[8 + q] = cross_ref[at]
    acc[...] = jnp.zeros_like(acc)
    run_pairs(
        list_ref,
        0,
        lambda mine: queries_ref[mine],
        lambda slot: keep[slot, ROW_K:ROW_V, :],
        lambda slot: keep[slot, ROW_V:ROW_Q, :],
        bias_ref,
        acc,
    )
    acc_ref[...] = acc[0:8]


def attend_last_kernel(blocks_ref, tail_ref, list_ref, bias_ref, queries_ref, cross_ref, acc_ref, extra_ref, out_ref, acc):
    me = lax.axis_index("seq")
    mine = head_of(me)
    starts = user_starts(blocks_ref)
    acc[0:8] = acc_ref[...]
    acc[8] = jnp.zeros((BLK, HD), jnp.float32)

    def at(slot):
        q = slot % 8
        return (q // 4) * 2 + q % 2

    run_pairs(
        list_ref,
        1,
        lambda own: queries_ref[own],
        lambda slot: cross_ref[at(slot), ROW_K:ROW_V, :],
        lambda slot: cross_ref[at(slot), ROW_V:ROW_Q, :],
        bias_ref,
        acc,
    )
    rows = []
    for user in range(USERS):
        end = starts[user] + blocks_ref[0, user] - 1
        here = set_of(end) == set_of(me)
        value = acc[head_of(end) ^ mine, pl.ds(tail_ref[0, user] - 1, 1), :]
        rows.append(jnp.where(here, value, 0.0))
    last = jnp.concatenate(rows + [jnp.zeros((16 - USERS, HD), jnp.float32)], axis=0).astype(jnp.bfloat16)
    row_at = lax.broadcasted_iota(jnp.int32, (BLK, HD), 0)
    for t in range(8):
        b = (t // 4) * 8 + set_of(me) * 4 + t % 4
        valid = jnp.int32(BLK)
        for user in range(USERS):
            valid = jnp.where(starts[user] + blocks_ref[0, user] - 1 == b, tail_ref[0, user], valid)
        out_ref[t, 0:ROW_E, :] = jnp.where(row_at < valid, acc[mine ^ t], 0.0).astype(jnp.bfloat16)
        out_ref[t, ROW_E:ROW_X, :] = last
        out_ref[t, ROW_X:ROWS_B, :] = extra_ref[...]


def state_kernel(blocks_ref, mixed_ref, gain_ref, w_ref, ta_ref, tb_ref, tc_ref, td_ref, score_ref):
    starts = user_starts(blocks_ref)
    tail = jnp.concatenate([mixed_ref[h, ROW_E - ROW_E : ROW_X - ROW_E, :].astype(jnp.float32) for h in range(HEADS)], axis=1)
    gates, tokens = [], []
    for user in range(USERS):
        end = starts[user] + blocks_ref[0, user] - 1
        rows = mixed_ref[head_of(end), ROW_X - ROW_E :, :].astype(jnp.float32)
        gates.append(jnp.concatenate([rows[h : h + 1] for h in range(HEADS)], axis=1))
        tokens.append(jnp.concatenate([rows[HEADS + h : HEADS + h + 1] for h in range(HEADS)], axis=1))
    zeros = jnp.zeros((16 - USERS, D), jnp.float32)
    gate_tail = jnp.concatenate(gates + [zeros], axis=0)
    token_tail = jnp.concatenate(tokens + [zeros], axis=0)
    gated = (layer_norm(tail) * gain_ref[...] * gate_tail).astype(jnp.bfloat16)
    states = (token_tail + jnp.dot(gated, w_ref[...], preferred_element_type=jnp.float32)).astype(jnp.bfloat16)
    parts = [
        lax.dot_general(states, t_ref[...], (((1,), (1,)), ((), ())), preferred_element_type=jnp.float32)
        for t_ref in (ta_ref, tb_ref, tc_ref, td_ref)
    ]
    rows = [part[user : user + 1] for user in range(USERS) for part in parts]
    block = jnp.concatenate(rows + [jnp.zeros((4, 128), jnp.float32)], axis=0)
    for to in range(NSEQ):
        score_ref[to] = block


def layer_kernel(mixed_ref, gate_ref, x_ref, gain_ref, w_ref, out_ref):
    mixed = jnp.concatenate([mixed_ref[h].astype(jnp.float32) for h in range(HEADS)], axis=1)
    gated = (layer_norm(mixed) * gain_ref[...] * gate_ref[...].astype(jnp.float32)).astype(jnp.bfloat16)
    out_ref[...] = (
        x_ref[...].astype(jnp.float32) + jnp.dot(gated, w_ref[...], preferred_element_type=jnp.float32)
    ).astype(jnp.bfloat16)


def pick_kernel(score_ref, hot_ref, row_ref, out_ref):
    scores = score_ref[...].reshape(NSEQ * 16, 128)
    row_at = lax.broadcasted_iota(jnp.int32, (NSEQ * 16, 64), 0)
    for user in range(USERS):
        found = jnp.dot(
            scores, hot_ref[user], preferred_element_type=jnp.float32, precision=lax.Precision.HIGHEST
        )
        hit = row_at == row_ref[user, 0:1, :]
        out_ref[user : user + 1, :] = jnp.sum(jnp.where(hit, found, 0.0), axis=0, keepdims=True)


def vmem():
    return pl.BlockSpec(memory_space=pltpu.VMEM)


def smem():
    return pl.BlockSpec(memory_space=pltpu.SMEM)


def whole(*shape):
    return pl.BlockSpec(shape, lambda i, *_: (0,) * len(shape))


def dp_shift(value, move):
    return lax.ppermute(value, "dp", [(i, move(i)) for i in range(16)])


def seq_xor(value, apart):
    return lax.ppermute(value, "seq", [(i, i ^ apart) for i in range(NSEQ)])


def sds(shape, dtype=jnp.bfloat16):
    return jax.ShapeDtypeStruct(shape, dtype)


def cost(flops, read):
    return pl.CostEstimate(flops=flops, bytes_accessed=read, transcendentals=0)


def body(
    tokens,
    in_gain,
    w_proj,
    out_gain,
    w_out,
    rab_slope,
    hist_blocks,
    hist_tail,
    node_table,
    subtree_map,
    beam_nodes,
):
    x_rows = tokens[0]
    seq = lax.axis_index("seq")
    mine = head_of(seq)

    def weight(group):
        return pl.BlockSpec((D, HD), lambda i, heads, g=group: (0, 8 * g + heads[i]))

    normed, *far_sent = pl.pallas_call(
        project_far_kernel,
        grid_spec=pltpu.PrefetchScalarGridSpec(
            num_scalar_prefetch=1,
            grid=(4,),
            in_specs=[whole(BLK, D), whole(1, D), weight(1), weight(2), weight(3)],
            out_specs=[whole(BLK, D)] + [whole(ROWS_A, HD)] * 4,
        ),
        out_shape=[sds((BLK, D))] + [sds((ROWS_A, HD))] * 4,
        name="project_far",
        cost_estimate=cost(2 * BLK * D * 12 * HD, 4 << 20),
    )(mine ^ jnp.array(FAR, jnp.int32), x_rows, in_gain[None, :], w_proj, w_proj, w_proj)
    far_got = [seq_xor(value, spread(q)) for q, value in zip(FAR, far_sent)]

    gate, *near_sent = pl.pallas_call(
        project_near_kernel,
        grid_spec=pltpu.PrefetchScalarGridSpec(
            num_scalar_prefetch=1,
            grid=(4,),
            in_specs=[
                whole(BLK, D),
                weight(1),
                weight(2),
                weight(3),
                pl.BlockSpec((D, 256), lambda i, heads: (0, i)),
            ],
            out_specs=[whole(BLK, D)] + [whole(ROWS_A, HD)] * 4,
        ),
        out_shape=[sds((BLK, D))] + [sds((ROWS_A, HD))] * 4,
        name="project_near",
        cost_estimate=cost(2 * BLK * D * 20 * HD, 6 << 20),
    )(mine ^ jnp.array(NEAR, jnp.int32), normed, w_proj, w_proj, w_proj, w_proj)
    near_got = [near_sent[0]] + [seq_xor(value, spread(q)) for q, value in zip(NEAR[1:], near_sent[1:])]

    own = lax.dynamic_slice_in_dim(node_table, mine * 32, 32, 0)
    own, _ = lax.optimization_barrier((own, gate))
    pair = jnp.concatenate([own, dp_shift(own, lambda i: i ^ 1)], axis=0)
    quad = jnp.concatenate([pair, dp_shift(pair, lambda i: i ^ 2)], axis=0)
    table = [quad] + [dp_shift(quad, lambda i, n=n: (i + 4 * n) % 16) for n in (1, 2, 3)]

    bias, pairs, hot, rows, extra = pl.pallas_call(
        prepare_kernel,
        in_specs=[smem(), smem(), smem()] + [vmem()] * 4,
        out_specs=[vmem(), smem(), vmem(), vmem(), vmem()],
        out_shape=[
            sds((MAXD, BLK, BLK), jnp.float32),
            sds((2 * LIST,), jnp.int32),
            sds((USERS, BLK, 64), jnp.float32),
            sds((USERS, 8, 64), jnp.int32),
            sds((16, HD)),
        ],
        name="prepare",
        cost_estimate=cost(1 << 28, 4 << 20),
    )(hist_blocks, hist_tail, rab_slope, beam_nodes, subtree_map[:, None], x_rows, gate)

    near_kv = jnp.stack([value[:ROW_Q] for value in near_got])
    near_cross = seq_xor(near_kv, 4)
    far_kv = jnp.stack([value[:ROW_Q] for value in far_got])
    far_cross = seq_xor(far_kv, 4)

    by_head = [None] * 8
    for q, value in zip(NEAR + FAR, near_got + far_got):
        by_head[q] = value
    part, queries = pl.pallas_call(
        attend_first_kernel,
        in_specs=[smem()] + [vmem()] * 10,
        out_specs=[vmem(), vmem()],
        out_shape=[sds((8, BLK, HD), jnp.float32), sds((8, BLK, HD))],
        scratch_shapes=[pltpu.VMEM((16, ROW_Q, HD), jnp.bfloat16), pltpu.VMEM((9, BLK, HD), jnp.float32)],
        name="attend_first",
        cost_estimate=cost(1 << 31, 4 << 20),
    )(pairs, bias, *by_head, near_cross)

    back = pl.pallas_call(
        attend_last_kernel,
        in_specs=[smem()] * 3 + [vmem()] * 5,
        out_specs=vmem(),
        out_shape=sds((8, ROWS_B, HD)),
        scratch_shapes=[pltpu.VMEM((9, BLK, HD), jnp.float32)],
        name="attend_last",
        cost_estimate=cost(1 << 30, 2 << 20),
    )(hist_blocks, hist_tail, pairs, bias, queries, far_cross, part, extra)
    back, table = lax.optimization_barrier((back, table))

    mixed = lax.all_to_all(back, "seq", 0, 0, tiled=True, axis_index_groups=SETS)

    sent = pl.pallas_call(
        state_kernel,
        grid=(1,),
        in_specs=[
            smem(),
            pl.BlockSpec((HEADS, 32, HD), lambda i: (0, ROW_E // 32, 0)),
            whole(1, D),
            whole(D, D),
        ]
        + [whole(BLK, D)] * 4,
        out_specs=whole(NSEQ, 16, 128),
        out_shape=sds((NSEQ, 16, 128), jnp.float32),
        name="state",
        cost_estimate=cost(2 * 16 * D * D, 3 << 20),
    )(hist_blocks, mixed, out_gain[None, :], w_out, *table)
    scores = lax.all_to_all(sent, "seq", 0, 0, tiled=True)

    layer_rows = pl.pallas_call(
        layer_kernel,
        grid=(1,),
        in_specs=[
            pl.BlockSpec((HEADS, BLK, HD), lambda i: (0, 0, 0)),
            whole(BLK, D),
            whole(BLK, D),
            whole(1, D),
            whole(D, D),
        ],
        out_specs=whole(BLK, D),
        out_shape=sds((BLK, D)),
        name="layer",
        cost_estimate=cost(2 * BLK * D * D, 3 << 20),
    )(mixed, gate, x_rows, out_gain[None, :], w_out)

    beam_scores = pl.pallas_call(
        pick_kernel,
        in_specs=[vmem()] * 3,
        out_specs=vmem(),
        out_shape=sds((USERS, 64), jnp.float32),
        name="pick",
        cost_estimate=cost(1 << 20, 1 << 17),
    )(scores, hot, rows)
    return (layer_rows[None], beam_scores)


def solution(mesh):
    placed = (
        P("dp", "seq", None),
        P(),
        P(),
        P(),
        P(),
        P(),
        P("dp", None),
        P("dp", None),
        P("dp", None),
        P(),
        P("dp", "seq"),
    )
    return jax.shard_map(
        body,
        mesh=mesh,
        in_specs=placed,
        out_specs=(P("dp", "seq", None), P("dp", "seq")),
        check_vma=False,
    )
```

```python
import jax
import jax.numpy as jnp
from jax import lax
from jax.experimental import pallas as pl
from jax.experimental.pallas import tpu as pltpu
from jax.sharding import PartitionSpec as P

BLK = 128
SUBT = 64
USERS = 3
D = 1024
HEADS = 8
HD = 128
NSEQ = 16
MAXD = 10
UNROLL = 4
MASKED = -1e30
ROW_K, ROW_V, ROW_Q, ROWS_A = 0, 128, 256, 384
ROW_E, ROW_X, ROWS_B = 128, 144, 160
FAR = (2, 3, 6, 7)
NEAR = (0, 1, 4, 5)
SETS = [[0, 1, 2, 3, 8, 9, 10, 11], [4, 5, 6, 7, 12, 13, 14, 15]]
LIST = 128
GRANT = pltpu.CompilerParams(vmem_limit_bytes=16 << 20)


def head_of(seq):
    return (seq // 8) * 4 + seq % 4


def set_of(seq):
    return (seq // 4) % 2


def spread(q):
    return (q // 4) * 8 + q % 4


def silu(x):
    half = 0.5 * x
    return half + half * jnp.tanh(half)


def layer_norm(rows):
    centred = rows - jnp.mean(rows, axis=-1, keepdims=True)
    spread_ = jnp.mean(centred * centred, axis=-1, keepdims=True)
    return centred * lax.rsqrt(spread_ + 1e-05)


def user_starts(blocks_ref):
    one = blocks_ref[0, 0]
    return (0, one, one + blocks_ref[0, 1])


def project_kernel(blocks_ref, tail_ref, x_ref, gain_ref, w_ref, gate_ref, extra_ref, *refs):
    out_refs, weights, sems = refs[:HEADS], refs[HEADS], refs[HEADS + 1]
    me = lax.axis_index("seq")
    order = FAR + NEAR

    def copies(at):
        head = head_of(me) ^ order[at]
        return [
            pltpu.make_async_copy(
                w_ref.at[:, pl.ds(pl.multiple_of((group * HEADS + head) * HD, HD), HD)],
                weights.at[at, :, group * HD : (group + 1) * HD],
                sems.at[at, group],
            )
            for group in range(4)
        ]

    for at in range(HEADS):
        for copy in copies(at):
            copy.start()
    normed = (layer_norm(x_ref[...].astype(jnp.float32)) * gain_ref[...]).astype(jnp.bfloat16)
    for at, out_ref in enumerate(out_refs):
        for copy in copies(at):
            copy.wait()
        parts = silu(jnp.dot(normed, weights[at], preferred_element_type=jnp.float32))
        head = head_of(me) ^ order[at]
        gate_ref[:, pl.ds(pl.multiple_of(head * HD, HD), HD)] = parts[:, :HD].astype(jnp.bfloat16)
        out_ref[ROW_K:ROW_V, :] = parts[:, 2 * HD : 3 * HD].T.astype(jnp.bfloat16)
        out_ref[ROW_V:ROW_Q, :] = parts[:, 3 * HD :].astype(jnp.bfloat16)
        out_ref[ROW_Q:ROWS_A, :] = parts[:, HD : 2 * HD].astype(jnp.bfloat16)

    starts = user_starts(blocks_ref)
    last = jnp.int32(-1)
    for user in range(USERS):
        last = jnp.where(starts[user] + blocks_ref[0, user] - 1 == me, tail_ref[0, user] - 1, last)
    pick = (lax.broadcasted_iota(jnp.int32, (16, BLK), 1) == last).astype(jnp.bfloat16)
    gate_row = jnp.dot(pick, gate_ref[...], preferred_element_type=jnp.float32)[0:1]
    token_row = jnp.dot(pick, x_ref[...], preferred_element_type=jnp.float32)[0:1]
    pieces = [row[:, h * HD : (h + 1) * HD] for row in (gate_row, token_row) for h in range(HEADS)]
    extra_ref[...] = jnp.concatenate(pieces, axis=0).astype(jnp.bfloat16)


def prepare_kernel(
    blocks_ref, slope_ref, ids_ref, map_ref, bias_ref, list_ref, hot_ref, row_ref
):
    me, dp = lax.axis_index("seq"), lax.axis_index("dp")
    starts = user_starts(blocks_ref)
    slope = slope_ref[head_of(me)]
    offset = lax.broadcasted_iota(jnp.int32, (BLK, BLK), 0) - lax.broadcasted_iota(jnp.int32, (BLK, BLK), 1)
    for d in range(MAXD):
        gap = offset + d * BLK
        table = slope * jnp.log1p(jnp.maximum(gap, 0).astype(jnp.float32))
        bias_ref[d] = jnp.where(gap >= 0, table, MASKED) if d == 0 else table

    def fill(t, counts):
        b = (t // 4) * 8 + set_of(me) * 4 + t % 4
        begin = jnp.where(b >= starts[2], starts[2], jnp.where(b >= starts[1], starts[1], 0))

        def put(j, counts):
            apart = j ^ me
            cross = (apart // 4) % 2
            q = (apart // 8) * 4 + apart % 4
            late = cross * ((q // 2) % 2)
            code = ((t ^ head_of(me)) * 16 + cross * 8 + q) * 16 + b - j
            first, second = counts
            list_ref[jnp.where(late == 1, LIST + second, first)] = code
            return (first + 1 - late, second + late)

        return lax.fori_loop(begin, b + 1, put, counts)

    counts = lax.fori_loop(0, 8, fill, (jnp.int32(0), jnp.int32(0)))
    for which, count in enumerate(counts):
        for pad in range(UNROLL - 1):
            list_ref[which * LIST + count + pad] = 8 * 256
        list_ref[which * LIST + LIST - 1] = (count + UNROLL - 1) // UNROLL

    my_x, my_zh, my_c = dp // 4, (dp // 2) % 2, dp % 2
    subtree = lax.broadcasted_iota(jnp.int32, (64, 64), 0)
    diagonal = subtree == lax.broadcasted_iota(jnp.int32, (64, 64), 1)
    places = jnp.sum(jnp.where(diagonal, map_ref[...], 0), axis=1, keepdims=True)
    for user in range(USERS):
        end = starts[user] + blocks_ref[0, user] - 1
        ids = ids_ref[user : user + 1, :]
        block = jnp.sum(jnp.where(subtree == ids // SUBT, places, 0), axis=0, keepdims=True)
        row = block * SUBT + ids % SUBT
        owner, inside = row // 256, row % 256
        shard, at = inside // 32, inside % 32
        x_rel = (my_x - owner // 4 + 4) % 4
        zh_rel = (my_zh - (owner // 2) % 2 + 2) % 2
        c_rel = (my_c - owner % 2 + 2) % 2
        lane = c_rel * 64 + zh_rel * 32 + at
        source = (shard // 4) * 8 + set_of(end) * 4 + shard % 4
        hot_ref[user] = (lax.broadcasted_iota(jnp.int32, (BLK, 64), 0) == lane).astype(jnp.float32)
        row_ref[user] = jnp.broadcast_to(source * 16 + user * 4 + x_rel, (8, 64))


def run_pairs(list_ref, which, query, keys, values, bias_ref, acc):
    scale = HD ** (-0.5)

    def some(step, carry):
        products, targets = [], []
        for t in range(UNROLL):
            code = list_ref[which * LIST + step * UNROLL + t]
            mine, slot, d = code // 256, (code // 16) % 16, code % 16
            scores = jnp.dot(query(jnp.minimum(mine, 7)), keys(slot), preferred_element_type=jnp.float32)
            weights = silu(scores * scale + bias_ref[d]).astype(jnp.bfloat16)
            products.append(jnp.dot(weights, values(slot), preferred_element_type=jnp.float32))
            targets.append(mine)
        for mine, product in zip(targets, products):
            acc[mine] += product
        return carry

    lax.fori_loop(0, list_ref[which * LIST + LIST - 1], some, 0)


def attend_first_kernel(list_ref, bias_ref, *refs):
    got_refs, cross_ref, acc_ref, queries_ref, keep, acc = refs[:8], refs[8], refs[9], refs[10], refs[11], refs[12]
    for q, got_ref in enumerate(got_refs):
        keep[q] = got_ref[ROW_K:ROW_Q, :]
        queries_ref[q] = got_ref[ROW_Q:ROWS_A, :]
    for at, q in enumerate(NEAR):
        keep[8 + q] = cross_ref[at]
    acc[...] = jnp.zeros_like(acc)
    run_pairs(
        list_ref,
        0,
        lambda mine: queries_ref[mine],
        lambda slot: keep[slot, ROW_K:ROW_V, :],
        lambda slot: keep[slot, ROW_V:ROW_Q, :],
        bias_ref,
        acc,
    )
    acc_ref[...] = acc[0:8]


def attend_last_kernel(blocks_ref, tail_ref, list_ref, bias_ref, queries_ref, cross_ref, acc_ref, extra_ref, out_ref, acc):
    me = lax.axis_index("seq")
    mine = head_of(me)
    starts = user_starts(blocks_ref)
    acc[0:8] = acc_ref[...]
    acc[8] = jnp.zeros((BLK, HD), jnp.float32)

    def at(slot):
        q = slot % 8
        return (q // 4) * 2 + q % 2

    run_pairs(
        list_ref,
        1,
        lambda own: queries_ref[own],
        lambda slot: cross_ref[at(slot), ROW_K:ROW_V, :],
        lambda slot: cross_ref[at(slot), ROW_V:ROW_Q, :],
        bias_ref,
        acc,
    )
    rows = []
    for user in range(USERS):
        end = starts[user] + blocks_ref[0, user] - 1
        here = set_of(end) == set_of(me)
        value = acc[head_of(end) ^ mine, pl.ds(tail_ref[0, user] - 1, 1), :]
        rows.append(jnp.where(here, value, 0.0))
    last = jnp.concatenate(rows + [jnp.zeros((16 - USERS, HD), jnp.float32)], axis=0).astype(jnp.bfloat16)
    row_at = lax.broadcasted_iota(jnp.int32, (BLK, HD), 0)
    for t in range(8):
        b = (t // 4) * 8 + set_of(me) * 4 + t % 4
        valid = jnp.int32(BLK)
        for user in range(USERS):
            valid = jnp.where(starts[user] + blocks_ref[0, user] - 1 == b, tail_ref[0, user], valid)
        out_ref[t, 0:ROW_E, :] = jnp.where(row_at < valid, acc[mine ^ t], 0.0).astype(jnp.bfloat16)
        out_ref[t, ROW_E:ROW_X, :] = last
        out_ref[t, ROW_X:ROWS_B, :] = extra_ref[...]


def state_kernel(blocks_ref, mixed_ref, gain_ref, w_ref, ta_ref, tb_ref, tc_ref, td_ref, score_ref):
    starts = user_starts(blocks_ref)
    tail = jnp.concatenate([mixed_ref[h, ROW_E:ROW_X, :].astype(jnp.float32) for h in range(HEADS)], axis=1)
    gates, tokens = [], []
    for user in range(USERS):
        end = starts[user] + blocks_ref[0, user] - 1
        rows = mixed_ref[head_of(end), ROW_X:ROWS_B, :].astype(jnp.float32)
        gates.append(jnp.concatenate([rows[h : h + 1] for h in range(HEADS)], axis=1))
        tokens.append(jnp.concatenate([rows[HEADS + h : HEADS + h + 1] for h in range(HEADS)], axis=1))
    zeros = jnp.zeros((16 - USERS, D), jnp.float32)
    gate_tail = jnp.concatenate(gates + [zeros], axis=0)
    token_tail = jnp.concatenate(tokens + [zeros], axis=0)
    gated = (layer_norm(tail) * gain_ref[...] * gate_tail).astype(jnp.bfloat16)
    states = (token_tail + jnp.dot(gated, w_ref[...], preferred_element_type=jnp.float32)).astype(jnp.bfloat16)
    parts = [
        lax.dot_general(states, t_ref[...], (((1,), (1,)), ((), ())), preferred_element_type=jnp.float32)
        for t_ref in (ta_ref, tb_ref, tc_ref, td_ref)
    ]
    rows = [part[user : user + 1] for user in range(USERS) for part in parts]
    block = jnp.concatenate(rows + [jnp.zeros((4, 128), jnp.float32)], axis=0)
    for to in range(NSEQ):
        score_ref[to] = block


def layer_kernel(mixed_ref, gate_ref, x_ref, gain_ref, w_ref, out_ref):
    mixed = jnp.concatenate([mixed_ref[h, 0:ROW_E, :].astype(jnp.float32) for h in range(HEADS)], axis=1)
    gated = (layer_norm(mixed) * gain_ref[...] * gate_ref[...].astype(jnp.float32)).astype(jnp.bfloat16)
    out_ref[...] = (
        x_ref[...].astype(jnp.float32) + jnp.dot(gated, w_ref[...], preferred_element_type=jnp.float32)
    ).astype(jnp.bfloat16)


def pick_kernel(score_ref, hot_ref, row_ref, out_ref):
    scores = score_ref[...].reshape(NSEQ * 16, 128)
    row_at = lax.broadcasted_iota(jnp.int32, (NSEQ * 16, 64), 0)
    for user in range(USERS):
        found = jnp.dot(
            scores, hot_ref[user], preferred_element_type=jnp.float32, precision=lax.Precision.HIGHEST
        )
        hit = row_at == row_ref[user, 0:1, :]
        out_ref[user : user + 1, :] = jnp.sum(jnp.where(hit, found, 0.0), axis=0, keepdims=True)


def vmem():
    return pl.BlockSpec(memory_space=pltpu.VMEM)


def smem():
    return pl.BlockSpec(memory_space=pltpu.SMEM)


def dp_shift(value, move):
    return lax.ppermute(value, "dp", [(i, move(i)) for i in range(16)])


def seq_xor(value, apart):
    return lax.ppermute(value, "seq", [(i, i ^ apart) for i in range(NSEQ)])


def sds(shape, dtype=jnp.bfloat16):
    return jax.ShapeDtypeStruct(shape, dtype)


def cost(flops, read):
    return pl.CostEstimate(flops=flops, bytes_accessed=read, transcendentals=0)


def body(
    tokens,
    in_gain,
    w_proj,
    out_gain,
    w_out,
    rab_slope,
    hist_blocks,
    hist_tail,
    node_table,
    subtree_map,
    beam_nodes,
):
    x_rows = tokens[0]
    seq = lax.axis_index("seq")
    mine = head_of(seq)

    gate, extra, *sent = pl.pallas_call(
        project_kernel,
        in_specs=[smem(), smem(), vmem(), vmem(), pl.BlockSpec(memory_space=pltpu.HBM)],
        out_specs=[vmem()] * (2 + HEADS),
        out_shape=[sds((BLK, D)), sds((16, HD))] + [sds((ROWS_A, HD))] * HEADS,
        scratch_shapes=[pltpu.VMEM((HEADS, D, 4 * HD), jnp.bfloat16), pltpu.SemaphoreType.DMA((HEADS, 4))],
        name="project",
        cost_estimate=cost(2 * BLK * D * 4 * D, 10 << 20),
        compiler_params=GRANT,
    )(*(pltpu.with_memory_space_constraint(value, pltpu.HBM) for value in (hist_blocks, hist_tail, x_rows, in_gain[None, :], w_proj)))
    far_got = [seq_xor(value, spread(q)) for q, value in zip(FAR, sent[:4])]
    near_got = [sent[4]] + [seq_xor(value, spread(q)) for q, value in zip(NEAR[1:], sent[5:])]

    own = lax.dynamic_slice_in_dim(node_table, mine * 32, 32, 0)
    own, _ = lax.optimization_barrier((own, gate))
    pair = jnp.concatenate([own, dp_shift(own, lambda i: i ^ 2)], axis=0)
    quad = jnp.concatenate([pair, dp_shift(pair, lambda i: i ^ 1)], axis=0)
    table = [quad] + [dp_shift(quad, lambda i, n=n: (i + 4 * n) % 16) for n in (1, 2, 3)]

    bias, pairs, hot, rows = pl.pallas_call(
        prepare_kernel,
        in_specs=[smem(), smem(), vmem(), vmem()],
        out_specs=[vmem(), smem(), vmem(), vmem()],
        out_shape=[
            sds((MAXD, BLK, BLK), jnp.float32),
            sds((2 * LIST,), jnp.int32),
            sds((USERS, BLK, 64), jnp.float32),
            sds((USERS, 8, 64), jnp.int32),
        ],
        name="prepare",
        cost_estimate=cost(1 << 28, 4 << 20),
        compiler_params=GRANT,
    )(hist_blocks, rab_slope, beam_nodes, subtree_map[None, :])

    near_kv = jnp.stack([value[:ROW_Q] for value in near_got])
    near_cross = seq_xor(near_kv, 4)
    far_kv = jnp.stack([value[:ROW_Q] for value in far_got])
    far_cross = seq_xor(far_kv, 4)

    by_head = [None] * 8
    for q, value in zip(NEAR + FAR, near_got + far_got):
        by_head[q] = value
    part, queries = pl.pallas_call(
        attend_first_kernel,
        in_specs=[smem()] + [vmem()] * 10,
        out_specs=[vmem(), vmem()],
        out_shape=[sds((8, BLK, HD), jnp.float32), sds((8, BLK, HD))],
        scratch_shapes=[pltpu.VMEM((16, ROW_Q, HD), jnp.bfloat16), pltpu.VMEM((9, BLK, HD), jnp.float32)],
        name="attend_first",
        cost_estimate=cost(1 << 31, 4 << 20),
        compiler_params=GRANT,
    )(pairs, bias, *by_head, near_cross)

    back = pl.pallas_call(
        attend_last_kernel,
        in_specs=[smem()] * 3 + [vmem()] * 5,
        out_specs=vmem(),
        out_shape=sds((8, ROWS_B, HD)),
        scratch_shapes=[pltpu.VMEM((9, BLK, HD), jnp.float32)],
        name="attend_last",
        cost_estimate=cost(1 << 30, 2 << 20),
        compiler_params=GRANT,
    )(hist_blocks, hist_tail, pairs, bias, queries, far_cross, part, extra)
    back, table = lax.optimization_barrier((back, table))

    mixed = lax.all_to_all(back, "seq", 0, 0, tiled=True, axis_index_groups=SETS)

    sent = pl.pallas_call(
        state_kernel,
        in_specs=[smem()] + [vmem()] * 7,
        out_specs=vmem(),
        out_shape=sds((NSEQ, 16, 128), jnp.float32),
        name="state",
        cost_estimate=cost(2 * 16 * D * D, 3 << 20),
        compiler_params=GRANT,
    )(hist_blocks, mixed, out_gain[None, :], w_out, *table)
    scores = lax.all_to_all(sent, "seq", 0, 0, tiled=True)

    layer_rows = pl.pallas_call(
        layer_kernel,
        in_specs=[vmem()] * 5,
        out_specs=vmem(),
        out_shape=sds((BLK, D)),
        name="layer",
        cost_estimate=cost(2 * BLK * D * D, 3 << 20),
        compiler_params=GRANT,
    )(mixed, gate, x_rows, out_gain[None, :], w_out)

    beam_scores = pl.pallas_call(
        pick_kernel,
        in_specs=[vmem()] * 3,
        out_specs=vmem(),
        out_shape=sds((USERS, 64), jnp.float32),
        name="pick",
        cost_estimate=cost(1 << 20, 1 << 17),
        compiler_params=GRANT,
    )(scores, hot, rows)
    return (layer_rows[None], beam_scores)


def solution(mesh):
    placed = (
        P("dp", "seq", None),
        P(),
        P(),
        P(),
        P(),
        P(),
        P("dp", None),
        P("dp", None),
        P("dp", None),
        P(),
        P("dp", "seq"),
    )
    return jax.shard_map(
        body,
        mesh=mesh,
        in_specs=placed,
        out_specs=(P("dp", "seq", None), P("dp", "seq")),
        check_vma=False,
    )
```

```python
import jax
import jax.numpy as jnp
from jax import lax
from jax.experimental import pallas as pl
from jax.experimental.pallas import tpu as pltpu
from jax.sharding import PartitionSpec as P


BLK = 128
SUBT = 64
USERS = 3
D = 1024
HEADS = 8
HD = 128
NSEQ = 16
MAXD = 10
UNROLL = 4
MASKED = -1e30
ROW_K, ROW_V, ROW_Q, ROWS_A = 0, 128, 256, 384
ROW_E, ROW_X, ROWS_B = 128, 144, 160
FAR = (2, 3, 6, 7)
NEAR = (0, 1, 4, 5)
SETS = [[0, 1, 2, 3, 8, 9, 10, 11], [4, 5, 6, 7, 12, 13, 14, 15]]
LIST = 128
GRANT = pltpu.CompilerParams(vmem_limit_bytes=16 << 20)


def head_of(seq):
    return (seq // 8) * 4 + seq % 4


def set_of(seq):
    return (seq // 4) % 2


def spread(q):
    return (q // 4) * 8 + q % 4


def place_of(q):
    return q % 2 + (q // 4) * 2 + ((q // 2) % 2) * 4


def silu(x):
    half = 0.5 * x
    return half + half * jnp.tanh(half)


def layer_norm(rows):
    centred = rows - jnp.mean(rows, axis=-1, keepdims=True)
    spread_ = jnp.mean(centred * centred, axis=-1, keepdims=True)
    return centred * lax.rsqrt(spread_ + 1e-05)


def user_starts(blocks_ref):
    one = blocks_ref[0, 0]
    return (0, one, one + blocks_ref[0, 1])


def project_kernel(blocks_ref, tail_ref, x_ref, gain_ref, w_ref, gate_ref, extra_ref, *refs):
    out_refs, weights, sems = refs[:HEADS], refs[HEADS], refs[HEADS + 1]
    me = lax.axis_index("seq")
    order = FAR + NEAR

    def copies(at):
        head = head_of(me) ^ order[at]
        return [
            pltpu.make_async_copy(
                w_ref.at[:, pl.ds(pl.multiple_of((group * HEADS + head) * HD, HD), HD)],
                weights.at[at, :, group * HD : (group + 1) * HD],
                sems.at[at, group],
            )
            for group in range(4)
        ]

    for at in range(HEADS):
        for copy in copies(at):
            copy.start()
    normed = (layer_norm(x_ref[...].astype(jnp.float32)) * gain_ref[...]).astype(jnp.bfloat16)
    for at, out_ref in enumerate(out_refs):
        for copy in copies(at):
            copy.wait()
        parts = silu(jnp.dot(normed, weights[at], preferred_element_type=jnp.float32))
        head = head_of(me) ^ order[at]
        gate_ref[:, pl.ds(pl.multiple_of(head * HD, HD), HD)] = parts[:, :HD].astype(jnp.bfloat16)
        out_ref[ROW_K:ROW_V, :] = parts[:, 2 * HD : 3 * HD].T.astype(jnp.bfloat16)
        out_ref[ROW_V:ROW_Q, :] = parts[:, 3 * HD :].astype(jnp.bfloat16)
        out_ref[ROW_Q:ROWS_A, :] = parts[:, HD : 2 * HD].astype(jnp.bfloat16)

    starts = user_starts(blocks_ref)
    last = jnp.int32(-1)
    for user in range(USERS):
        last = jnp.where(starts[user] + blocks_ref[0, user] - 1 == me, tail_ref[0, user] - 1, last)
    pick = (lax.broadcasted_iota(jnp.int32, (16, BLK), 1) == last).astype(jnp.bfloat16)
    gate_row = jnp.dot(pick, gate_ref[...], preferred_element_type=jnp.float32)[0:1]
    token_row = jnp.dot(pick, x_ref[...], preferred_element_type=jnp.float32)[0:1]
    pieces = [row[:, h * HD : (h + 1) * HD] for row in (gate_row, token_row) for h in range(HEADS)]
    extra_ref[...] = jnp.concatenate(pieces, axis=0).astype(jnp.bfloat16)


def prepare_kernel(
    blocks_ref, slope_ref, ids_ref, map_ref, bias_ref, list_ref, place_ref
):
    me, dp = lax.axis_index("seq"), lax.axis_index("dp")
    starts = user_starts(blocks_ref)
    slope = slope_ref[head_of(me)]
    offset = lax.broadcasted_iota(jnp.int32, (BLK, BLK), 0) - lax.broadcasted_iota(jnp.int32, (BLK, BLK), 1)
    for d in range(MAXD):
        gap = offset + d * BLK
        table = slope * jnp.log1p(jnp.maximum(gap, 0).astype(jnp.float32))
        bias_ref[d] = jnp.where(gap >= 0, table, MASKED) if d == 0 else table

    def fill(t, counts):
        b = (t // 4) * 8 + set_of(me) * 4 + t % 4
        begin = jnp.where(b >= starts[2], starts[2], jnp.where(b >= starts[1], starts[1], 0))

        def put(j, counts):
            apart = j ^ me
            cross = (apart // 4) % 2
            q = (apart // 8) * 4 + apart % 4
            late = cross * ((q // 2) % 2)
            code = (place_of(t ^ head_of(me)) * 16 + cross * 8 + place_of(q)) * 16 + b - j
            first, second = counts
            list_ref[jnp.where(late == 1, LIST + second, first)] = code
            return (first + 1 - late, second + late)

        return lax.fori_loop(begin, b + 1, put, counts)

    counts = lax.fori_loop(0, 8, fill, (jnp.int32(0), jnp.int32(0)))
    for which, count in enumerate(counts):
        for pad in range(UNROLL - 1):
            list_ref[which * LIST + count + pad] = 8 * 256
        list_ref[which * LIST + LIST - 1] = (count + UNROLL - 1) // UNROLL

    my_x, my_zh, my_c = dp // 4, (dp // 2) % 2, dp % 2
    subtree = lax.broadcasted_iota(jnp.int32, (64, 64), 0)
    diagonal = subtree == lax.broadcasted_iota(jnp.int32, (64, 64), 1)
    places = jnp.sum(jnp.where(diagonal, map_ref[...], 0), axis=1, keepdims=True)
    for user in range(USERS):
        end = starts[user] + blocks_ref[0, user] - 1
        ids = ids_ref[user : user + 1, :]
        block = jnp.sum(jnp.where(subtree == ids // SUBT, places, 0), axis=0, keepdims=True)
        row = block * SUBT + ids % SUBT
        owner, inside = row // 256, row % 256
        shard, at = inside // 32, inside % 32
        x_rel = (my_x - owner // 4 + 4) % 4
        zh_rel = (my_zh - (owner // 2) % 2 + 2) % 2
        c_rel = (my_c - owner % 2 + 2) % 2
        lane = c_rel * 64 + zh_rel * 32 + at
        source = (shard // 4) * 8 + set_of(end) * 4 + shard % 4
        place_ref[2 * user : 2 * user + 1, :] = source * 16 + user * 4 + x_rel
        place_ref[2 * user + 1 : 2 * user + 2, :] = lane


def run_pairs(list_ref, which, query, keys, values, bias_ref, acc):
    scale = HD ** (-0.5)

    def some(step, carry):
        products, targets = [], []
        for t in range(UNROLL):
            code = list_ref[which * LIST + step * UNROLL + t]
            mine, slot, d = code // 256, (code // 16) % 16, code % 16
            scores = jnp.dot(query(jnp.minimum(mine, 7)), keys(slot), preferred_element_type=jnp.float32)
            weights = silu(scores * scale + bias_ref[d]).astype(jnp.bfloat16)
            products.append(jnp.dot(weights, values(slot), preferred_element_type=jnp.float32))
            targets.append(mine)
        for mine, product in zip(targets, products):
            acc[mine] += product
        return carry

    lax.fori_loop(0, list_ref[which * LIST + LIST - 1], some, 0)


def sort_kernel(*refs):
    got_refs, kv_ref, queries_ref = refs[:4], refs[4], refs[5]
    for at, got_ref in enumerate(got_refs):
        kv_ref[at] = got_ref[ROW_K:ROW_Q, :]
        queries_ref[at] = got_ref[ROW_Q:ROWS_A, :]


def attend_first_kernel(
    list_ref, bias_ref, near_ref, far_ref, cross_ref, near_q_ref, far_q_ref, acc_ref, queries_ref, keep, acc
):
    for at in range(4):
        keep[at] = near_ref[at]
        keep[4 + at] = far_ref[at]
        keep[8 + at] = cross_ref[at]
        queries_ref[at] = near_q_ref[at]
        queries_ref[4 + at] = far_q_ref[at]
    acc[...] = jnp.zeros_like(acc)
    run_pairs(
        list_ref,
        0,
        lambda mine: queries_ref[mine],
        lambda slot: keep[slot, ROW_K:ROW_V, :],
        lambda slot: keep[slot, ROW_V:ROW_Q, :],
        bias_ref,
        acc,
    )
    acc_ref[...] = acc[0:8]


def attend_last_kernel(blocks_ref, tail_ref, list_ref, bias_ref, queries_ref, cross_ref, acc_ref, extra_ref, out_ref, acc):
    me = lax.axis_index("seq")
    mine = head_of(me)
    starts = user_starts(blocks_ref)
    acc[0:8] = acc_ref[...]
    acc[8] = jnp.zeros((BLK, HD), jnp.float32)

    def at(slot):
        return slot % 4

    run_pairs(
        list_ref,
        1,
        lambda own: queries_ref[own],
        lambda slot: cross_ref[at(slot), ROW_K:ROW_V, :],
        lambda slot: cross_ref[at(slot), ROW_V:ROW_Q, :],
        bias_ref,
        acc,
    )
    rows = []
    for user in range(USERS):
        end = starts[user] + blocks_ref[0, user] - 1
        here = set_of(end) == set_of(me)
        value = acc[place_of(head_of(end) ^ mine), pl.ds(tail_ref[0, user] - 1, 1), :]
        rows.append(jnp.where(here, value, 0.0))
    last = jnp.concatenate(rows + [jnp.zeros((16 - USERS, HD), jnp.float32)], axis=0).astype(jnp.bfloat16)
    row_at = lax.broadcasted_iota(jnp.int32, (BLK, HD), 0)
    for t in range(8):
        b = (t // 4) * 8 + set_of(me) * 4 + t % 4
        valid = jnp.int32(BLK)
        for user in range(USERS):
            valid = jnp.where(starts[user] + blocks_ref[0, user] - 1 == b, tail_ref[0, user], valid)
        out_ref[t, 0:ROW_E, :] = jnp.where(row_at < valid, acc[place_of(mine ^ t)], 0.0).astype(jnp.bfloat16)
        out_ref[t, ROW_E:ROW_X, :] = last
        out_ref[t, ROW_X:ROWS_B, :] = extra_ref[...]


def state_kernel(blocks_ref, mixed_ref, gain_ref, w_ref, ta_ref, tb_ref, tc_ref, td_ref, score_ref, table, sems):
    copies = [
        pltpu.make_async_copy(t_ref, table.at[x], sems.at[x]) for x, t_ref in enumerate((ta_ref, tb_ref, tc_ref, td_ref))
    ]
    for copy in copies:
        copy.start()
    starts = user_starts(blocks_ref)
    tail = jnp.concatenate([mixed_ref[h, ROW_E:ROW_X, :].astype(jnp.float32) for h in range(HEADS)], axis=1)
    gates, tokens = [], []
    for user in range(USERS):
        end = starts[user] + blocks_ref[0, user] - 1
        rows = mixed_ref[head_of(end), ROW_X:ROWS_B, :].astype(jnp.float32)
        gates.append(jnp.concatenate([rows[h : h + 1] for h in range(HEADS)], axis=1))
        tokens.append(jnp.concatenate([rows[HEADS + h : HEADS + h + 1] for h in range(HEADS)], axis=1))
    zeros = jnp.zeros((16 - USERS, D), jnp.float32)
    gate_tail = jnp.concatenate(gates + [zeros], axis=0)
    token_tail = jnp.concatenate(tokens + [zeros], axis=0)
    gated = (layer_norm(tail) * gain_ref[...] * gate_tail).astype(jnp.bfloat16)
    states = (token_tail + jnp.dot(gated, w_ref[...], preferred_element_type=jnp.float32)).astype(jnp.bfloat16)
    for copy in copies:
        copy.wait()
    parts = [
        lax.dot_general(states, table[x], (((1,), (1,)), ((), ())), preferred_element_type=jnp.float32) for x in range(4)
    ]
    rows = [part[user : user + 1] for user in range(USERS) for part in parts]
    block = jnp.concatenate(rows + [jnp.zeros((4, 128), jnp.float32)], axis=0)
    for to in range(NSEQ):
        score_ref[to] = block


def layer_kernel(mixed_ref, gate_ref, x_ref, gain_ref, w_ref, out_ref):
    mixed = jnp.concatenate([mixed_ref[h, 0:ROW_E, :].astype(jnp.float32) for h in range(HEADS)], axis=1)
    gated = (layer_norm(mixed) * gain_ref[...] * gate_ref[...].astype(jnp.float32)).astype(jnp.bfloat16)
    out_ref[...] = (
        x_ref[...].astype(jnp.float32) + jnp.dot(gated, w_ref[...], preferred_element_type=jnp.float32)
    ).astype(jnp.bfloat16)


def pick_kernel(score_ref, place_ref, out_ref):
    scores = score_ref[...].reshape(NSEQ * 16, 128)
    row_at = lax.broadcasted_iota(jnp.int32, (NSEQ * 16, 64), 0)
    lane_at = lax.broadcasted_iota(jnp.int32, (128, 64), 0)
    for user in range(USERS):
        row, lane = place_ref[2 * user : 2 * user + 1, :], place_ref[2 * user + 1 : 2 * user + 2, :]
        found = jnp.dot(
            scores,
            (lane_at == lane).astype(jnp.float32),
            preferred_element_type=jnp.float32,
            precision=lax.Precision.HIGHEST,
        )
        out_ref[user : user + 1, :] = jnp.sum(jnp.where(row_at == row, found, 0.0), axis=0, keepdims=True)


def vmem():
    return pl.BlockSpec(memory_space=pltpu.VMEM)


def in_hbm(value):
    return pltpu.with_memory_space_constraint(value, pltpu.HBM)


def smem():
    return pl.BlockSpec(memory_space=pltpu.SMEM)


def dp_shift(value, move):
    return lax.ppermute(value, "dp", [(i, move(i)) for i in range(16)])


def seq_xor(value, apart):
    return lax.ppermute(value, "seq", [(i, i ^ apart) for i in range(NSEQ)])


def sds(shape, dtype=jnp.bfloat16):
    return jax.ShapeDtypeStruct(shape, dtype)


def cost(flops, read):
    return pl.CostEstimate(flops=flops, bytes_accessed=read, transcendentals=0)


def layer(
    tokens,
    in_gain,
    w_proj,
    out_gain,
    w_out,
    rab_slope,
    hist_blocks,
    hist_tail,
    node_table,
    subtree_map,
    beam_nodes,
):
    x_rows = tokens[0]
    seq = lax.axis_index("seq")
    mine = head_of(seq)

    gate, extra, *sent = pl.pallas_call(
        project_kernel,
        in_specs=[smem(), smem(), vmem(), vmem(), pl.BlockSpec(memory_space=pltpu.HBM)],
        out_specs=[vmem()] * (2 + HEADS),
        out_shape=[pltpu.HBM((BLK, D), jnp.bfloat16), sds((16, HD))] + [sds((ROWS_A, HD))] * HEADS,
        scratch_shapes=[pltpu.VMEM((HEADS, D, 4 * HD), jnp.bfloat16), pltpu.SemaphoreType.DMA((HEADS, 4))],
        name="project",
        cost_estimate=cost(2 * BLK * D * 4 * D, 10 << 20),
        compiler_params=GRANT,
    )(*(in_hbm(value) for value in (hist_blocks, hist_tail, x_rows, in_gain[None, :], w_proj)))
    far_got, near_got = [], [sent[4]]
    for q, value in zip(FAR, sent[:4]):
        far_got.append(seq_xor(value, spread(q)))
    for q, value in zip(NEAR[1:], sent[5:]):
        near_got.append(seq_xor(value, spread(q)))

    bias, pairs, places = pl.pallas_call(
        prepare_kernel,
        in_specs=[smem(), smem(), vmem(), vmem()],
        out_specs=[vmem(), smem(), vmem()],
        out_shape=[
            sds((MAXD, BLK, BLK), jnp.float32),
            sds((2 * LIST,), jnp.int32),
            sds((8, 64), jnp.int32),
        ],
        name="prepare",
        cost_estimate=cost(1 << 28, 4 << 20),
        compiler_params=GRANT,
    )(hist_blocks, rab_slope, beam_nodes, subtree_map[None, :])

    def sort(got):
        return pl.pallas_call(
            sort_kernel,
            in_specs=[vmem()] * 4,
            out_specs=[vmem()] * 2,
            out_shape=[sds((4, ROW_Q, HD)), sds((4, BLK, HD))],
            cost_estimate=cost(1 << 10, 1 << 19),
            compiler_params=GRANT,
        )(*got)

    near_kv, near_q = sort(near_got)
    near_cross = seq_xor(near_kv, 4)
    far_kv, far_q = sort(far_got)
    far_cross = seq_xor(far_kv, 4)

    own = lax.dynamic_slice_in_dim(node_table, mine * 32, 32, 0)
    pair = jnp.concatenate([own, dp_shift(own, lambda i: i ^ 2)], axis=0)
    quad = jnp.concatenate([pair, dp_shift(pair, lambda i: i ^ 1)], axis=0)
    table = [quad]
    for n in (1, 2, 3):
        table.append(dp_shift(quad, lambda i, n=n: (i + 4 * n) % 16))

    part, queries = pl.pallas_call(
        attend_first_kernel,
        in_specs=[smem()] + [vmem()] * 6,
        out_specs=[vmem(), vmem()],
        out_shape=[sds((8, BLK, HD), jnp.float32), sds((8, BLK, HD))],
        scratch_shapes=[pltpu.VMEM((12, ROW_Q, HD), jnp.bfloat16), pltpu.VMEM((9, BLK, HD), jnp.float32)],
        name="attend_first",
        cost_estimate=cost(1 << 31, 4 << 20),
        compiler_params=GRANT,
    )(pairs, bias, near_kv, far_kv, near_cross, near_q, far_q)

    back = pl.pallas_call(
        attend_last_kernel,
        in_specs=[smem()] * 3 + [vmem()] * 5,
        out_specs=vmem(),
        out_shape=sds((8, ROWS_B, HD)),
        scratch_shapes=[pltpu.VMEM((9, BLK, HD), jnp.float32)],
        name="attend_last",
        cost_estimate=cost(1 << 30, 2 << 20),
        compiler_params=GRANT,
    )(hist_blocks, hist_tail, pairs, bias, queries, far_cross, part, extra)

    mixed = lax.all_to_all(back, "seq", 0, 0, tiled=True, axis_index_groups=SETS)

    sent = pl.pallas_call(
        state_kernel,
        in_specs=[smem()] + [vmem()] * 3 + [pl.BlockSpec(memory_space=pltpu.HBM)] * 4,
        out_specs=vmem(),
        out_shape=pltpu.HBM((NSEQ, 16, 128), jnp.float32),
        scratch_shapes=[pltpu.VMEM((4, BLK, D), jnp.bfloat16), pltpu.SemaphoreType.DMA((4,))],
        name="state",
        cost_estimate=cost(2 * 16 * D * D, 3 << 20),
        compiler_params=GRANT,
    )(hist_blocks, mixed, out_gain[None, :], w_out, *(in_hbm(piece) for piece in table))
    scores = lax.all_to_all(sent, "seq", 0, 0, tiled=True)

    layer_rows = pl.pallas_call(
        layer_kernel,
        in_specs=[vmem()] * 5,
        out_specs=vmem(),
        out_shape=sds((BLK, D)),
        name="layer",
        cost_estimate=cost(2 * BLK * D * D, 3 << 20),
        compiler_params=GRANT,
    )(mixed, gate, x_rows, out_gain[None, :], w_out)

    beam_scores = pl.pallas_call(
        pick_kernel,
        in_specs=[vmem()] * 2,
        out_specs=vmem(),
        out_shape=sds((USERS, 64), jnp.float32),
        name="pick",
        cost_estimate=cost(1 << 20, 1 << 17),
        compiler_params=GRANT,
    )(scores, places)
    return (layer_rows[None], beam_scores)


def solution(mesh):
    placed = (
        P("dp", "seq", None),
        P(),
        P(),
        P(),
        P(),
        P(),
        P("dp", None),
        P("dp", None),
        P("dp", None),
        P(),
        P("dp", "seq"),
    )
    return jax.shard_map(
        layer,
        mesh=mesh,
        in_specs=placed,
        out_specs=(P("dp", "seq", None), P("dp", "seq")),
        check_vma=False,
    )
```

```python
import jax
import jax.numpy as jnp
from jax import lax
from jax.experimental import pallas as pl
from jax.experimental.pallas import tpu as pltpu
from jax.sharding import PartitionSpec as P


BLK = 128
SUBT = 64
USERS = 3
D = 1024
HEADS = 8
HD = 128
NSEQ = 16
MAXD = 10
UNROLL = 4
MASKED = -1e30
ROW_K, ROW_V, ROW_Q, ROWS_A = 0, 128, 256, 384
ROW_E, ROW_X, ROWS_B = 128, 144, 160
FAR = (2, 3, 6, 7)
NEAR = (0, 1, 4, 5)
SETS = [[0, 1, 2, 3, 8, 9, 10, 11], [4, 5, 6, 7, 12, 13, 14, 15]]
LIST = 128
GRANT = pltpu.CompilerParams(vmem_limit_bytes=16 << 20)


def head_of(seq):
    return (seq // 8) * 4 + seq % 4


def set_of(seq):
    return (seq // 4) % 2


def spread(q):
    return (q // 4) * 8 + q % 4


def place_of(q):
    return q % 2 + (q // 4) * 2 + ((q // 2) % 2) * 4


def silu(x):
    half = 0.5 * x
    return half + half * jnp.tanh(half)


def layer_norm(rows):
    centred = rows - jnp.mean(rows, axis=-1, keepdims=True)
    spread_ = jnp.mean(centred * centred, axis=-1, keepdims=True)
    return centred * lax.rsqrt(spread_ + 1e-05)


def user_starts(blocks_ref):
    one = blocks_ref[0, 0]
    return (0, one, one + blocks_ref[0, 1])


def project_kernel(blocks_ref, tail_ref, x_ref, gain_ref, w_ref, gate_ref, extra_ref, *refs):
    out_refs, weights, sems = refs[:HEADS], refs[HEADS], refs[HEADS + 1]
    me = lax.axis_index("seq")
    order = FAR + NEAR

    def copies(at):
        head = head_of(me) ^ order[at]
        return [
            pltpu.make_async_copy(
                w_ref.at[:, pl.ds(pl.multiple_of((group * HEADS + head) * HD, HD), HD)],
                weights.at[at, :, group * HD : (group + 1) * HD],
                sems.at[at, group],
            )
            for group in range(4)
        ]

    for at in range(HEADS):
        for copy in copies(at):
            copy.start()
    normed = (layer_norm(x_ref[...].astype(jnp.float32)) * gain_ref[...]).astype(jnp.bfloat16)
    for at, out_ref in enumerate(out_refs):
        for copy in copies(at):
            copy.wait()
        parts = silu(jnp.dot(normed, weights[at], preferred_element_type=jnp.float32))
        head = head_of(me) ^ order[at]
        gate_ref[:, pl.ds(pl.multiple_of(head * HD, HD), HD)] = parts[:, :HD].astype(jnp.bfloat16)
        out_ref[ROW_K:ROW_V, :] = parts[:, 2 * HD : 3 * HD].T.astype(jnp.bfloat16)
        out_ref[ROW_V:ROW_Q, :] = parts[:, 3 * HD :].astype(jnp.bfloat16)
        out_ref[ROW_Q:ROWS_A, :] = parts[:, HD : 2 * HD].astype(jnp.bfloat16)

    starts = user_starts(blocks_ref)
    last = jnp.int32(-1)
    for user in range(USERS):
        last = jnp.where(starts[user] + blocks_ref[0, user] - 1 == me, tail_ref[0, user] - 1, last)
    pick = (lax.broadcasted_iota(jnp.int32, (16, BLK), 1) == last).astype(jnp.bfloat16)
    gate_row = jnp.dot(pick, gate_ref[...], preferred_element_type=jnp.float32)[0:1]
    token_row = jnp.dot(pick, x_ref[...], preferred_element_type=jnp.float32)[0:1]
    pieces = [row[:, h * HD : (h + 1) * HD] for row in (gate_row, token_row) for h in range(HEADS)]
    extra_ref[...] = jnp.concatenate(pieces, axis=0).astype(jnp.bfloat16)


def prepare_kernel(
    blocks_ref, slope_ref, ids_ref, map_ref, bias_ref, list_ref, place_ref
):
    me, dp = lax.axis_index("seq"), lax.axis_index("dp")
    starts = user_starts(blocks_ref)
    slope = slope_ref[head_of(me)]
    offset = lax.broadcasted_iota(jnp.int32, (BLK, BLK), 0) - lax.broadcasted_iota(jnp.int32, (BLK, BLK), 1)
    for d in range(MAXD):
        gap = offset + d * BLK
        table = slope * jnp.log1p(jnp.maximum(gap, 0).astype(jnp.float32))
        bias_ref[d] = jnp.where(gap >= 0, table, MASKED) if d == 0 else table

    def fill(t, counts):
        b = (t // 4) * 8 + set_of(me) * 4 + t % 4
        begin = jnp.where(b >= starts[2], starts[2], jnp.where(b >= starts[1], starts[1], 0))

        def put(j, counts):
            apart = j ^ me
            cross = (apart // 4) % 2
            q = (apart // 8) * 4 + apart % 4
            late = cross * ((q // 2) % 2)
            code = (place_of(t ^ head_of(me)) * 16 + cross * 8 + place_of(q)) * 16 + b - j
            first, second = counts
            list_ref[jnp.where(late == 1, LIST + second, first)] = code
            return (first + 1 - late, second + late)

        return lax.fori_loop(begin, b + 1, put, counts)

    counts = lax.fori_loop(0, 8, fill, (jnp.int32(0), jnp.int32(0)))
    for which, count in enumerate(counts):
        for pad in range(UNROLL - 1):
            list_ref[which * LIST + count + pad] = 8 * 256
        list_ref[which * LIST + LIST - 1] = (count + UNROLL - 1) // UNROLL

    my_x, my_zh, my_c = dp // 4, (dp // 2) % 2, dp % 2
    subtree = lax.broadcasted_iota(jnp.int32, (64, 64), 0)
    diagonal = subtree == lax.broadcasted_iota(jnp.int32, (64, 64), 1)
    places = jnp.sum(jnp.where(diagonal, map_ref[...], 0), axis=1, keepdims=True)
    for user in range(USERS):
        end = starts[user] + blocks_ref[0, user] - 1
        ids = ids_ref[user : user + 1, :]
        block = jnp.sum(jnp.where(subtree == ids // SUBT, places, 0), axis=0, keepdims=True)
        row = block * SUBT + ids % SUBT
        owner, inside = row // 256, row % 256
        shard, at = inside // 32, inside % 32
        x_rel = (my_x - owner // 4 + 4) % 4
        zh_rel = (my_zh - (owner // 2) % 2 + 2) % 2
        c_rel = (my_c - owner % 2 + 2) % 2
        lane = c_rel * 64 + zh_rel * 32 + at
        source = (shard // 4) * 8 + set_of(end) * 4 + shard % 4
        place_ref[2 * user : 2 * user + 1, :] = source * 16 + user * 4 + x_rel
        place_ref[2 * user + 1 : 2 * user + 2, :] = lane


def run_pairs(list_ref, which, query, keys, values, bias_ref, acc):
    scale = HD ** (-0.5)

    def some(step, carry):
        products, targets = [], []
        for t in range(UNROLL):
            code = list_ref[which * LIST + step * UNROLL + t]
            mine, slot, d = code // 256, (code // 16) % 16, code % 16
            scores = jnp.dot(query(jnp.minimum(mine, 7)), keys(slot), preferred_element_type=jnp.float32)
            weights = silu(scores * scale + bias_ref[d]).astype(jnp.bfloat16)
            products.append(jnp.dot(weights, values(slot), preferred_element_type=jnp.float32))
            targets.append(mine)
        for mine, product in zip(targets, products):
            acc[mine] += product
        return carry

    lax.fori_loop(0, list_ref[which * LIST + LIST - 1], some, 0)


def sort_kernel(*refs):
    got_refs, kv_ref, queries_ref = refs[:4], refs[4], refs[5]
    for at, got_ref in enumerate(got_refs):
        kv_ref[at] = got_ref[ROW_K:ROW_Q, :]
        queries_ref[at] = got_ref[ROW_Q:ROWS_A, :]


def attend_first_kernel(
    list_ref, bias_ref, near_ref, far_ref, cross_ref, near_q_ref, far_q_ref, acc_ref, queries_ref, keep, acc
):
    for at in range(4):
        keep[at] = near_ref[at]
        keep[4 + at] = far_ref[at]
        keep[8 + at] = cross_ref[at]
        queries_ref[at] = near_q_ref[at]
        queries_ref[4 + at] = far_q_ref[at]
    acc[...] = jnp.zeros_like(acc)
    run_pairs(
        list_ref,
        0,
        lambda mine: queries_ref[mine],
        lambda slot: keep[slot, ROW_K:ROW_V, :],
        lambda slot: keep[slot, ROW_V:ROW_Q, :],
        bias_ref,
        acc,
    )
    acc_ref[...] = acc[0:8]


def attend_last_kernel(blocks_ref, tail_ref, list_ref, bias_ref, queries_ref, cross_ref, acc_ref, extra_ref, out_ref, acc):
    me = lax.axis_index("seq")
    mine = head_of(me)
    starts = user_starts(blocks_ref)
    acc[0:8] = acc_ref[...]
    acc[8] = jnp.zeros((BLK, HD), jnp.float32)

    def at(slot):
        return slot % 4

    run_pairs(
        list_ref,
        1,
        lambda own: queries_ref[own],
        lambda slot: cross_ref[at(slot), ROW_K:ROW_V, :],
        lambda slot: cross_ref[at(slot), ROW_V:ROW_Q, :],
        bias_ref,
        acc,
    )
    rows = []
    for user in range(USERS):
        end = starts[user] + blocks_ref[0, user] - 1
        here = set_of(end) == set_of(me)
        value = acc[place_of(head_of(end) ^ mine), pl.ds(tail_ref[0, user] - 1, 1), :]
        rows.append(jnp.where(here, value, 0.0))
    last = jnp.concatenate(rows + [jnp.zeros((16 - USERS, HD), jnp.float32)], axis=0).astype(jnp.bfloat16)
    row_at = lax.broadcasted_iota(jnp.int32, (BLK, HD), 0)
    for t in range(8):
        b = (t // 4) * 8 + set_of(me) * 4 + t % 4
        valid = jnp.int32(BLK)
        for user in range(USERS):
            valid = jnp.where(starts[user] + blocks_ref[0, user] - 1 == b, tail_ref[0, user], valid)
        out_ref[t, 0:ROW_E, :] = jnp.where(row_at < valid, acc[place_of(mine ^ t)], 0.0).astype(jnp.bfloat16)
        out_ref[t, ROW_E:ROW_X, :] = last
        out_ref[t, ROW_X:ROWS_B, :] = extra_ref[...]


def state_kernel(blocks_ref, mixed_ref, gain_ref, w_ref, ta_ref, tb_ref, tc_ref, td_ref, score_ref):
    starts = user_starts(blocks_ref)
    tail = jnp.concatenate([mixed_ref[h, ROW_E:ROW_X, :].astype(jnp.float32) for h in range(HEADS)], axis=1)
    gates, tokens = [], []
    for user in range(USERS):
        end = starts[user] + blocks_ref[0, user] - 1
        rows = mixed_ref[head_of(end), ROW_X:ROWS_B, :].astype(jnp.float32)
        gates.append(jnp.concatenate([rows[h : h + 1] for h in range(HEADS)], axis=1))
        tokens.append(jnp.concatenate([rows[HEADS + h : HEADS + h + 1] for h in range(HEADS)], axis=1))
    zeros = jnp.zeros((16 - USERS, D), jnp.float32)
    gate_tail = jnp.concatenate(gates + [zeros], axis=0)
    token_tail = jnp.concatenate(tokens + [zeros], axis=0)
    gated = (layer_norm(tail) * gain_ref[...] * gate_tail).astype(jnp.bfloat16)
    states = (token_tail + jnp.dot(gated, w_ref[...], preferred_element_type=jnp.float32)).astype(jnp.bfloat16)
    parts = [
        lax.dot_general(states, t_ref[...], (((1,), (1,)), ((), ())), preferred_element_type=jnp.float32)
        for t_ref in (ta_ref, tb_ref, tc_ref, td_ref)
    ]
    rows = [part[user : user + 1] for user in range(USERS) for part in parts]
    block = jnp.concatenate(rows + [jnp.zeros((4, 128), jnp.float32)], axis=0)
    for to in range(NSEQ):
        score_ref[to] = block


def layer_kernel(mixed_ref, gate_ref, x_ref, gain_ref, w_ref, out_ref):
    mixed = jnp.concatenate([mixed_ref[h, 0:ROW_E, :].astype(jnp.float32) for h in range(HEADS)], axis=1)
    gated = (layer_norm(mixed) * gain_ref[...] * gate_ref[...].astype(jnp.float32)).astype(jnp.bfloat16)
    out_ref[...] = (
        x_ref[...].astype(jnp.float32) + jnp.dot(gated, w_ref[...], preferred_element_type=jnp.float32)
    ).astype(jnp.bfloat16)


def pick_kernel(score_ref, place_ref, out_ref):
    scores = score_ref[...].reshape(NSEQ * 16, 128)
    row_at = lax.broadcasted_iota(jnp.int32, (NSEQ * 16, 64), 0)
    lane_at = lax.broadcasted_iota(jnp.int32, (128, 64), 0)
    for user in range(USERS):
        row, lane = place_ref[2 * user : 2 * user + 1, :], place_ref[2 * user + 1 : 2 * user + 2, :]
        found = jnp.dot(
            scores,
            (lane_at == lane).astype(jnp.float32),
            preferred_element_type=jnp.float32,
            precision=lax.Precision.HIGHEST,
        )
        out_ref[user : user + 1, :] = jnp.sum(jnp.where(row_at == row, found, 0.0), axis=0, keepdims=True)


def vmem():
    return pl.BlockSpec(memory_space=pltpu.VMEM)


def in_hbm(value):
    return pltpu.with_memory_space_constraint(value, pltpu.HBM)


def smem():
    return pl.BlockSpec(memory_space=pltpu.SMEM)


def dp_shift(value, move):
    return lax.ppermute(value, "dp", [(i, move(i)) for i in range(16)])


def seq_xor(value, apart):
    return lax.ppermute(value, "seq", [(i, i ^ apart) for i in range(NSEQ)])


def sds(shape, dtype=jnp.bfloat16):
    return jax.ShapeDtypeStruct(shape, dtype)


def cost(flops, read):
    return pl.CostEstimate(flops=flops, bytes_accessed=read, transcendentals=0)


def layer(
    tokens,
    in_gain,
    w_proj,
    out_gain,
    w_out,
    rab_slope,
    hist_blocks,
    hist_tail,
    node_table,
    subtree_map,
    beam_nodes,
):
    x_rows = tokens[0]
    seq = lax.axis_index("seq")
    mine = head_of(seq)

    gate, extra, *sent = pl.pallas_call(
        project_kernel,
        in_specs=[smem(), smem(), vmem(), vmem(), pl.BlockSpec(memory_space=pltpu.HBM)],
        out_specs=[vmem()] * (2 + HEADS),
        out_shape=[pltpu.HBM((BLK, D), jnp.bfloat16), sds((16, HD))] + [sds((ROWS_A, HD))] * HEADS,
        scratch_shapes=[pltpu.VMEM((HEADS, D, 4 * HD), jnp.bfloat16), pltpu.SemaphoreType.DMA((HEADS, 4))],
        name="project",
        cost_estimate=cost(2 * BLK * D * 4 * D, 10 << 20),
        compiler_params=GRANT,
    )(*(in_hbm(value) for value in (hist_blocks, hist_tail, x_rows, in_gain[None, :], w_proj)))
    far_got, near_got = [], [sent[4]]
    for q, value in zip(FAR, sent[:4]):
        far_got.append(seq_xor(value, spread(q)))
    for q, value in zip(NEAR[1:], sent[5:]):
        near_got.append(seq_xor(value, spread(q)))

    bias, pairs, places = pl.pallas_call(
        prepare_kernel,
        in_specs=[smem(), smem(), vmem(), vmem()],
        out_specs=[vmem(), smem(), vmem()],
        out_shape=[
            sds((MAXD, BLK, BLK), jnp.float32),
            sds((2 * LIST,), jnp.int32),
            sds((8, 64), jnp.int32),
        ],
        name="prepare",
        cost_estimate=cost(1 << 28, 4 << 20),
        compiler_params=GRANT,
    )(hist_blocks, rab_slope, beam_nodes, subtree_map[None, :])

    def sort(got):
        return pl.pallas_call(
            sort_kernel,
            in_specs=[vmem()] * 4,
            out_specs=[vmem()] * 2,
            out_shape=[sds((4, ROW_Q, HD)), sds((4, BLK, HD))],
            cost_estimate=cost(1 << 10, 1 << 19),
            compiler_params=GRANT,
        )(*got)

    near_kv, near_q = sort(near_got)
    near_cross = seq_xor(near_kv, 4)
    far_kv, far_q = sort(far_got)
    far_cross = seq_xor(far_kv, 4)

    own = lax.dynamic_slice_in_dim(node_table, mine * 32, 32, 0)
    pair = jnp.concatenate([own, dp_shift(own, lambda i: i ^ 2)], axis=0)
    quad = jnp.concatenate([pair, dp_shift(pair, lambda i: i ^ 1)], axis=0)
    table = [quad]
    for n in (1, 2, 3):
        table.append(dp_shift(quad, lambda i, n=n: (i + 4 * n) % 16))

    part, queries = pl.pallas_call(
        attend_first_kernel,
        in_specs=[smem()] + [vmem()] * 6,
        out_specs=[vmem(), vmem()],
        out_shape=[sds((8, BLK, HD), jnp.float32), sds((8, BLK, HD))],
        scratch_shapes=[pltpu.VMEM((12, ROW_Q, HD), jnp.bfloat16), pltpu.VMEM((9, BLK, HD), jnp.float32)],
        name="attend_first",
        cost_estimate=cost(1 << 31, 4 << 20),
        compiler_params=GRANT,
    )(pairs, bias, near_kv, far_kv, near_cross, near_q, far_q)

    back = pl.pallas_call(
        attend_last_kernel,
        in_specs=[smem()] * 3 + [vmem()] * 5,
        out_specs=vmem(),
        out_shape=sds((8, ROWS_B, HD)),
        scratch_shapes=[pltpu.VMEM((9, BLK, HD), jnp.float32)],
        name="attend_last",
        cost_estimate=cost(1 << 30, 2 << 20),
        compiler_params=GRANT,
    )(hist_blocks, hist_tail, pairs, bias, queries, far_cross, part, extra)

    mixed = lax.all_to_all(back, "seq", 0, 0, tiled=True, axis_index_groups=SETS)

    sent = pl.pallas_call(
        state_kernel,
        in_specs=[smem()] + [vmem()] * 7,
        out_specs=vmem(),
        out_shape=pltpu.HBM((NSEQ, 16, 128), jnp.float32),
        name="state",
        cost_estimate=cost(2 * 16 * D * D, 3 << 20),
        compiler_params=GRANT,
    )(hist_blocks, mixed, out_gain[None, :], w_out, *table)
    scores = lax.all_to_all(sent, "seq", 0, 0, tiled=True)

    layer_rows = pl.pallas_call(
        layer_kernel,
        in_specs=[vmem()] * 5,
        out_specs=vmem(),
        out_shape=sds((BLK, D)),
        name="layer",
        cost_estimate=cost(2 * BLK * D * D, 3 << 20),
        compiler_params=GRANT,
    )(mixed, gate, x_rows, out_gain[None, :], w_out)

    beam_scores = pl.pallas_call(
        pick_kernel,
        in_specs=[vmem()] * 2,
        out_specs=vmem(),
        out_shape=sds((USERS, 64), jnp.float32),
        name="pick",
        cost_estimate=cost(1 << 20, 1 << 17),
        compiler_params=GRANT,
    )(scores, places)
    return (layer_rows[None], beam_scores)


def solution(mesh):
    placed = (
        P("dp", "seq", None),
        P(),
        P(),
        P(),
        P(),
        P(),
        P("dp", None),
        P("dp", None),
        P("dp", None),
        P(),
        P("dp", "seq"),
    )
    return jax.shard_map(
        layer,
        mesh=mesh,
        in_specs=placed,
        out_specs=(P("dp", "seq", None), P("dp", "seq")),
        check_vma=False,
    )
```

```python
import jax
import jax.numpy as jnp
from jax import lax
from jax.experimental import pallas as pl
from jax.experimental.pallas import tpu as pltpu
from jax.sharding import PartitionSpec as P


BLK = 128
SUBT = 64
USERS = 3
D = 1024
HEADS = 8
HD = 128
NSEQ = 16
MAXD = 10
UNROLL = 4
MASKED = -1e30
ROW_K, ROW_V, ROW_Q, ROWS_A = 0, 128, 256, 384
ROW_E, ROW_X, ROWS_B = 128, 144, 160
FAR = (2, 3, 6, 7)
NEAR = (0, 1, 4, 5)
SETS = [[0, 1, 2, 3, 8, 9, 10, 11], [4, 5, 6, 7, 12, 13, 14, 15]]
LIST = 128
GRANT = pltpu.CompilerParams(vmem_limit_bytes=16 << 20)


def head_of(seq):
    return (seq // 8) * 4 + seq % 4


def set_of(seq):
    return (seq // 4) % 2


def spread(q):
    return (q // 4) * 8 + q % 4


def place_of(q):
    return q % 2 + (q // 4) * 2 + ((q // 2) % 2) * 4


def silu(x):
    half = 0.5 * x
    return half + half * jnp.tanh(half)


def layer_norm(rows):
    centred = rows - jnp.mean(rows, axis=-1, keepdims=True)
    spread_ = jnp.mean(centred * centred, axis=-1, keepdims=True)
    return centred * lax.rsqrt(spread_ + 1e-05)


def user_starts(blocks_ref):
    one = blocks_ref[0, 0]
    return (0, one, one + blocks_ref[0, 1])


def message(parts, out_ref):
    out_ref[ROW_K:ROW_V, :] = parts[:, HD : 2 * HD].T.astype(jnp.bfloat16)
    out_ref[ROW_V:ROW_Q, :] = parts[:, 2 * HD :].astype(jnp.bfloat16)
    out_ref[ROW_Q:ROWS_A, :] = parts[:, :HD].astype(jnp.bfloat16)


def project_far_kernel(x_ref, gain_ref, w_ref, normed_ref, *refs):
    out_refs, weights, sems = refs[:4], refs[4], refs[5]
    mine = head_of(lax.axis_index("seq"))

    def copies(at):
        head = mine ^ FAR[at]
        return [
            pltpu.make_async_copy(
                w_ref.at[:, pl.ds(pl.multiple_of(((group + 1) * HEADS + head) * HD, HD), HD)],
                weights.at[at, :, group * HD : (group + 1) * HD],
                sems.at[at, group],
            )
            for group in range(3)
        ]

    for at in range(4):
        for copy in copies(at):
            copy.start()
    normed = (layer_norm(x_ref[...].astype(jnp.float32)) * gain_ref[...]).astype(jnp.bfloat16)
    normed_ref[...] = normed
    for at, out_ref in enumerate(out_refs):
        for copy in copies(at):
            copy.wait()
        message(silu(jnp.dot(normed, weights[at], preferred_element_type=jnp.float32)), out_ref)


def project_near_kernel(blocks_ref, tail_ref, x_ref, normed_ref, w_ref, gate_ref, extra_ref, *out_refs):
    me = lax.axis_index("seq")
    normed = normed_ref[...]
    for q, out_ref in zip(NEAR, out_refs):
        head = head_of(me) ^ q

        def part(group, head=head):
            columns = pl.ds(pl.multiple_of((group * HEADS + head) * HD, HD), HD)
            return silu(jnp.dot(normed, w_ref[:, columns], preferred_element_type=jnp.float32))

        message(jnp.concatenate([part(1), part(2), part(3)], axis=1), out_ref)
    gate = silu(jnp.dot(normed, w_ref[:, :D], preferred_element_type=jnp.float32)).astype(jnp.bfloat16)
    gate_ref[...] = gate

    starts = user_starts(blocks_ref)
    last = jnp.int32(-1)
    for user in range(USERS):
        last = jnp.where(starts[user] + blocks_ref[0, user] - 1 == me, tail_ref[0, user] - 1, last)
    pick = (lax.broadcasted_iota(jnp.int32, (16, BLK), 1) == last).astype(jnp.bfloat16)
    gate_row = jnp.dot(pick, gate, preferred_element_type=jnp.float32)[0:1]
    token_row = jnp.dot(pick, x_ref[...], preferred_element_type=jnp.float32)[0:1]
    pieces = [row[:, h * HD : (h + 1) * HD] for row in (gate_row, token_row) for h in range(HEADS)]
    extra_ref[...] = jnp.concatenate(pieces, axis=0).astype(jnp.bfloat16)


def prepare_kernel(
    blocks_ref, slope_ref, ids_ref, map_ref, bias_ref, list_ref, place_ref
):
    me, dp = lax.axis_index("seq"), lax.axis_index("dp")
    starts = user_starts(blocks_ref)
    slope = slope_ref[head_of(me)]
    offset = lax.broadcasted_iota(jnp.int32, (BLK, BLK), 0) - lax.broadcasted_iota(jnp.int32, (BLK, BLK), 1)
    for d in range(MAXD):
        gap = offset + d * BLK
        table = slope * jnp.log1p(jnp.maximum(gap, 0).astype(jnp.float32))
        bias_ref[d] = jnp.where(gap >= 0, table, MASKED) if d == 0 else table

    def fill(t, counts):
        b = (t // 4) * 8 + set_of(me) * 4 + t % 4
        begin = jnp.where(b >= starts[2], starts[2], jnp.where(b >= starts[1], starts[1], 0))

        def put(j, counts):
            apart = j ^ me
            cross = (apart // 4) % 2
            q = (apart // 8) * 4 + apart % 4
            late = cross * ((q // 2) % 2)
            code = (place_of(t ^ head_of(me)) * 16 + cross * 8 + place_of(q)) * 16 + b - j
            first, second = counts
            list_ref[jnp.where(late == 1, LIST + second, first)] = code
            return (first + 1 - late, second + late)

        return lax.fori_loop(begin, b + 1, put, counts)

    counts = lax.fori_loop(0, 8, fill, (jnp.int32(0), jnp.int32(0)))
    for which, count in enumerate(counts):
        for pad in range(UNROLL - 1):
            list_ref[which * LIST + count + pad] = 8 * 256
        list_ref[which * LIST + LIST - 1] = (count + UNROLL - 1) // UNROLL

    my_x, my_zh, my_c = dp // 4, (dp // 2) % 2, dp % 2
    subtree = lax.broadcasted_iota(jnp.int32, (64, 64), 0)
    diagonal = subtree == lax.broadcasted_iota(jnp.int32, (64, 64), 1)
    places = jnp.sum(jnp.where(diagonal, map_ref[...], 0), axis=1, keepdims=True)
    for user in range(USERS):
        end = starts[user] + blocks_ref[0, user] - 1
        ids = ids_ref[user : user + 1, :]
        block = jnp.sum(jnp.where(subtree == ids // SUBT, places, 0), axis=0, keepdims=True)
        row = block * SUBT + ids % SUBT
        owner, inside = row // 256, row % 256
        shard, at = inside // 32, inside % 32
        x_rel = (my_x - owner // 4 + 4) % 4
        zh_rel = (my_zh - (owner // 2) % 2 + 2) % 2
        c_rel = (my_c - owner % 2 + 2) % 2
        lane = c_rel * 64 + zh_rel * 32 + at
        source = (shard // 4) * 8 + set_of(end) * 4 + shard % 4
        place_ref[2 * user : 2 * user + 1, :] = source * 16 + user * 4 + x_rel
        place_ref[2 * user + 1 : 2 * user + 2, :] = lane


def run_pairs(list_ref, which, query, keys, values, bias_ref, acc):
    scale = HD ** (-0.5)

    def some(step, carry):
        products, targets = [], []
        for t in range(UNROLL):
            code = list_ref[which * LIST + step * UNROLL + t]
            mine, slot, d = code // 256, (code // 16) % 16, code % 16
            scores = jnp.dot(query(jnp.minimum(mine, 7)), keys(slot), preferred_element_type=jnp.float32)
            weights = silu(scores * scale + bias_ref[d]).astype(jnp.bfloat16)
            products.append(jnp.dot(weights, values(slot), preferred_element_type=jnp.float32))
            targets.append(mine)
        for mine, product in zip(targets, products):
            acc[mine] += product
        return carry

    lax.fori_loop(0, list_ref[which * LIST + LIST - 1], some, 0)


def sort_kernel(*refs):
    got_refs, kv_ref, queries_ref = refs[:4], refs[4], refs[5]
    for at, got_ref in enumerate(got_refs):
        kv_ref[at] = got_ref[ROW_K:ROW_Q, :]
        queries_ref[at] = got_ref[ROW_Q:ROWS_A, :]


def attend_first_kernel(
    list_ref, bias_ref, near_ref, far_ref, cross_ref, near_q_ref, far_q_ref, acc_ref, queries_ref, keep, acc
):
    for at in range(4):
        keep[at] = near_ref[at]
        keep[4 + at] = far_ref[at]
        keep[8 + at] = cross_ref[at]
        queries_ref[at] = near_q_ref[at]
        queries_ref[4 + at] = far_q_ref[at]
    acc[...] = jnp.zeros_like(acc)
    run_pairs(
        list_ref,
        0,
        lambda mine: queries_ref[mine],
        lambda slot: keep[slot, ROW_K:ROW_V, :],
        lambda slot: keep[slot, ROW_V:ROW_Q, :],
        bias_ref,
        acc,
    )
    acc_ref[...] = acc[0:8]


def attend_last_kernel(blocks_ref, tail_ref, list_ref, bias_ref, queries_ref, cross_ref, acc_ref, extra_ref, out_ref, acc):
    me = lax.axis_index("seq")
    mine = head_of(me)
    starts = user_starts(blocks_ref)
    acc[0:8] = acc_ref[...]
    acc[8] = jnp.zeros((BLK, HD), jnp.float32)

    def at(slot):
        return slot % 4

    run_pairs(
        list_ref,
        1,
        lambda own: queries_ref[own],
        lambda slot: cross_ref[at(slot), ROW_K:ROW_V, :],
        lambda slot: cross_ref[at(slot), ROW_V:ROW_Q, :],
        bias_ref,
        acc,
    )
    rows = []
    for user in range(USERS):
        end = starts[user] + blocks_ref[0, user] - 1
        here = set_of(end) == set_of(me)
        value = acc[place_of(head_of(end) ^ mine), pl.ds(tail_ref[0, user] - 1, 1), :]
        rows.append(jnp.where(here, value, 0.0))
    last = jnp.concatenate(rows + [jnp.zeros((16 - USERS, HD), jnp.float32)], axis=0).astype(jnp.bfloat16)
    row_at = lax.broadcasted_iota(jnp.int32, (BLK, HD), 0)
    for t in range(8):
        b = (t // 4) * 8 + set_of(me) * 4 + t % 4
        valid = jnp.int32(BLK)
        for user in range(USERS):
            valid = jnp.where(starts[user] + blocks_ref[0, user] - 1 == b, tail_ref[0, user], valid)
        out_ref[t, 0:ROW_E, :] = jnp.where(row_at < valid, acc[place_of(mine ^ t)], 0.0).astype(jnp.bfloat16)
        out_ref[t, ROW_E:ROW_X, :] = last
        out_ref[t, ROW_X:ROWS_B, :] = extra_ref[...]


def state_kernel(blocks_ref, mixed_ref, gain_ref, w_ref, ta_ref, tb_ref, tc_ref, td_ref, te_ref, score_ref):
    starts = user_starts(blocks_ref)
    tail = jnp.concatenate([mixed_ref[h, ROW_E:ROW_X, :].astype(jnp.float32) for h in range(HEADS)], axis=1)
    gates, tokens = [], []
    for user in range(USERS):
        end = starts[user] + blocks_ref[0, user] - 1
        rows = mixed_ref[head_of(end), ROW_X:ROWS_B, :].astype(jnp.float32)
        gates.append(jnp.concatenate([rows[h : h + 1] for h in range(HEADS)], axis=1))
        tokens.append(jnp.concatenate([rows[HEADS + h : HEADS + h + 1] for h in range(HEADS)], axis=1))
    zeros = jnp.zeros((16 - USERS, D), jnp.float32)
    gate_tail = jnp.concatenate(gates + [zeros], axis=0)
    token_tail = jnp.concatenate(tokens + [zeros], axis=0)
    gated = (layer_norm(tail) * gain_ref[...] * gate_tail).astype(jnp.bfloat16)
    states = (token_tail + jnp.dot(gated, w_ref[...], preferred_element_type=jnp.float32)).astype(jnp.bfloat16)
    parts = [
        lax.dot_general(states, t_ref[...], (((1,), (1,)), ((), ())), preferred_element_type=jnp.float32)
        for t_ref in (ta_ref, tb_ref, tc_ref, td_ref, te_ref)
    ]
    parts[2:4] = [jnp.concatenate(parts[2:4], axis=1)]
    rows = [part[user : user + 1] for user in range(USERS) for part in parts]
    block = jnp.concatenate(rows + [jnp.zeros((4, 128), jnp.float32)], axis=0)
    for to in range(NSEQ):
        score_ref[to] = block


def layer_kernel(mixed_ref, gate_ref, x_ref, gain_ref, w_ref, out_ref):
    mixed = jnp.concatenate([mixed_ref[h, 0:ROW_E, :].astype(jnp.float32) for h in range(HEADS)], axis=1)
    gated = (layer_norm(mixed) * gain_ref[...] * gate_ref[...].astype(jnp.float32)).astype(jnp.bfloat16)
    out_ref[...] = (
        x_ref[...].astype(jnp.float32) + jnp.dot(gated, w_ref[...], preferred_element_type=jnp.float32)
    ).astype(jnp.bfloat16)


def pick_kernel(score_ref, place_ref, out_ref):
    scores = score_ref[...].reshape(NSEQ * 16, 128)
    row_at = lax.broadcasted_iota(jnp.int32, (NSEQ * 16, 64), 0)
    lane_at = lax.broadcasted_iota(jnp.int32, (128, 64), 0)
    for user in range(USERS):
        row, lane = place_ref[2 * user : 2 * user + 1, :], place_ref[2 * user + 1 : 2 * user + 2, :]
        found = jnp.dot(
            scores,
            (lane_at == lane).astype(jnp.float32),
            preferred_element_type=jnp.float32,
            precision=lax.Precision.HIGHEST,
        )
        out_ref[user : user + 1, :] = jnp.sum(jnp.where(row_at == row, found, 0.0), axis=0, keepdims=True)


def vmem():
    return pl.BlockSpec(memory_space=pltpu.VMEM)


def in_hbm(value):
    return pltpu.with_memory_space_constraint(value, pltpu.HBM)


def smem():
    return pl.BlockSpec(memory_space=pltpu.SMEM)


def dp_shift(value, move):
    return lax.ppermute(value, "dp", [(i, move(i)) for i in range(16)])


def seq_xor(value, apart):
    return lax.ppermute(value, "seq", [(i, i ^ apart) for i in range(NSEQ)])


def sds(shape, dtype=jnp.bfloat16):
    return jax.ShapeDtypeStruct(shape, dtype)


def cost(flops, read):
    return pl.CostEstimate(flops=flops, bytes_accessed=read, transcendentals=0)


def layer(
    tokens,
    in_gain,
    w_proj,
    out_gain,
    w_out,
    rab_slope,
    hist_blocks,
    hist_tail,
    node_table,
    subtree_map,
    beam_nodes,
):
    x_rows = tokens[0]
    seq = lax.axis_index("seq")
    mine = head_of(seq)

    normed, *far_sent = pl.pallas_call(
        project_far_kernel,
        in_specs=[vmem(), vmem(), pl.BlockSpec(memory_space=pltpu.HBM)],
        out_specs=[vmem()] * 5,
        out_shape=[sds((BLK, D))] + [sds((ROWS_A, HD))] * 4,
        scratch_shapes=[pltpu.VMEM((4, D, 3 * HD), jnp.bfloat16), pltpu.SemaphoreType.DMA((4, 3))],
        name="project_far",
        cost_estimate=cost(2 * BLK * D * 12 * HD, 4 << 20),
        compiler_params=GRANT,
    )(*(in_hbm(value) for value in (x_rows, in_gain[None, :], w_proj)))
    far_got = []
    for q, value in zip(FAR, far_sent):
        far_got.append(seq_xor(value, spread(q)))
    gate, extra, *near_sent = pl.pallas_call(
        project_near_kernel,
        in_specs=[smem(), smem(), vmem(), vmem(), vmem()],
        out_specs=[vmem()] * 6,
        out_shape=[pltpu.HBM((BLK, D), jnp.bfloat16), sds((16, HD))] + [sds((ROWS_A, HD))] * 4,
        name="project_near",
        cost_estimate=cost(2 * BLK * D * 20 * HD, 9 << 20),
        compiler_params=GRANT,
    )(hist_blocks, hist_tail, x_rows, normed, w_proj)
    near_got = [near_sent[0]]
    for q, value in zip(NEAR[1:], near_sent[1:]):
        near_got.append(seq_xor(value, spread(q)))

    bias, pairs, places = pl.pallas_call(
        prepare_kernel,
        in_specs=[smem(), smem(), vmem(), vmem()],
        out_specs=[vmem(), smem(), vmem()],
        out_shape=[
            sds((MAXD, BLK, BLK), jnp.float32),
            sds((2 * LIST,), jnp.int32),
            sds((8, 64), jnp.int32),
        ],
        name="prepare",
        cost_estimate=cost(1 << 28, 4 << 20),
        compiler_params=GRANT,
    )(hist_blocks, rab_slope, beam_nodes, subtree_map[None, :])

    def sort(got):
        return pl.pallas_call(
            sort_kernel,
            in_specs=[vmem()] * 4,
            out_specs=[vmem()] * 2,
            out_shape=[sds((4, ROW_Q, HD)), sds((4, BLK, HD))],
            cost_estimate=cost(1 << 10, 1 << 19),
            compiler_params=GRANT,
        )(*got)

    near_kv, near_q = sort(near_got)
    near_cross = seq_xor(near_kv, 4)
    far_kv, far_q = sort(far_got)
    far_cross = seq_xor(far_kv, 4)

    own = lax.dynamic_slice_in_dim(node_table, mine * 32, 32, 0)
    pair = jnp.concatenate([own, dp_shift(own, lambda i: i ^ 2)], axis=0)
    quad = jnp.concatenate([pair, dp_shift(pair, lambda i: i ^ 1)], axis=0)
    below = dp_shift(quad, lambda i: (i + 4) % 16)
    above = dp_shift(quad, lambda i: (i + 12) % 16)
    opposite_first = dp_shift(below[:64], lambda i: (i + 4) % 16)
    opposite_last = dp_shift(above[64:], lambda i: (i + 12) % 16)
    table = [quad, below, opposite_first, opposite_last, above]

    part, queries = pl.pallas_call(
        attend_first_kernel,
        in_specs=[smem()] + [vmem()] * 6,
        out_specs=[vmem(), vmem()],
        out_shape=[sds((8, BLK, HD), jnp.float32), sds((8, BLK, HD))],
        scratch_shapes=[pltpu.VMEM((12, ROW_Q, HD), jnp.bfloat16), pltpu.VMEM((9, BLK, HD), jnp.float32)],
        name="attend_first",
        cost_estimate=cost(1 << 31, 4 << 20),
        compiler_params=GRANT,
    )(pairs, bias, near_kv, far_kv, near_cross, near_q, far_q)

    back = pl.pallas_call(
        attend_last_kernel,
        in_specs=[smem()] * 3 + [vmem()] * 5,
        out_specs=vmem(),
        out_shape=sds((8, ROWS_B, HD)),
        scratch_shapes=[pltpu.VMEM((9, BLK, HD), jnp.float32)],
        name="attend_last",
        cost_estimate=cost(1 << 30, 2 << 20),
        compiler_params=GRANT,
    )(hist_blocks, hist_tail, pairs, bias, queries, far_cross, part, extra)

    mixed = lax.all_to_all(back, "seq", 0, 0, tiled=True, axis_index_groups=SETS)

    sent = pl.pallas_call(
        state_kernel,
        in_specs=[smem()] + [vmem()] * 8,
        out_specs=vmem(),
        out_shape=pltpu.HBM((NSEQ, 16, 128), jnp.float32),
        name="state",
        cost_estimate=cost(2 * 16 * D * D, 3 << 20),
        compiler_params=GRANT,
    )(hist_blocks, mixed, out_gain[None, :], w_out, *table)
    scores = lax.all_to_all(sent, "seq", 0, 0, tiled=True)

    layer_rows = pl.pallas_call(
        layer_kernel,
        in_specs=[vmem()] * 5,
        out_specs=vmem(),
        out_shape=sds((BLK, D)),
        name="layer",
        cost_estimate=cost(2 * BLK * D * D, 3 << 20),
        compiler_params=GRANT,
    )(mixed, gate, x_rows, out_gain[None, :], w_out)

    beam_scores = pl.pallas_call(
        pick_kernel,
        in_specs=[vmem()] * 2,
        out_specs=vmem(),
        out_shape=sds((USERS, 64), jnp.float32),
        name="pick",
        cost_estimate=cost(1 << 20, 1 << 17),
        compiler_params=GRANT,
    )(scores, places)
    return (layer_rows[None], beam_scores)


def solution(mesh):
    placed = (
        P("dp", "seq", None),
        P(),
        P(),
        P(),
        P(),
        P(),
        P("dp", None),
        P("dp", None),
        P("dp", None),
        P(),
        P("dp", "seq"),
    )
    return jax.shard_map(
        layer,
        mesh=mesh,
        in_specs=placed,
        out_specs=(P("dp", "seq", None), P("dp", "seq")),
        check_vma=False,
    )
```

```python
import jax
import jax.numpy as jnp
from jax import lax
from jax.experimental import pallas as pl
from jax.experimental.pallas import tpu as pltpu
from jax.sharding import PartitionSpec as P


BLK = 128
SUBT = 64
USERS = 3
D = 1024
HEADS = 8
HD = 128
NSEQ = 16
MAXD = 10
UNROLL = 4
MASKED = -1e30
ROW_K, ROW_V, ROW_Q, ROWS_A = 0, 128, 256, 384
ROW_E, ROW_X, ROWS_B = 128, 144, 160
FAR = (2, 3, 6, 7)
NEAR = (0, 1, 4, 5)
SETS = [[0, 1, 2, 3, 8, 9, 10, 11], [4, 5, 6, 7, 12, 13, 14, 15]]
LIST = 128
GRANT = pltpu.CompilerParams(vmem_limit_bytes=16 << 20)


def head_of(seq):
    return (seq // 8) * 4 + seq % 4


def set_of(seq):
    return (seq // 4) % 2


def spread(q):
    return (q // 4) * 8 + q % 4


def place_of(q):
    return q % 2 + (q // 4) * 2 + ((q // 2) % 2) * 4


def silu(x):
    half = 0.5 * x
    return half + half * jnp.tanh(half)


def layer_norm(rows):
    centred = rows - jnp.mean(rows, axis=-1, keepdims=True)
    spread_ = jnp.mean(centred * centred, axis=-1, keepdims=True)
    return centred * lax.rsqrt(spread_ + 1e-05)


def user_starts(blocks_ref):
    one = blocks_ref[0, 0]
    return (0, one, one + blocks_ref[0, 1])


def prepare(blocks_ref, slope_ref, ids_ref, map_ref, bias_ref, list_ref, place_ref):
    me, dp = lax.axis_index("seq"), lax.axis_index("dp")
    starts = user_starts(blocks_ref)
    slope = slope_ref[head_of(me)]
    offset = lax.broadcasted_iota(jnp.int32, (BLK, BLK), 0) - lax.broadcasted_iota(jnp.int32, (BLK, BLK), 1)
    for d in range(MAXD):
        gap = offset + d * BLK
        table = slope * jnp.log(jnp.maximum(gap + 1, 1).astype(jnp.float32))
        bias_ref[d] = jnp.where(gap >= 0, table, MASKED) if d == 0 else table

    def fill(t, counts):
        b = (t // 4) * 8 + set_of(me) * 4 + t % 4
        begin = jnp.where(b >= starts[2], starts[2], jnp.where(b >= starts[1], starts[1], 0))

        def put(j, counts):
            apart = j ^ me
            cross = (apart // 4) % 2
            q = (apart // 8) * 4 + apart % 4
            late = cross * ((q // 2) % 2)
            code = (place_of(t ^ head_of(me)) * 16 + cross * 8 + place_of(q)) * 16 + b - j
            first, second = counts
            list_ref[jnp.where(late == 1, LIST + second, first)] = code
            return (first + 1 - late, second + late)

        return lax.fori_loop(begin, b + 1, put, counts)

    counts = lax.fori_loop(0, 8, fill, (jnp.int32(0), jnp.int32(0)))
    for which, count in enumerate(counts):
        for pad in range(UNROLL - 1):
            list_ref[which * LIST + count + pad] = 8 * 256
        list_ref[which * LIST + LIST - 1] = (count + UNROLL - 1) // UNROLL

    my_x, my_zh, my_c = dp // 4, (dp // 2) % 2, dp % 2
    subtree = lax.broadcasted_iota(jnp.int32, (64, 64), 0)
    diagonal = subtree == lax.broadcasted_iota(jnp.int32, (64, 64), 1)
    places = jnp.sum(jnp.where(diagonal, map_ref[...], 0), axis=1, keepdims=True)
    for user in range(USERS):
        end = starts[user] + blocks_ref[0, user] - 1
        ids = ids_ref[user : user + 1, :]
        block = jnp.sum(jnp.where(subtree == ids // SUBT, places, 0), axis=0, keepdims=True)
        row = block * SUBT + ids % SUBT
        owner, inside = row // 256, row % 256
        shard, at = inside // 32, inside % 32
        x_rel = (my_x - owner // 4 + 4) % 4
        zh_rel = (my_zh - (owner // 2) % 2 + 2) % 2
        c_rel = (my_c - owner % 2 + 2) % 2
        lane = c_rel * 64 + zh_rel * 32 + at
        source = (shard // 4) * 8 + set_of(end) * 4 + shard % 4
        place_ref[2 * user : 2 * user + 1, :] = source * 16 + user * 4 + x_rel
        place_ref[2 * user + 1 : 2 * user + 2, :] = lane


def project_kernel(
    blocks_ref,
    tail_ref,
    slope_ref,
    ids_ref,
    map_ref,
    x_ref,
    gain_ref,
    w_ref,
    gate_ref,
    extra_ref,
    bias_ref,
    list_ref,
    place_ref,
    *refs,
):
    out_refs, weights, sems = refs[:HEADS], refs[HEADS], refs[HEADS + 1]
    me = lax.axis_index("seq")
    order = FAR + NEAR

    def copies(at):
        head = head_of(me) ^ order[at]
        return [
            pltpu.make_async_copy(
                w_ref.at[:, pl.ds(pl.multiple_of((group * HEADS + head) * HD, HD), HD)],
                weights.at[at, :, group * HD : (group + 1) * HD],
                sems.at[at, group],
            )
            for group in range(4)
        ]

    for at in range(HEADS):
        for copy in copies(at):
            copy.start()
    normed = (layer_norm(x_ref[...].astype(jnp.float32)) * gain_ref[...]).astype(jnp.bfloat16)
    prepare(blocks_ref, slope_ref, ids_ref, map_ref, bias_ref, list_ref, place_ref)
    for at, out_ref in enumerate(out_refs):
        for copy in copies(at):
            copy.wait()
        parts = silu(jnp.dot(normed, weights[at], preferred_element_type=jnp.float32))
        head = head_of(me) ^ order[at]
        gate_ref[:, pl.ds(pl.multiple_of(head * HD, HD), HD)] = parts[:, :HD].astype(jnp.bfloat16)
        out_ref[ROW_K:ROW_V, :] = parts[:, 2 * HD : 3 * HD].T.astype(jnp.bfloat16)
        out_ref[ROW_V:ROW_Q, :] = parts[:, 3 * HD :].astype(jnp.bfloat16)
        out_ref[ROW_Q:ROWS_A, :] = parts[:, HD : 2 * HD].astype(jnp.bfloat16)

    starts = user_starts(blocks_ref)
    last = jnp.int32(-1)
    for user in range(USERS):
        last = jnp.where(starts[user] + blocks_ref[0, user] - 1 == me, tail_ref[0, user] - 1, last)
    pick = (lax.broadcasted_iota(jnp.int32, (16, BLK), 1) == last).astype(jnp.bfloat16)
    gate_row = jnp.dot(pick, gate_ref[...], preferred_element_type=jnp.float32)[0:1]
    token_row = jnp.dot(pick, x_ref[...], preferred_element_type=jnp.float32)[0:1]
    pieces = [row[:, h * HD : (h + 1) * HD] for row in (gate_row, token_row) for h in range(HEADS)]
    extra_ref[...] = jnp.concatenate(pieces, axis=0).astype(jnp.bfloat16)


def run_pairs(list_ref, which, query, keys, values, bias_ref, acc):
    scale = HD ** (-0.5)

    def some(step, carry):
        products, targets = [], []
        for t in range(UNROLL):
            code = list_ref[which * LIST + step * UNROLL + t]
            mine, slot, d = code // 256, (code // 16) % 16, code % 16
            scores = jnp.dot(query(jnp.minimum(mine, 7)), keys(slot), preferred_element_type=jnp.float32)
            weights = silu(scores * scale + bias_ref[d]).astype(jnp.bfloat16)
            products.append(jnp.dot(weights, values(slot), preferred_element_type=jnp.float32))
            targets.append(mine)
        for mine, product in zip(targets, products):
            acc[mine] += product
        return carry

    lax.fori_loop(0, list_ref[which * LIST + LIST - 1], some, 0)


def sort_kernel(*refs):
    got_refs, kv_ref, queries_ref = refs[:4], refs[4], refs[5]
    for at, got_ref in enumerate(got_refs):
        kv_ref[at] = got_ref[ROW_K:ROW_Q, :]
        queries_ref[at] = got_ref[ROW_Q:ROWS_A, :]


def attend_first_kernel(
    list_ref, bias_ref, near_ref, far_ref, cross_ref, near_q_ref, far_q_ref, acc_ref, queries_ref, keep, acc
):
    for at in range(4):
        keep[at] = near_ref[at]
        keep[4 + at] = far_ref[at]
        keep[8 + at] = cross_ref[at]
        queries_ref[at] = near_q_ref[at]
        queries_ref[4 + at] = far_q_ref[at]
    acc[...] = jnp.zeros_like(acc)
    run_pairs(
        list_ref,
        0,
        lambda mine: queries_ref[mine],
        lambda slot: keep[slot, ROW_K:ROW_V, :],
        lambda slot: keep[slot, ROW_V:ROW_Q, :],
        bias_ref,
        acc,
    )
    acc_ref[...] = acc[0:8]


def attend_last_kernel(blocks_ref, tail_ref, list_ref, bias_ref, queries_ref, cross_ref, acc_ref, extra_ref, out_ref, acc):
    me = lax.axis_index("seq")
    mine = head_of(me)
    starts = user_starts(blocks_ref)
    acc[0:8] = acc_ref[...]
    acc[8] = jnp.zeros((BLK, HD), jnp.float32)

    def at(slot):
        return slot % 4

    run_pairs(
        list_ref,
        1,
        lambda own: queries_ref[own],
        lambda slot: cross_ref[at(slot), ROW_K:ROW_V, :],
        lambda slot: cross_ref[at(slot), ROW_V:ROW_Q, :],
        bias_ref,
        acc,
    )
    rows = []
    for user in range(USERS):
        end = starts[user] + blocks_ref[0, user] - 1
        here = set_of(end) == set_of(me)
        value = acc[place_of(head_of(end) ^ mine), pl.ds(tail_ref[0, user] - 1, 1), :]
        rows.append(jnp.where(here, value, 0.0))
    last = jnp.concatenate(rows + [jnp.zeros((16 - USERS, HD), jnp.float32)], axis=0).astype(jnp.bfloat16)
    row_at = lax.broadcasted_iota(jnp.int32, (BLK, HD), 0)
    for t in range(8):
        b = (t // 4) * 8 + set_of(me) * 4 + t % 4
        valid = jnp.int32(BLK)
        for user in range(USERS):
            valid = jnp.where(starts[user] + blocks_ref[0, user] - 1 == b, tail_ref[0, user], valid)
        out_ref[t, 0:ROW_E, :] = jnp.where(row_at < valid, acc[place_of(mine ^ t)], 0.0).astype(jnp.bfloat16)
        out_ref[t, ROW_E:ROW_X, :] = last
        out_ref[t, ROW_X:ROWS_B, :] = extra_ref[...]


def state_kernel(blocks_ref, mixed_ref, gain_ref, w_ref, ta_ref, tb_ref, tc_ref, td_ref, te_ref, score_ref):
    starts = user_starts(blocks_ref)
    tail = jnp.concatenate([mixed_ref[h, ROW_E:ROW_X, :].astype(jnp.float32) for h in range(HEADS)], axis=1)
    gates, tokens = [], []
    for user in range(USERS):
        end = starts[user] + blocks_ref[0, user] - 1
        rows = mixed_ref[head_of(end), ROW_X:ROWS_B, :].astype(jnp.float32)
        gates.append(jnp.concatenate([rows[h : h + 1] for h in range(HEADS)], axis=1))
        tokens.append(jnp.concatenate([rows[HEADS + h : HEADS + h + 1] for h in range(HEADS)], axis=1))
    zeros = jnp.zeros((16 - USERS, D), jnp.float32)
    gate_tail = jnp.concatenate(gates + [zeros], axis=0)
    token_tail = jnp.concatenate(tokens + [zeros], axis=0)
    gated = (layer_norm(tail) * gain_ref[...] * gate_tail).astype(jnp.bfloat16)
    states = (token_tail + jnp.dot(gated, w_ref[...], preferred_element_type=jnp.float32)).astype(jnp.bfloat16)
    parts = [
        lax.dot_general(states, t_ref[...], (((1,), (1,)), ((), ())), preferred_element_type=jnp.float32)
        for t_ref in (ta_ref, tb_ref, tc_ref, td_ref, te_ref)
    ]
    parts[2:4] = [jnp.concatenate(parts[2:4], axis=1)]
    rows = [part[user : user + 1] for user in range(USERS) for part in parts]
    block = jnp.concatenate(rows + [jnp.zeros((4, 128), jnp.float32)], axis=0)
    for to in range(NSEQ):
        score_ref[to] = block


def layer_kernel(mixed_ref, gate_ref, x_ref, gain_ref, w_ref, out_ref):
    mixed = jnp.concatenate([mixed_ref[h, 0:ROW_E, :].astype(jnp.float32) for h in range(HEADS)], axis=1)
    gated = (layer_norm(mixed) * gain_ref[...] * gate_ref[...].astype(jnp.float32)).astype(jnp.bfloat16)
    out_ref[...] = (
        x_ref[...].astype(jnp.float32) + jnp.dot(gated, w_ref[...], preferred_element_type=jnp.float32)
    ).astype(jnp.bfloat16)


def pick_kernel(score_ref, place_ref, out_ref):
    scores = score_ref[...].reshape(NSEQ * 16, 128)
    row_at = lax.broadcasted_iota(jnp.int32, (NSEQ * 16, 64), 0)
    lane_at = lax.broadcasted_iota(jnp.int32, (128, 64), 0)
    for user in range(USERS):
        row, lane = place_ref[2 * user : 2 * user + 1, :], place_ref[2 * user + 1 : 2 * user + 2, :]
        found = jnp.dot(
            scores,
            (lane_at == lane).astype(jnp.float32),
            preferred_element_type=jnp.float32,
            precision=lax.Precision.HIGHEST,
        )
        out_ref[user : user + 1, :] = jnp.sum(jnp.where(row_at == row, found, 0.0), axis=0, keepdims=True)


def vmem():
    return pl.BlockSpec(memory_space=pltpu.VMEM)


def in_hbm(value):
    return pltpu.with_memory_space_constraint(value, pltpu.HBM)


def smem():
    return pl.BlockSpec(memory_space=pltpu.SMEM)


def dp_shift(value, move):
    return lax.ppermute(value, "dp", [(i, move(i)) for i in range(16)])


def seq_xor(value, apart):
    return lax.ppermute(value, "seq", [(i, i ^ apart) for i in range(NSEQ)])


def sds(shape, dtype=jnp.bfloat16):
    return jax.ShapeDtypeStruct(shape, dtype)


def cost(flops, read):
    return pl.CostEstimate(flops=flops, bytes_accessed=read, transcendentals=0)


def layer(
    tokens,
    in_gain,
    w_proj,
    out_gain,
    w_out,
    rab_slope,
    hist_blocks,
    hist_tail,
    node_table,
    subtree_map,
    beam_nodes,
):
    x_rows = tokens[0]
    seq = lax.axis_index("seq")
    mine = head_of(seq)

    gate, extra, bias, pairs, places, *sent = pl.pallas_call(
        project_kernel,
        in_specs=[smem(), smem(), smem()] + [vmem()] * 4 + [pl.BlockSpec(memory_space=pltpu.HBM)],
        out_specs=[vmem()] * 3 + [smem()] + [vmem()] * (1 + HEADS),
        out_shape=[
            pltpu.HBM((BLK, D), jnp.bfloat16),
            sds((16, HD)),
            pltpu.HBM((MAXD, BLK, BLK), jnp.float32),
            sds((2 * LIST,), jnp.int32),
            sds((8, 64), jnp.int32),
        ]
        + [sds((ROWS_A, HD))] * HEADS,
        scratch_shapes=[pltpu.VMEM((HEADS, D, 4 * HD), jnp.bfloat16), pltpu.SemaphoreType.DMA((HEADS, 4))],
        name="project",
        cost_estimate=cost(2 * BLK * D * 4 * D, 10 << 20),
        compiler_params=GRANT,
    )(
        *(
            in_hbm(value)
            for value in (
                hist_blocks,
                hist_tail,
                rab_slope,
                beam_nodes,
                subtree_map[None, :],
                x_rows,
                in_gain[None, :],
                w_proj,
            )
        )
    )
    far_got, near_got = [], [sent[4]]
    for q, value in zip(FAR, sent[:4]):
        far_got.append(seq_xor(value, spread(q)))
    for q, value in zip(NEAR[1:], sent[5:]):
        near_got.append(seq_xor(value, spread(q)))

    def sort(got):
        return pl.pallas_call(
            sort_kernel,
            in_specs=[vmem()] * 4,
            out_specs=[vmem()] * 2,
            out_shape=[sds((4, ROW_Q, HD)), sds((4, BLK, HD))],
            cost_estimate=cost(1 << 10, 1 << 19),
            compiler_params=GRANT,
        )(*got)

    near_kv, near_q = sort(near_got)
    near_cross = seq_xor(near_kv, 4)
    far_kv, far_q = sort(far_got)
    far_cross = seq_xor(far_kv, 4)

    own = lax.dynamic_slice_in_dim(node_table, mine * 32, 32, 0)
    pair = jnp.concatenate([own, dp_shift(own, lambda i: i ^ 2)], axis=0)
    quad = jnp.concatenate([pair, dp_shift(pair, lambda i: i ^ 1)], axis=0)
    below = dp_shift(quad, lambda i: (i + 4) % 16)
    above = dp_shift(quad, lambda i: (i + 12) % 16)
    opposite_first = dp_shift(below[:64], lambda i: (i + 4) % 16)
    opposite_last = dp_shift(above[64:], lambda i: (i + 12) % 16)
    table = [quad, below, opposite_first, opposite_last, above]

    part, queries = pl.pallas_call(
        attend_first_kernel,
        in_specs=[smem()] + [vmem()] * 6,
        out_specs=[vmem(), vmem()],
        out_shape=[sds((8, BLK, HD), jnp.float32), sds((8, BLK, HD))],
        scratch_shapes=[pltpu.VMEM((12, ROW_Q, HD), jnp.bfloat16), pltpu.VMEM((9, BLK, HD), jnp.float32)],
        name="attend_first",
        cost_estimate=cost(1 << 31, 4 << 20),
        compiler_params=GRANT,
    )(pairs, bias, near_kv, far_kv, near_cross, near_q, far_q)

    back = pl.pallas_call(
        attend_last_kernel,
        in_specs=[smem()] * 3 + [vmem()] * 5,
        out_specs=vmem(),
        out_shape=sds((8, ROWS_B, HD)),
        scratch_shapes=[pltpu.VMEM((9, BLK, HD), jnp.float32)],
        name="attend_last",
        cost_estimate=cost(1 << 30, 2 << 20),
        compiler_params=GRANT,
    )(hist_blocks, hist_tail, pairs, bias, queries, far_cross, part, extra)

    mixed = lax.all_to_all(back, "seq", 0, 0, tiled=True, axis_index_groups=SETS)

    sent = pl.pallas_call(
        state_kernel,
        in_specs=[smem()] + [vmem()] * 8,
        out_specs=vmem(),
        out_shape=pltpu.HBM((NSEQ, 16, 128), jnp.float32),
        name="state",
        cost_estimate=cost(2 * 16 * D * D, 3 << 20),
        compiler_params=GRANT,
    )(hist_blocks, mixed, out_gain[None, :], w_out, *table)
    scores = lax.all_to_all(sent, "seq", 0, 0, tiled=True)

    layer_rows = pl.pallas_call(
        layer_kernel,
        in_specs=[vmem()] * 5,
        out_specs=vmem(),
        out_shape=sds((BLK, D)),
        name="layer",
        cost_estimate=cost(2 * BLK * D * D, 3 << 20),
        compiler_params=GRANT,
    )(mixed, gate, x_rows, out_gain[None, :], w_out)

    beam_scores = pl.pallas_call(
        pick_kernel,
        in_specs=[vmem()] * 2,
        out_specs=vmem(),
        out_shape=sds((USERS, 64), jnp.float32),
        name="pick",
        cost_estimate=cost(1 << 20, 1 << 17),
        compiler_params=GRANT,
    )(scores, places)
    return (layer_rows[None], beam_scores)


def solution(mesh):
    placed = (
        P("dp", "seq", None),
        P(),
        P(),
        P(),
        P(),
        P(),
        P("dp", None),
        P("dp", None),
        P("dp", None),
        P(),
        P("dp", "seq"),
    )
    return jax.shard_map(
        layer,
        mesh=mesh,
        in_specs=placed,
        out_specs=(P("dp", "seq", None), P("dp", "seq")),
        check_vma=False,
    )
```

```python
import jax
import jax.numpy as jnp
from jax import lax
from jax.experimental import pallas as pl
from jax.experimental.pallas import tpu as pltpu
from jax.sharding import PartitionSpec as P


BLK = 128
SUBT = 64
USERS = 3
D = 1024
HEADS = 8
HD = 128
NSEQ = 16
MAXD = 10
UNROLL = 4
MASKED = -1e30
ROW_K, ROW_V, ROW_Q, ROWS_A = 0, 128, 256, 384
ROW_E, ROW_X, ROWS_B = 128, 144, 160
FAR = (2, 3, 6, 7)
NEAR = (0, 1, 4, 5)
SETS = [[0, 1, 2, 3, 8, 9, 10, 11], [4, 5, 6, 7, 12, 13, 14, 15]]
LIST = 128
GRANT = pltpu.CompilerParams(vmem_limit_bytes=16 << 20)


def head_of(seq):
    return (seq // 8) * 4 + seq % 4


def set_of(seq):
    return (seq // 4) % 2


def spread(q):
    return (q // 4) * 8 + q % 4


def place_of(q):
    return q % 2 + (q // 4) * 2 + ((q // 2) % 2) * 4


def silu(x):
    half = 0.5 * x
    return half + half * jnp.tanh(half)


def layer_norm(rows):
    centred = rows - jnp.mean(rows, axis=-1, keepdims=True)
    spread_ = jnp.mean(centred * centred, axis=-1, keepdims=True)
    return centred * lax.rsqrt(spread_ + 1e-05)


def user_starts(blocks_ref):
    one = blocks_ref[0, 0]
    return (0, one, one + blocks_ref[0, 1])


def prepare_kernel(blocks_ref, slope_ref, ids_ref, map_ref, bias_ref, list_ref, place_ref):
    me, dp = lax.axis_index("seq"), lax.axis_index("dp")
    starts = user_starts(blocks_ref)
    slope = slope_ref[head_of(me)]
    offset = lax.broadcasted_iota(jnp.int32, (BLK, BLK), 0) - lax.broadcasted_iota(jnp.int32, (BLK, BLK), 1)
    for d in range(MAXD):
        gap = offset + d * BLK
        table = slope * jnp.log(jnp.maximum(gap + 1, 1).astype(jnp.float32))
        bias_ref[d] = jnp.where(gap >= 0, table, MASKED) if d == 0 else table

    def fill(t, counts):
        b = (t // 4) * 8 + set_of(me) * 4 + t % 4
        begin = jnp.where(b >= starts[2], starts[2], jnp.where(b >= starts[1], starts[1], 0))

        def put(j, counts):
            apart = j ^ me
            cross = (apart // 4) % 2
            q = (apart // 8) * 4 + apart % 4
            late = cross * ((q // 2) % 2)
            code = (place_of(t ^ head_of(me)) * 16 + cross * 8 + place_of(q)) * 16 + b - j
            first, second = counts
            list_ref[jnp.where(late == 1, LIST + second, first)] = code
            return (first + 1 - late, second + late)

        return lax.fori_loop(begin, b + 1, put, counts)

    counts = lax.fori_loop(0, 8, fill, (jnp.int32(0), jnp.int32(0)))
    for which, count in enumerate(counts):
        for pad in range(UNROLL - 1):
            list_ref[which * LIST + count + pad] = 8 * 256
        list_ref[which * LIST + LIST - 1] = (count + UNROLL - 1) // UNROLL

    my_x, my_zh, my_c = dp // 4, (dp // 2) % 2, dp % 2
    subtree = lax.broadcasted_iota(jnp.int32, (64, 64), 0)
    diagonal = subtree == lax.broadcasted_iota(jnp.int32, (64, 64), 1)
    places = jnp.sum(jnp.where(diagonal, map_ref[...], 0), axis=1, keepdims=True)
    for user in range(USERS):
        end = starts[user] + blocks_ref[0, user] - 1
        ids = ids_ref[user : user + 1, :]
        block = jnp.sum(jnp.where(subtree == ids // SUBT, places, 0), axis=0, keepdims=True)
        row = block * SUBT + ids % SUBT
        owner, inside = row // 256, row % 256
        shard, at = inside // 32, inside % 32
        x_rel = (my_x - owner // 4 + 4) % 4
        zh_rel = (my_zh - (owner // 2) % 2 + 2) % 2
        c_rel = (my_c - owner % 2 + 2) % 2
        lane = c_rel * 64 + zh_rel * 32 + at
        source = (shard // 4) * 8 + set_of(end) * 4 + shard % 4
        place_ref[2 * user : 2 * user + 1, :] = source * 16 + user * 4 + x_rel
        place_ref[2 * user + 1 : 2 * user + 2, :] = lane


def project_kernel(blocks_ref, tail_ref, x_ref, gain_ref, w_ref, gate_ref, extra_ref, *out_refs):
    me = lax.axis_index("seq")
    normed = (layer_norm(x_ref[...].astype(jnp.float32)) * gain_ref[...]).astype(jnp.bfloat16)
    for q, out_ref in zip(FAR + NEAR, out_refs):
        head = head_of(me) ^ q

        def part(group, head=head):
            columns = pl.ds(pl.multiple_of((group * HEADS + head) * HD, HD), HD)
            return silu(jnp.dot(normed, w_ref[:, columns], preferred_element_type=jnp.float32))

        out_ref[ROW_K:ROW_V, :] = part(2).T.astype(jnp.bfloat16)
        out_ref[ROW_V:ROW_Q, :] = part(3).astype(jnp.bfloat16)
        out_ref[ROW_Q:ROWS_A, :] = part(1).astype(jnp.bfloat16)
    gate = silu(jnp.dot(normed, w_ref[:, :D], preferred_element_type=jnp.float32)).astype(jnp.bfloat16)
    gate_ref[...] = gate

    starts = user_starts(blocks_ref)
    last = jnp.int32(-1)
    for user in range(USERS):
        last = jnp.where(starts[user] + blocks_ref[0, user] - 1 == me, tail_ref[0, user] - 1, last)
    pick = (lax.broadcasted_iota(jnp.int32, (16, BLK), 1) == last).astype(jnp.bfloat16)
    gate_row = jnp.dot(pick, gate, preferred_element_type=jnp.float32)[0:1]
    token_row = jnp.dot(pick, x_ref[...], preferred_element_type=jnp.float32)[0:1]
    pieces = [row[:, h * HD : (h + 1) * HD] for row in (gate_row, token_row) for h in range(HEADS)]
    extra_ref[...] = jnp.concatenate(pieces, axis=0).astype(jnp.bfloat16)


def run_pairs(list_ref, which, query, keys, values, bias_ref, acc):
    scale = HD ** (-0.5)

    def some(step, carry):
        products, targets = [], []
        for t in range(UNROLL):
            code = list_ref[which * LIST + step * UNROLL + t]
            mine, slot, d = code // 256, (code // 16) % 16, code % 16
            scores = jnp.dot(query(jnp.minimum(mine, 7)), keys(slot), preferred_element_type=jnp.float32)
            weights = silu(scores * scale + bias_ref[d]).astype(jnp.bfloat16)
            products.append(jnp.dot(weights, values(slot), preferred_element_type=jnp.float32))
            targets.append(mine)
        for mine, product in zip(targets, products):
            acc[mine] += product
        return carry

    lax.fori_loop(0, list_ref[which * LIST + LIST - 1], some, 0)


def sort_kernel(*refs):
    got_refs, kv_ref, queries_ref = refs[:4], refs[4], refs[5]
    for at, got_ref in enumerate(got_refs):
        kv_ref[at] = got_ref[ROW_K:ROW_Q, :]
        queries_ref[at] = got_ref[ROW_Q:ROWS_A, :]


def attend_first_kernel(
    list_ref, bias_ref, near_ref, far_ref, cross_ref, near_q_ref, far_q_ref, acc_ref, queries_ref, keep, acc
):
    for at in range(4):
        keep[at] = near_ref[at]
        keep[4 + at] = far_ref[at]
        keep[8 + at] = cross_ref[at]
        queries_ref[at] = near_q_ref[at]
        queries_ref[4 + at] = far_q_ref[at]
    acc[...] = jnp.zeros_like(acc)
    run_pairs(
        list_ref,
        0,
        lambda mine: queries_ref[mine],
        lambda slot: keep[slot, ROW_K:ROW_V, :],
        lambda slot: keep[slot, ROW_V:ROW_Q, :],
        bias_ref,
        acc,
    )
    acc_ref[...] = acc[0:8]


def attend_last_kernel(blocks_ref, tail_ref, list_ref, bias_ref, queries_ref, cross_ref, acc_ref, extra_ref, out_ref, acc):
    me = lax.axis_index("seq")
    mine = head_of(me)
    starts = user_starts(blocks_ref)
    acc[0:8] = acc_ref[...]
    acc[8] = jnp.zeros((BLK, HD), jnp.float32)

    def at(slot):
        return slot % 4

    run_pairs(
        list_ref,
        1,
        lambda own: queries_ref[own],
        lambda slot: cross_ref[at(slot), ROW_K:ROW_V, :],
        lambda slot: cross_ref[at(slot), ROW_V:ROW_Q, :],
        bias_ref,
        acc,
    )
    rows = []
    for user in range(USERS):
        end = starts[user] + blocks_ref[0, user] - 1
        here = set_of(end) == set_of(me)
        value = acc[place_of(head_of(end) ^ mine), pl.ds(tail_ref[0, user] - 1, 1), :]
        rows.append(jnp.where(here, value, 0.0))
    last = jnp.concatenate(rows + [jnp.zeros((16 - USERS, HD), jnp.float32)], axis=0).astype(jnp.bfloat16)
    row_at = lax.broadcasted_iota(jnp.int32, (BLK, HD), 0)
    for t in range(8):
        b = (t // 4) * 8 + set_of(me) * 4 + t % 4
        valid = jnp.int32(BLK)
        for user in range(USERS):
            valid = jnp.where(starts[user] + blocks_ref[0, user] - 1 == b, tail_ref[0, user], valid)
        out_ref[t, 0:ROW_E, :] = jnp.where(row_at < valid, acc[place_of(mine ^ t)], 0.0).astype(jnp.bfloat16)
        out_ref[t, ROW_E:ROW_X, :] = last
        out_ref[t, ROW_X:ROWS_B, :] = extra_ref[...]


def state_kernel(blocks_ref, mixed_ref, gain_ref, w_ref, ta_ref, tb_ref, tc_ref, td_ref, te_ref, score_ref):
    starts = user_starts(blocks_ref)
    tail = jnp.concatenate([mixed_ref[h, ROW_E:ROW_X, :].astype(jnp.float32) for h in range(HEADS)], axis=1)
    gates, tokens = [], []
    for user in range(USERS):
        end = starts[user] + blocks_ref[0, user] - 1
        rows = mixed_ref[head_of(end), ROW_X:ROWS_B, :].astype(jnp.float32)
        gates.append(jnp.concatenate([rows[h : h + 1] for h in range(HEADS)], axis=1))
        tokens.append(jnp.concatenate([rows[HEADS + h : HEADS + h + 1] for h in range(HEADS)], axis=1))
    zeros = jnp.zeros((16 - USERS, D), jnp.float32)
    gate_tail = jnp.concatenate(gates + [zeros], axis=0)
    token_tail = jnp.concatenate(tokens + [zeros], axis=0)
    gated = (layer_norm(tail) * gain_ref[...] * gate_tail).astype(jnp.bfloat16)
    states = (token_tail + jnp.dot(gated, w_ref[...], preferred_element_type=jnp.float32)).astype(jnp.bfloat16)
    parts = [
        lax.dot_general(states, t_ref[...], (((1,), (1,)), ((), ())), preferred_element_type=jnp.float32)
        for t_ref in (ta_ref, tb_ref, tc_ref, td_ref, te_ref)
    ]
    parts[2:4] = [jnp.concatenate(parts[2:4], axis=1)]
    rows = [part[user : user + 1] for user in range(USERS) for part in parts]
    block = jnp.concatenate(rows + [jnp.zeros((4, 128), jnp.float32)], axis=0)
    for to in range(NSEQ):
        score_ref[to] = block


def layer_kernel(mixed_ref, gate_ref, x_ref, gain_ref, w_ref, out_ref):
    mixed = jnp.concatenate([mixed_ref[h, 0:ROW_E, :].astype(jnp.float32) for h in range(HEADS)], axis=1)
    gated = (layer_norm(mixed) * gain_ref[...] * gate_ref[...].astype(jnp.float32)).astype(jnp.bfloat16)
    out_ref[...] = (
        x_ref[...].astype(jnp.float32) + jnp.dot(gated, w_ref[...], preferred_element_type=jnp.float32)
    ).astype(jnp.bfloat16)


def pick_kernel(score_ref, place_ref, out_ref):
    scores = score_ref[...].reshape(NSEQ * 16, 128)
    row_at = lax.broadcasted_iota(jnp.int32, (NSEQ * 16, 64), 0)
    lane_at = lax.broadcasted_iota(jnp.int32, (128, 64), 0)
    for user in range(USERS):
        row, lane = place_ref[2 * user : 2 * user + 1, :], place_ref[2 * user + 1 : 2 * user + 2, :]
        found = jnp.dot(
            scores,
            (lane_at == lane).astype(jnp.float32),
            preferred_element_type=jnp.float32,
            precision=lax.Precision.HIGHEST,
        )
        out_ref[user : user + 1, :] = jnp.sum(jnp.where(row_at == row, found, 0.0), axis=0, keepdims=True)


def vmem():
    return pl.BlockSpec(memory_space=pltpu.VMEM)


def in_hbm(value):
    return pltpu.with_memory_space_constraint(value, pltpu.HBM)


def smem():
    return pl.BlockSpec(memory_space=pltpu.SMEM)


def dp_shift(value, move):
    return lax.ppermute(value, "dp", [(i, move(i)) for i in range(16)])


def seq_xor(value, apart):
    return lax.ppermute(value, "seq", [(i, i ^ apart) for i in range(NSEQ)])


def sds(shape, dtype=jnp.bfloat16):
    return jax.ShapeDtypeStruct(shape, dtype)


def cost(flops, read):
    return pl.CostEstimate(flops=flops, bytes_accessed=read, transcendentals=0)


def layer(
    tokens,
    in_gain,
    w_proj,
    out_gain,
    w_out,
    rab_slope,
    hist_blocks,
    hist_tail,
    node_table,
    subtree_map,
    beam_nodes,
):
    x_rows = tokens[0]
    seq = lax.axis_index("seq")
    mine = head_of(seq)

    own = lax.dynamic_slice_in_dim(node_table, mine * 32, 32, 0)
    pair = jnp.concatenate([own, dp_shift(own, lambda i: i ^ 2)], axis=0)
    quad = jnp.concatenate([pair, dp_shift(pair, lambda i: i ^ 1)], axis=0)
    below = dp_shift(quad, lambda i: (i + 4) % 16)
    above = dp_shift(quad, lambda i: (i + 12) % 16)
    opposite_first = dp_shift(below[:64], lambda i: (i + 4) % 16)
    opposite_last = dp_shift(above[64:], lambda i: (i + 12) % 16)
    table = [quad, below, opposite_first, opposite_last, above]

    bias, pairs, places = pl.pallas_call(
        prepare_kernel,
        in_specs=[smem(), smem(), vmem(), vmem()],
        out_specs=[vmem(), smem(), vmem()],
        out_shape=[
            sds((MAXD, BLK, BLK), jnp.float32),
            sds((2 * LIST,), jnp.int32),
            sds((8, 64), jnp.int32),
        ],
        name="prepare",
        cost_estimate=cost(1 << 32, 1 << 24),
        compiler_params=GRANT,
    )(*(in_hbm(value) for value in (hist_blocks, rab_slope, beam_nodes, subtree_map[None, :])))
    x_here, _ = lax.optimization_barrier((x_rows, pairs))

    gate, extra, *sent = pl.pallas_call(
        project_kernel,
        in_specs=[smem(), smem()] + [vmem()] * 3,
        out_specs=[vmem()] * (2 + HEADS),
        out_shape=[pltpu.HBM((BLK, D), jnp.bfloat16), sds((16, HD))] + [sds((ROWS_A, HD))] * HEADS,
        name="project",
        cost_estimate=cost(2 * BLK * D * 4 * D, 10 << 20),
        compiler_params=GRANT,
    )(hist_blocks, hist_tail, x_here, in_gain[None, :], w_proj)
    far_got, near_got = [], [sent[4]]
    for q, value in zip(FAR, sent[:4]):
        far_got.append(seq_xor(value, spread(q)))
    for q, value in zip(NEAR[1:], sent[5:]):
        near_got.append(seq_xor(value, spread(q)))

    def sort(got):
        return pl.pallas_call(
            sort_kernel,
            in_specs=[vmem()] * 4,
            out_specs=[vmem()] * 2,
            out_shape=[sds((4, ROW_Q, HD)), sds((4, BLK, HD))],
            cost_estimate=cost(1 << 10, 1 << 19),
            compiler_params=GRANT,
        )(*got)

    near_kv, near_q = sort(near_got)
    near_cross = seq_xor(near_kv, 4)
    far_kv, far_q = sort(far_got)
    far_cross = seq_xor(far_kv, 4)

    part, queries = pl.pallas_call(
        attend_first_kernel,
        in_specs=[smem()] + [vmem()] * 6,
        out_specs=[vmem(), vmem()],
        out_shape=[sds((8, BLK, HD), jnp.float32), sds((8, BLK, HD))],
        scratch_shapes=[pltpu.VMEM((12, ROW_Q, HD), jnp.bfloat16), pltpu.VMEM((9, BLK, HD), jnp.float32)],
        name="attend_first",
        cost_estimate=cost(1 << 31, 4 << 20),
        compiler_params=GRANT,
    )(pairs, bias, near_kv, far_kv, near_cross, near_q, far_q)

    back = pl.pallas_call(
        attend_last_kernel,
        in_specs=[smem()] * 3 + [vmem()] * 5,
        out_specs=vmem(),
        out_shape=sds((8, ROWS_B, HD)),
        scratch_shapes=[pltpu.VMEM((9, BLK, HD), jnp.float32)],
        name="attend_last",
        cost_estimate=cost(1 << 30, 2 << 20),
        compiler_params=GRANT,
    )(hist_blocks, hist_tail, pairs, bias, queries, far_cross, part, extra)

    mixed = lax.all_to_all(back, "seq", 0, 0, tiled=True, axis_index_groups=SETS)

    sent = pl.pallas_call(
        state_kernel,
        in_specs=[smem()] + [vmem()] * 8,
        out_specs=vmem(),
        out_shape=pltpu.HBM((NSEQ, 16, 128), jnp.float32),
        name="state",
        cost_estimate=cost(2 * 16 * D * D, 3 << 20),
        compiler_params=GRANT,
    )(hist_blocks, mixed, out_gain[None, :], w_out, *table)
    scores = lax.all_to_all(sent, "seq", 0, 0, tiled=True)

    layer_rows = pl.pallas_call(
        layer_kernel,
        in_specs=[vmem()] * 5,
        out_specs=vmem(),
        out_shape=sds((BLK, D)),
        name="layer",
        cost_estimate=cost(2 * BLK * D * D, 3 << 20),
        compiler_params=GRANT,
    )(mixed, gate, x_rows, out_gain[None, :], w_out)

    beam_scores = pl.pallas_call(
        pick_kernel,
        in_specs=[vmem()] * 2,
        out_specs=vmem(),
        out_shape=sds((USERS, 64), jnp.float32),
        name="pick",
        cost_estimate=cost(1 << 20, 1 << 17),
        compiler_params=GRANT,
    )(scores, places)
    return (layer_rows[None], beam_scores)


def solution(mesh):
    placed = (
        P("dp", "seq", None),
        P(),
        P(),
        P(),
        P(),
        P(),
        P("dp", None),
        P("dp", None),
        P("dp", None),
        P(),
        P("dp", "seq"),
    )
    return jax.shard_map(
        layer,
        mesh=mesh,
        in_specs=placed,
        out_specs=(P("dp", "seq", None), P("dp", "seq")),
        check_vma=False,
    )
```

```python
import jax
import jax.numpy as jnp
from jax import lax
from jax.experimental import pallas as pl
from jax.experimental.pallas import tpu as pltpu
from jax.sharding import PartitionSpec as P


BLK = 128
SUBT = 64
USERS = 3
D = 1024
HEADS = 8
HD = 128
NSEQ = 16
MAXD = 10
UNROLL = 4
MASKED = -1e30
ROW_K, ROW_V, ROW_Q, ROWS_A = 0, 128, 256, 384
ROW_E, ROW_X, ROWS_B = 128, 144, 160
NEAR = (0, 1, 4)
LATE = (2, 3, 6, 7, 5)
PLACES = 0x65724310
SETS = [[0, 1, 2, 3, 8, 9, 10, 11], [4, 5, 6, 7, 12, 13, 14, 15]]
LIST = 128
GRANT = pltpu.CompilerParams(vmem_limit_bytes=16 << 20)


def head_of(seq):
    return (seq // 8) * 4 + seq % 4


def set_of(seq):
    return (seq // 4) % 2


def spread(q):
    return (q // 4) * 8 + q % 4


def place_of(q):
    return (PLACES >> (4 * q)) & 7


def silu(x):
    half = 0.5 * x
    return half + half * jnp.tanh(half)


def layer_norm(rows):
    centred = rows - jnp.mean(rows, axis=-1, keepdims=True)
    spread_ = jnp.mean(centred * centred, axis=-1, keepdims=True)
    return centred * lax.rsqrt(spread_ + 1e-05)


def user_starts(blocks_ref):
    one = blocks_ref[0, 0]
    return (0, one, one + blocks_ref[0, 1])


def prepare_kernel(blocks_ref, slope_ref, ids_ref, map_ref, bias_ref, list_ref, place_ref):
    me, dp = lax.axis_index("seq"), lax.axis_index("dp")
    starts = user_starts(blocks_ref)
    slope = slope_ref[head_of(me)]
    offset = lax.broadcasted_iota(jnp.int32, (BLK, BLK), 0) - lax.broadcasted_iota(jnp.int32, (BLK, BLK), 1)
    for d in range(MAXD):
        gap = offset + d * BLK
        table = slope * jnp.log(jnp.maximum(gap + 1, 1).astype(jnp.float32))
        bias_ref[d] = jnp.where(gap >= 0, table, MASKED) if d == 0 else table

    def fill(t, counts):
        b = (t // 4) * 8 + set_of(me) * 4 + t % 4
        begin = jnp.where(b >= starts[2], starts[2], jnp.where(b >= starts[1], starts[1], 0))

        def put(j, counts):
            apart = j ^ me
            cross = (apart // 4) % 2
            q = (apart // 8) * 4 + apart % 4
            late = cross * (place_of(q) >= len(NEAR)).astype(jnp.int32)
            code = (place_of(t ^ head_of(me)) * 16 + cross * 8 + place_of(q)) * 16 + b - j
            first, second = counts
            list_ref[jnp.where(late == 1, LIST + second, first)] = code
            return (first + 1 - late, second + late)

        return lax.fori_loop(begin, b + 1, put, counts)

    counts = lax.fori_loop(0, 8, fill, (jnp.int32(0), jnp.int32(0)))
    for which, count in enumerate(counts):
        for pad in range(UNROLL - 1):
            list_ref[which * LIST + count + pad] = 8 * 256
        list_ref[which * LIST + LIST - 1] = (count + UNROLL - 1) // UNROLL

    my_x, my_zh, my_c = dp // 4, (dp // 2) % 2, dp % 2
    subtree = lax.broadcasted_iota(jnp.int32, (64, 64), 0)
    diagonal = subtree == lax.broadcasted_iota(jnp.int32, (64, 64), 1)
    places = jnp.sum(jnp.where(diagonal, map_ref[...], 0), axis=1, keepdims=True)
    for user in range(USERS):
        end = starts[user] + blocks_ref[0, user] - 1
        ids = ids_ref[user : user + 1, :]
        block = jnp.sum(jnp.where(subtree == ids // SUBT, places, 0), axis=0, keepdims=True)
        row = block * SUBT + ids % SUBT
        owner, inside = row // 256, row % 256
        shard, at = inside // 32, inside % 32
        x_rel = (my_x - owner // 4 + 4) % 4
        zh_rel = (my_zh - (owner // 2) % 2 + 2) % 2
        c_rel = (my_c - owner % 2 + 2) % 2
        lane = c_rel * 64 + zh_rel * 32 + at
        source = (shard // 4) * 8 + set_of(end) * 4 + shard % 4
        place_ref[2 * user : 2 * user + 1, :] = source * 16 + user * 4 + x_rel
        place_ref[2 * user + 1 : 2 * user + 2, :] = lane


def project_kernel(blocks_ref, tail_ref, x_ref, gain_ref, w_ref, gate_ref, extra_ref, *out_refs):
    me = lax.axis_index("seq")
    normed = (layer_norm(x_ref[...].astype(jnp.float32)) * gain_ref[...]).astype(jnp.bfloat16)
    mine = head_of(me)
    outs = dict(zip(NEAR + LATE, out_refs))
    for q in (2, 6, 0, 4):
        odd = (mine ^ q) % 2 == 1

        def pair(group, q=q, odd=odd):
            first = (mine ^ q) // 2 * 2
            columns = pl.ds(pl.multiple_of((group * HEADS + first) * HD, 2 * HD), 2 * HD)
            both = silu(jnp.dot(normed, w_ref[:, columns], preferred_element_type=jnp.float32))
            low, high = both[:, :HD], both[:, HD:]
            return jnp.where(odd, high, low), jnp.where(odd, low, high)

        for here, key, value, query in zip((q, q + 1), pair(2), pair(3), pair(1)):
            outs[here][ROW_K:ROW_V, :] = key.T.astype(jnp.bfloat16)
            outs[here][ROW_V:ROW_Q, :] = value.astype(jnp.bfloat16)
            outs[here][ROW_Q:ROWS_A, :] = query.astype(jnp.bfloat16)
    gate = silu(jnp.dot(normed, w_ref[:, :D], preferred_element_type=jnp.float32)).astype(jnp.bfloat16)
    gate_ref[...] = gate

    starts = user_starts(blocks_ref)
    last = jnp.int32(-1)
    for user in range(USERS):
        last = jnp.where(starts[user] + blocks_ref[0, user] - 1 == me, tail_ref[0, user] - 1, last)
    pick = (lax.broadcasted_iota(jnp.int32, (16, BLK), 1) == last).astype(jnp.bfloat16)
    gate_row = jnp.dot(pick, gate, preferred_element_type=jnp.float32)[0:1]
    token_row = jnp.dot(pick, x_ref[...], preferred_element_type=jnp.float32)[0:1]
    pieces = [row[:, h * HD : (h + 1) * HD] for row in (gate_row, token_row) for h in range(HEADS)]
    extra_ref[...] = jnp.concatenate(pieces, axis=0).astype(jnp.bfloat16)


def run_pairs(list_ref, which, query, keys, values, bias_ref, acc):
    scale = HD ** (-0.5)

    def some(step, carry):
        products, targets = [], []
        for t in range(UNROLL):
            code = list_ref[which * LIST + step * UNROLL + t]
            mine, slot, d = code // 256, (code // 16) % 16, code % 16
            scores = jnp.dot(query(jnp.minimum(mine, 7)), keys(slot), preferred_element_type=jnp.float32)
            weights = silu(scores * scale + bias_ref[d]).astype(jnp.bfloat16)
            products.append(jnp.dot(weights, values(slot), preferred_element_type=jnp.float32))
            targets.append(mine)
        for mine, product in zip(targets, products):
            acc[mine] += product
        return carry

    lax.fori_loop(0, list_ref[which * LIST + LIST - 1], some, 0)


def sort_kernel(*refs):
    got_refs, kv_ref, queries_ref = refs[:-2], refs[-2], refs[-1]
    for at, got_ref in enumerate(got_refs):
        kv_ref[at] = got_ref[ROW_K:ROW_Q, :]
        queries_ref[at] = got_ref[ROW_Q:ROWS_A, :]


def attend_first_kernel(
    list_ref, bias_ref, near_ref, late_ref, cross_ref, near_q_ref, late_q_ref, acc_ref, queries_ref, keep, acc
):
    near, late = len(NEAR), len(LATE)
    for at in range(near):
        keep[at] = near_ref[at]
        keep[HEADS + at] = cross_ref[at]
        queries_ref[at] = near_q_ref[at]
    for at in range(late):
        keep[near + at] = late_ref[at]
        queries_ref[near + at] = late_q_ref[at]
    acc[...] = jnp.zeros_like(acc)
    run_pairs(
        list_ref,
        0,
        lambda mine: queries_ref[mine],
        lambda slot: keep[slot, ROW_K:ROW_V, :],
        lambda slot: keep[slot, ROW_V:ROW_Q, :],
        bias_ref,
        acc,
    )
    acc_ref[...] = acc[0:8]


def attend_last_kernel(blocks_ref, tail_ref, list_ref, bias_ref, queries_ref, cross_ref, acc_ref, extra_ref, out_ref, acc):
    me = lax.axis_index("seq")
    mine = head_of(me)
    starts = user_starts(blocks_ref)
    acc[0:8] = acc_ref[...]
    acc[8] = jnp.zeros((BLK, HD), jnp.float32)

    def at(slot):
        return jnp.maximum(slot - HEADS - len(NEAR), 0)

    run_pairs(
        list_ref,
        1,
        lambda own: queries_ref[own],
        lambda slot: cross_ref[at(slot), ROW_K:ROW_V, :],
        lambda slot: cross_ref[at(slot), ROW_V:ROW_Q, :],
        bias_ref,
        acc,
    )
    rows = []
    for user in range(USERS):
        end = starts[user] + blocks_ref[0, user] - 1
        here = set_of(end) == set_of(me)
        value = acc[place_of(head_of(end) ^ mine), pl.ds(tail_ref[0, user] - 1, 1), :]
        rows.append(jnp.where(here, value, 0.0))
    last = jnp.concatenate(rows + [jnp.zeros((16 - USERS, HD), jnp.float32)], axis=0).astype(jnp.bfloat16)
    row_at = lax.broadcasted_iota(jnp.int32, (BLK, HD), 0)
    for t in range(8):
        b = (t // 4) * 8 + set_of(me) * 4 + t % 4
        valid = jnp.int32(BLK)
        for user in range(USERS):
            valid = jnp.where(starts[user] + blocks_ref[0, user] - 1 == b, tail_ref[0, user], valid)
        out_ref[t, 0:ROW_E, :] = jnp.where(row_at < valid, acc[place_of(mine ^ t)], 0.0).astype(jnp.bfloat16)
        out_ref[t, ROW_E:ROW_X, :] = last
        out_ref[t, ROW_X:ROWS_B, :] = extra_ref[...]


def state_kernel(blocks_ref, mixed_ref, gain_ref, w_ref, ta_ref, tb_ref, tc_ref, td_ref, te_ref, score_ref):
    starts = user_starts(blocks_ref)
    tail = jnp.concatenate([mixed_ref[h, ROW_E:ROW_X, :].astype(jnp.float32) for h in range(HEADS)], axis=1)
    gates, tokens = [], []
    for user in range(USERS):
        end = starts[user] + blocks_ref[0, user] - 1
        rows = mixed_ref[head_of(end), ROW_X:ROWS_B, :].astype(jnp.float32)
        gates.append(jnp.concatenate([rows[h : h + 1] for h in range(HEADS)], axis=1))
        tokens.append(jnp.concatenate([rows[HEADS + h : HEADS + h + 1] for h in range(HEADS)], axis=1))
    zeros = jnp.zeros((16 - USERS, D), jnp.float32)
    gate_tail = jnp.concatenate(gates + [zeros], axis=0)
    token_tail = jnp.concatenate(tokens + [zeros], axis=0)
    gated = (layer_norm(tail) * gain_ref[...] * gate_tail).astype(jnp.bfloat16)
    states = (token_tail + jnp.dot(gated, w_ref[...], preferred_element_type=jnp.float32)).astype(jnp.bfloat16)
    parts = [
        lax.dot_general(states, t_ref[...], (((1,), (1,)), ((), ())), preferred_element_type=jnp.float32)
        for t_ref in (ta_ref, tb_ref, tc_ref, td_ref, te_ref)
    ]
    parts[2:4] = [jnp.concatenate(parts[2:4], axis=1)]
    rows = [part[user : user + 1] for user in range(USERS) for part in parts]
    block = jnp.concatenate(rows + [jnp.zeros((4, 128), jnp.float32)], axis=0)
    for to in range(NSEQ):
        score_ref[to] = block


def layer_kernel(mixed_ref, gate_ref, x_ref, gain_ref, w_ref, out_ref):
    mixed = jnp.concatenate([mixed_ref[h, 0:ROW_E, :].astype(jnp.float32) for h in range(HEADS)], axis=1)
    gated = (layer_norm(mixed) * gain_ref[...] * gate_ref[...].astype(jnp.float32)).astype(jnp.bfloat16)
    out_ref[...] = (
        x_ref[...].astype(jnp.float32) + jnp.dot(gated, w_ref[...], preferred_element_type=jnp.float32)
    ).astype(jnp.bfloat16)


def pick_kernel(score_ref, place_ref, out_ref):
    scores = score_ref[...].reshape(NSEQ * 16, 128)
    row_at = lax.broadcasted_iota(jnp.int32, (NSEQ * 16, 64), 0)
    lane_at = lax.broadcasted_iota(jnp.int32, (128, 64), 0)
    for user in range(USERS):
        row, lane = place_ref[2 * user : 2 * user + 1, :], place_ref[2 * user + 1 : 2 * user + 2, :]
        found = jnp.dot(
            scores,
            (lane_at == lane).astype(jnp.float32),
            preferred_element_type=jnp.float32,
            precision=lax.Precision.HIGHEST,
        )
        out_ref[user : user + 1, :] = jnp.sum(jnp.where(row_at == row, found, 0.0), axis=0, keepdims=True)


def vmem():
    return pl.BlockSpec(memory_space=pltpu.VMEM)


def in_hbm(value):
    return pltpu.with_memory_space_constraint(value, pltpu.HBM)


def smem():
    return pl.BlockSpec(memory_space=pltpu.SMEM)


def dp_shift(value, move):
    return lax.ppermute(value, "dp", [(i, move(i)) for i in range(16)])


def seq_xor(value, apart):
    return lax.ppermute(value, "seq", [(i, i ^ apart) for i in range(NSEQ)])


def sds(shape, dtype=jnp.bfloat16):
    return jax.ShapeDtypeStruct(shape, dtype)


def cost(flops, read):
    return pl.CostEstimate(flops=flops, bytes_accessed=read, transcendentals=0)


def layer(
    tokens,
    in_gain,
    w_proj,
    out_gain,
    w_out,
    rab_slope,
    hist_blocks,
    hist_tail,
    node_table,
    subtree_map,
    beam_nodes,
):
    x_rows = tokens[0]
    seq = lax.axis_index("seq")
    mine = head_of(seq)

    own = lax.dynamic_slice_in_dim(node_table, mine * 32, 32, 0)
    pair = jnp.concatenate([own, dp_shift(own, lambda i: i ^ 2)], axis=0)
    quad = jnp.concatenate([pair, dp_shift(pair, lambda i: i ^ 1)], axis=0)
    below = dp_shift(quad, lambda i: (i + 4) % 16)
    above = dp_shift(quad, lambda i: (i + 12) % 16)
    opposite_first = dp_shift(below[:64], lambda i: (i + 4) % 16)
    opposite_last = dp_shift(above[64:], lambda i: (i + 12) % 16)
    table = [quad, below, opposite_first, opposite_last, above]

    bias, pairs, places = pl.pallas_call(
        prepare_kernel,
        in_specs=[smem(), smem(), vmem(), vmem()],
        out_specs=[vmem(), smem(), vmem()],
        out_shape=[
            sds((MAXD, BLK, BLK), jnp.float32),
            sds((2 * LIST,), jnp.int32),
            sds((8, 64), jnp.int32),
        ],
        name="prepare",
        cost_estimate=cost(1 << 32, 1 << 24),
        compiler_params=GRANT,
    )(*(in_hbm(value) for value in (hist_blocks, rab_slope, beam_nodes, subtree_map[None, :])))
    x_here, _ = lax.optimization_barrier((x_rows, pairs))

    gate, extra, *sent = pl.pallas_call(
        project_kernel,
        in_specs=[smem(), smem()] + [vmem()] * 3,
        out_specs=[vmem()] * (2 + HEADS),
        out_shape=[pltpu.HBM((BLK, D), jnp.bfloat16), sds((16, HD))] + [sds((ROWS_A, HD))] * HEADS,
        name="project",
        cost_estimate=cost(2 * BLK * D * 4 * D, 10 << 20),
        compiler_params=GRANT,
    )(hist_blocks, hist_tail, x_here, in_gain[None, :], w_proj)
    got = []
    for q, value in zip(NEAR + LATE, sent):
        got.append(seq_xor(value, spread(q)) if q else value)

    def sort(got):
        return pl.pallas_call(
            sort_kernel,
            in_specs=[vmem()] * len(got),
            out_specs=[vmem()] * 2,
            out_shape=[sds((len(got), ROW_Q, HD)), sds((len(got), BLK, HD))],
            cost_estimate=cost(1 << 10, 1 << 19),
            compiler_params=GRANT,
        )(*got)

    near_kv, near_q = sort(got[: len(NEAR)])
    near_cross = seq_xor(near_kv, 4)
    late_kv, late_q = sort(got[len(NEAR) :])
    late_cross = seq_xor(late_kv, 4)

    part, queries = pl.pallas_call(
        attend_first_kernel,
        in_specs=[smem()] + [vmem()] * 6,
        out_specs=[vmem(), vmem()],
        out_shape=[sds((8, BLK, HD), jnp.float32), sds((8, BLK, HD))],
        scratch_shapes=[pltpu.VMEM((HEADS + len(NEAR), ROW_Q, HD), jnp.bfloat16), pltpu.VMEM((9, BLK, HD), jnp.float32)],
        name="attend_first",
        cost_estimate=cost(1 << 31, 4 << 20),
        compiler_params=GRANT,
    )(pairs, bias, near_kv, late_kv, near_cross, near_q, late_q)

    back = pl.pallas_call(
        attend_last_kernel,
        in_specs=[smem()] * 3 + [vmem()] * 5,
        out_specs=vmem(),
        out_shape=sds((8, ROWS_B, HD)),
        scratch_shapes=[pltpu.VMEM((9, BLK, HD), jnp.float32)],
        name="attend_last",
        cost_estimate=cost(1 << 30, 2 << 20),
        compiler_params=GRANT,
    )(hist_blocks, hist_tail, pairs, bias, queries, late_cross, part, extra)

    mixed = lax.all_to_all(back, "seq", 0, 0, tiled=True, axis_index_groups=SETS)

    sent = pl.pallas_call(
        state_kernel,
        in_specs=[smem()] + [vmem()] * 8,
        out_specs=vmem(),
        out_shape=pltpu.HBM((NSEQ, 16, 128), jnp.float32),
        name="state",
        cost_estimate=cost(2 * 16 * D * D, 3 << 20),
        compiler_params=GRANT,
    )(hist_blocks, mixed, out_gain[None, :], w_out, *table)
    scores = lax.all_to_all(sent, "seq", 0, 0, tiled=True)

    layer_rows = pl.pallas_call(
        layer_kernel,
        in_specs=[vmem()] * 5,
        out_specs=vmem(),
        out_shape=sds((BLK, D)),
        name="layer",
        cost_estimate=cost(2 * BLK * D * D, 3 << 20),
        compiler_params=GRANT,
    )(mixed, gate, x_rows, out_gain[None, :], w_out)

    beam_scores = pl.pallas_call(
        pick_kernel,
        in_specs=[vmem()] * 2,
        out_specs=vmem(),
        out_shape=sds((USERS, 64), jnp.float32),
        name="pick",
        cost_estimate=cost(1 << 20, 1 << 17),
        compiler_params=GRANT,
    )(scores, places)
    return (layer_rows[None], beam_scores)


def solution(mesh):
    placed = (
        P("dp", "seq", None),
        P(),
        P(),
        P(),
        P(),
        P(),
        P("dp", None),
        P("dp", None),
        P("dp", None),
        P(),
        P("dp", "seq"),
    )
    return jax.shard_map(
        layer,
        mesh=mesh,
        in_specs=placed,
        out_specs=(P("dp", "seq", None), P("dp", "seq")),
        check_vma=False,
    )
```

```python
import jax
import jax.numpy as jnp
from jax import lax
from jax.experimental import pallas as pl
from jax.experimental.pallas import tpu as pltpu
from jax.sharding import PartitionSpec as P


BLK = 128
SUBT = 64
USERS = 3
D = 1024
HEADS = 8
HD = 128
NSEQ = 16
MAXD = 10
UNROLL = 4
MASKED = -1e30
ROW_K, ROW_V, ROW_Q, ROWS_A = 0, 128, 256, 384
ROW_E, ROW_X, ROWS_B = 128, 144, 160
NEAR = (0, 1, 4)
LATE = (2, 3, 6, 7, 5)
PLACES = 0x65724310
SETS = [[0, 1, 2, 3, 8, 9, 10, 11], [4, 5, 6, 7, 12, 13, 14, 15]]
LIST = 128
GRANT = pltpu.CompilerParams(vmem_limit_bytes=16 << 20)


def head_of(seq):
    return (seq // 8) * 4 + seq % 4


def set_of(seq):
    return (seq // 4) % 2


def spread(q):
    return (q // 4) * 8 + q % 4


def place_of(q):
    return (PLACES >> (4 * q)) & 7


def silu(x):
    half = 0.5 * x
    return half + half * jnp.tanh(half)


def layer_norm(rows):
    centred = rows - jnp.mean(rows, axis=-1, keepdims=True)
    spread_ = jnp.mean(centred * centred, axis=-1, keepdims=True)
    return centred * lax.rsqrt(spread_ + 1e-05)


def user_starts(blocks_ref):
    one = blocks_ref[0, 0]
    return (0, one, one + blocks_ref[0, 1])


def bias_kernel(slope_ref, bias_ref):
    slope = slope_ref[head_of(lax.axis_index("seq"))]
    offset = lax.broadcasted_iota(jnp.int32, (BLK, BLK), 0) - lax.broadcasted_iota(jnp.int32, (BLK, BLK), 1)
    for d in range(MAXD):
        gap = offset + d * BLK
        table = slope * jnp.log(jnp.maximum(gap + 1, 1).astype(jnp.float32))
        bias_ref[d] = jnp.where(gap >= 0, table, MASKED) if d == 0 else table


def prepare_kernel(blocks_ref, ids_ref, map_ref, list_ref, place_ref):
    me, dp = lax.axis_index("seq"), lax.axis_index("dp")
    starts = user_starts(blocks_ref)

    def fill(t, counts):
        b = (t // 4) * 8 + set_of(me) * 4 + t % 4
        begin = jnp.where(b >= starts[2], starts[2], jnp.where(b >= starts[1], starts[1], 0))

        def put(j, counts):
            apart = j ^ me
            cross = (apart // 4) % 2
            q = (apart // 8) * 4 + apart % 4
            late = cross * (place_of(q) >= len(NEAR)).astype(jnp.int32)
            code = (place_of(t ^ head_of(me)) * 16 + cross * 8 + place_of(q)) * 16 + b - j
            first, second = counts
            list_ref[jnp.where(late == 1, LIST + second, first)] = code
            return (first + 1 - late, second + late)

        return lax.fori_loop(begin, b + 1, put, counts)

    counts = lax.fori_loop(0, 8, fill, (jnp.int32(0), jnp.int32(0)))
    for which, count in enumerate(counts):
        for pad in range(UNROLL - 1):
            list_ref[which * LIST + count + pad] = 8 * 256
        list_ref[which * LIST + LIST - 1] = (count + UNROLL - 1) // UNROLL

    my_x, my_zh, my_c = dp // 4, (dp // 2) % 2, dp % 2
    subtree = lax.broadcasted_iota(jnp.int32, (64, 64), 0)
    diagonal = subtree == lax.broadcasted_iota(jnp.int32, (64, 64), 1)
    places = jnp.sum(jnp.where(diagonal, map_ref[...], 0), axis=1, keepdims=True)
    for user in range(USERS):
        end = starts[user] + blocks_ref[0, user] - 1
        ids = ids_ref[user : user + 1, :]
        block = jnp.sum(jnp.where(subtree == ids // SUBT, places, 0), axis=0, keepdims=True)
        row = block * SUBT + ids % SUBT
        owner, inside = row // 256, row % 256
        shard, at = inside // 32, inside % 32
        x_rel = (my_x - owner // 4 + 4) % 4
        zh_rel = (my_zh - (owner // 2) % 2 + 2) % 2
        c_rel = (my_c - owner % 2 + 2) % 2
        lane = c_rel * 64 + zh_rel * 32 + at
        source = (shard // 4) * 8 + set_of(end) * 4 + shard % 4
        place_ref[2 * user : 2 * user + 1, :] = source * 16 + user * 4 + x_rel
        place_ref[2 * user + 1 : 2 * user + 2, :] = lane


def project_kernel(blocks_ref, tail_ref, x_ref, gain_ref, w_ref, gate_ref, extra_ref, *out_refs):
    me = lax.axis_index("seq")
    normed = (layer_norm(x_ref[...].astype(jnp.float32)) * gain_ref[...]).astype(jnp.bfloat16)
    mine = head_of(me)
    outs = dict(zip(NEAR + LATE, out_refs))
    for q in (2, 6, 0, 4):
        odd = (mine ^ q) % 2 == 1

        def pair(group, q=q, odd=odd):
            first = (mine ^ q) // 2 * 2
            columns = pl.ds(pl.multiple_of((group * HEADS + first) * HD, 2 * HD), 2 * HD)
            both = silu(jnp.dot(normed, w_ref[:, columns], preferred_element_type=jnp.float32))
            low, high = both[:, :HD], both[:, HD:]
            return jnp.where(odd, high, low), jnp.where(odd, low, high)

        for here, key, value, query in zip((q, q + 1), pair(2), pair(3), pair(1)):
            outs[here][ROW_K:ROW_V, :] = key.T.astype(jnp.bfloat16)
            outs[here][ROW_V:ROW_Q, :] = value.astype(jnp.bfloat16)
            outs[here][ROW_Q:ROWS_A, :] = query.astype(jnp.bfloat16)
    gate = silu(jnp.dot(normed, w_ref[:, :D], preferred_element_type=jnp.float32)).astype(jnp.bfloat16)
    gate_ref[...] = gate

    starts = user_starts(blocks_ref)
    last = jnp.int32(-1)
    for user in range(USERS):
        last = jnp.where(starts[user] + blocks_ref[0, user] - 1 == me, tail_ref[0, user] - 1, last)
    pick = (lax.broadcasted_iota(jnp.int32, (16, BLK), 1) == last).astype(jnp.bfloat16)
    gate_row = jnp.dot(pick, gate, preferred_element_type=jnp.float32)[0:1]
    token_row = jnp.dot(pick, x_ref[...], preferred_element_type=jnp.float32)[0:1]
    pieces = [row[:, h * HD : (h + 1) * HD] for row in (gate_row, token_row) for h in range(HEADS)]
    extra_ref[...] = jnp.concatenate(pieces, axis=0).astype(jnp.bfloat16)


def run_pairs(list_ref, which, query, keys, values, bias_ref, acc):
    scale = HD ** (-0.5)

    def some(step, carry):
        products, targets = [], []
        for t in range(UNROLL):
            code = list_ref[which * LIST + step * UNROLL + t]
            mine, slot, d = code // 256, (code // 16) % 16, code % 16
            scores = jnp.dot(query(jnp.minimum(mine, 7)), keys(slot), preferred_element_type=jnp.float32)
            weights = silu(scores * scale + bias_ref[d]).astype(jnp.bfloat16)
            products.append(jnp.dot(weights, values(slot), preferred_element_type=jnp.float32))
            targets.append(mine)
        for mine, product in zip(targets, products):
            acc[mine] += product
        return carry

    lax.fori_loop(0, list_ref[which * LIST + LIST - 1], some, 0)


def sort_kernel(*refs):
    got_refs, kv_ref, queries_ref = refs[:-2], refs[-2], refs[-1]
    for at, got_ref in enumerate(got_refs):
        kv_ref[at] = got_ref[ROW_K:ROW_Q, :]
        queries_ref[at] = got_ref[ROW_Q:ROWS_A, :]


def attend_first_kernel(
    list_ref, bias_ref, near_ref, late_ref, cross_ref, near_q_ref, late_q_ref, acc_ref, queries_ref, keep, acc
):
    near, late = len(NEAR), len(LATE)
    for at in range(near):
        keep[at] = near_ref[at]
        keep[HEADS + at] = cross_ref[at]
        queries_ref[at] = near_q_ref[at]
    for at in range(late):
        keep[near + at] = late_ref[at]
        queries_ref[near + at] = late_q_ref[at]
    acc[...] = jnp.zeros_like(acc)
    run_pairs(
        list_ref,
        0,
        lambda mine: queries_ref[mine],
        lambda slot: keep[slot, ROW_K:ROW_V, :],
        lambda slot: keep[slot, ROW_V:ROW_Q, :],
        bias_ref,
        acc,
    )
    acc_ref[...] = acc[0:8]


def attend_last_kernel(blocks_ref, tail_ref, list_ref, bias_ref, queries_ref, cross_ref, acc_ref, extra_ref, out_ref, acc):
    me = lax.axis_index("seq")
    mine = head_of(me)
    starts = user_starts(blocks_ref)
    acc[0:8] = acc_ref[...]
    acc[8] = jnp.zeros((BLK, HD), jnp.float32)

    def at(slot):
        return jnp.maximum(slot - HEADS - len(NEAR), 0)

    run_pairs(
        list_ref,
        1,
        lambda own: queries_ref[own],
        lambda slot: cross_ref[at(slot), ROW_K:ROW_V, :],
        lambda slot: cross_ref[at(slot), ROW_V:ROW_Q, :],
        bias_ref,
        acc,
    )
    rows = []
    for user in range(USERS):
        end = starts[user] + blocks_ref[0, user] - 1
        here = set_of(end) == set_of(me)
        value = acc[place_of(head_of(end) ^ mine), pl.ds(tail_ref[0, user] - 1, 1), :]
        rows.append(jnp.where(here, value, 0.0))
    last = jnp.concatenate(rows + [jnp.zeros((16 - USERS, HD), jnp.float32)], axis=0).astype(jnp.bfloat16)
    row_at = lax.broadcasted_iota(jnp.int32, (BLK, HD), 0)
    for t in range(8):
        b = (t // 4) * 8 + set_of(me) * 4 + t % 4
        valid = jnp.int32(BLK)
        for user in range(USERS):
            valid = jnp.where(starts[user] + blocks_ref[0, user] - 1 == b, tail_ref[0, user], valid)
        out_ref[t, 0:ROW_E, :] = jnp.where(row_at < valid, acc[place_of(mine ^ t)], 0.0).astype(jnp.bfloat16)
        out_ref[t, ROW_E:ROW_X, :] = last
        out_ref[t, ROW_X:ROWS_B, :] = extra_ref[...]


def state_kernel(blocks_ref, mixed_ref, gain_ref, w_ref, ta_ref, tb_ref, tc_ref, td_ref, te_ref, score_ref):
    starts = user_starts(blocks_ref)
    tail = jnp.concatenate([mixed_ref[h, ROW_E:ROW_X, :].astype(jnp.float32) for h in range(HEADS)], axis=1)
    gates, tokens = [], []
    for user in range(USERS):
        end = starts[user] + blocks_ref[0, user] - 1
        rows = mixed_ref[head_of(end), ROW_X:ROWS_B, :].astype(jnp.float32)
        gates.append(jnp.concatenate([rows[h : h + 1] for h in range(HEADS)], axis=1))
        tokens.append(jnp.concatenate([rows[HEADS + h : HEADS + h + 1] for h in range(HEADS)], axis=1))
    zeros = jnp.zeros((16 - USERS, D), jnp.float32)
    gate_tail = jnp.concatenate(gates + [zeros], axis=0)
    token_tail = jnp.concatenate(tokens + [zeros], axis=0)
    gated = (layer_norm(tail) * gain_ref[...] * gate_tail).astype(jnp.bfloat16)
    states = (token_tail + jnp.dot(gated, w_ref[...], preferred_element_type=jnp.float32)).astype(jnp.bfloat16)
    parts = [
        lax.dot_general(states, t_ref[...], (((1,), (1,)), ((), ())), preferred_element_type=jnp.float32)
        for t_ref in (ta_ref, tb_ref, tc_ref, td_ref, te_ref)
    ]
    parts[2:4] = [jnp.concatenate(parts[2:4], axis=1)]
    rows = [part[user : user + 1] for user in range(USERS) for part in parts]
    block = jnp.concatenate(rows + [jnp.zeros((4, 128), jnp.float32)], axis=0)
    for to in range(NSEQ):
        score_ref[to] = block


def layer_kernel(mixed_ref, gate_ref, x_ref, gain_ref, w_ref, out_ref):
    mixed = jnp.concatenate([mixed_ref[h, 0:ROW_E, :].astype(jnp.float32) for h in range(HEADS)], axis=1)
    gated = (layer_norm(mixed) * gain_ref[...] * gate_ref[...].astype(jnp.float32)).astype(jnp.bfloat16)
    out_ref[...] = (
        x_ref[...].astype(jnp.float32) + jnp.dot(gated, w_ref[...], preferred_element_type=jnp.float32)
    ).astype(jnp.bfloat16)


def pick_kernel(score_ref, place_ref, out_ref):
    scores = score_ref[...].reshape(NSEQ * 16, 128)
    row_at = lax.broadcasted_iota(jnp.int32, (NSEQ * 16, 64), 0)
    lane_at = lax.broadcasted_iota(jnp.int32, (128, 64), 0)
    lanes = [place_ref[2 * user + 1 : 2 * user + 2, :] for user in range(USERS)]
    hot = jnp.concatenate([(lane_at == lane).astype(jnp.float32) for lane in lanes], axis=1)
    found = jnp.dot(scores, hot, preferred_element_type=jnp.float32, precision=lax.Precision.HIGHEST)
    for user in range(USERS):
        mine = jnp.where(row_at == place_ref[2 * user : 2 * user + 1, :], found[:, user * 64 : (user + 1) * 64], 0.0)
        out_ref[user : user + 1, :] = jnp.sum(mine, axis=0, keepdims=True)


def vmem():
    return pl.BlockSpec(memory_space=pltpu.VMEM)


def in_hbm(value):
    return pltpu.with_memory_space_constraint(value, pltpu.HBM)


def smem():
    return pl.BlockSpec(memory_space=pltpu.SMEM)


def dp_shift(value, move):
    return lax.ppermute(value, "dp", [(i, move(i)) for i in range(16)])


def seq_xor(value, apart):
    return lax.ppermute(value, "seq", [(i, i ^ apart) for i in range(NSEQ)])


def sds(shape, dtype=jnp.bfloat16):
    return jax.ShapeDtypeStruct(shape, dtype)


def cost(flops, read):
    return pl.CostEstimate(flops=flops, bytes_accessed=read, transcendentals=0)


def layer(
    tokens,
    in_gain,
    w_proj,
    out_gain,
    w_out,
    rab_slope,
    hist_blocks,
    hist_tail,
    node_table,
    subtree_map,
    beam_nodes,
):
    x_rows = tokens[0]
    seq = lax.axis_index("seq")
    mine = head_of(seq)

    own = lax.dynamic_slice_in_dim(node_table, mine * 32, 32, 0)
    pair = jnp.concatenate([own, dp_shift(own, lambda i: i ^ 2)], axis=0)
    quad = jnp.concatenate([pair, dp_shift(pair, lambda i: i ^ 1)], axis=0)
    below = dp_shift(quad, lambda i: (i + 4) % 16)
    above = dp_shift(quad, lambda i: (i + 12) % 16)
    opposite_first = dp_shift(below[:64], lambda i: (i + 4) % 16)
    opposite_last = dp_shift(above[64:], lambda i: (i + 12) % 16)
    table = [quad, below, opposite_first, opposite_last, above]

    pairs, places = pl.pallas_call(
        prepare_kernel,
        in_specs=[smem(), vmem(), vmem()],
        out_specs=[smem(), vmem()],
        out_shape=[sds((2 * LIST,), jnp.int32), sds((8, 64), jnp.int32)],
        name="prepare",
        cost_estimate=cost(1 << 32, 1 << 24),
        compiler_params=GRANT,
    )(*(in_hbm(value) for value in (hist_blocks, beam_nodes, subtree_map[None, :])))
    x_here, _ = lax.optimization_barrier((x_rows, pairs))

    gate, extra, *sent = pl.pallas_call(
        project_kernel,
        in_specs=[smem(), smem()] + [vmem()] * 3,
        out_specs=[vmem()] * (2 + HEADS),
        out_shape=[pltpu.HBM((BLK, D), jnp.bfloat16), sds((16, HD))] + [sds((ROWS_A, HD))] * HEADS,
        name="project",
        cost_estimate=cost(2 * BLK * D * 4 * D, 10 << 20),
        compiler_params=GRANT,
    )(hist_blocks, hist_tail, x_here, in_gain[None, :], w_proj)
    got = []
    for q, value in zip(NEAR + LATE, sent):
        got.append(seq_xor(value, spread(q)) if q else value)

    def sort(got):
        return pl.pallas_call(
            sort_kernel,
            in_specs=[vmem()] * len(got),
            out_specs=[vmem()] * 2,
            out_shape=[sds((len(got), ROW_Q, HD)), sds((len(got), BLK, HD))],
            cost_estimate=cost(1 << 10, 1 << 19),
            compiler_params=GRANT,
        )(*got)

    near_kv, near_q = sort(got[: len(NEAR)])
    near_cross = seq_xor(near_kv, 4)
    late_kv, late_q = sort(got[len(NEAR) :])
    late_cross = seq_xor(late_kv, 4)

    bias = pl.pallas_call(
        bias_kernel,
        in_specs=[smem()],
        out_specs=vmem(),
        out_shape=sds((MAXD, BLK, BLK), jnp.float32),
        name="bias",
        cost_estimate=cost(1 << 28, 1 << 20),
        compiler_params=GRANT,
    )(rab_slope)
    part, queries = pl.pallas_call(
        attend_first_kernel,
        in_specs=[smem()] + [vmem()] * 6,
        out_specs=[vmem(), vmem()],
        out_shape=[sds((8, BLK, HD), jnp.float32), sds((8, BLK, HD))],
        scratch_shapes=[pltpu.VMEM((HEADS + len(NEAR), ROW_Q, HD), jnp.bfloat16), pltpu.VMEM((9, BLK, HD), jnp.float32)],
        name="attend_first",
        cost_estimate=cost(1 << 31, 4 << 20),
        compiler_params=GRANT,
    )(pairs, bias, near_kv, late_kv, near_cross, near_q, late_q)

    back = pl.pallas_call(
        attend_last_kernel,
        in_specs=[smem()] * 3 + [vmem()] * 5,
        out_specs=vmem(),
        out_shape=sds((8, ROWS_B, HD)),
        scratch_shapes=[pltpu.VMEM((9, BLK, HD), jnp.float32)],
        name="attend_last",
        cost_estimate=cost(1 << 30, 2 << 20),
        compiler_params=GRANT,
    )(hist_blocks, hist_tail, pairs, bias, queries, late_cross, part, extra)

    mixed = lax.all_to_all(back, "seq", 0, 0, tiled=True, axis_index_groups=SETS)

    sent = pl.pallas_call(
        state_kernel,
        in_specs=[smem()] + [vmem()] * 8,
        out_specs=vmem(),
        out_shape=pltpu.HBM((NSEQ, 16, 128), jnp.float32),
        name="state",
        cost_estimate=cost(2 * 16 * D * D, 3 << 20),
        compiler_params=GRANT,
    )(hist_blocks, mixed, out_gain[None, :], w_out, *table)
    scores = lax.all_to_all(sent, "seq", 0, 0, tiled=True)

    layer_rows = pl.pallas_call(
        layer_kernel,
        in_specs=[vmem()] * 5,
        out_specs=vmem(),
        out_shape=sds((BLK, D)),
        name="layer",
        cost_estimate=cost(2 * BLK * D * D, 3 << 20),
        compiler_params=GRANT,
    )(mixed, gate, x_rows, out_gain[None, :], w_out)

    beam_scores = pl.pallas_call(
        pick_kernel,
        in_specs=[vmem()] * 2,
        out_specs=vmem(),
        out_shape=sds((USERS, 64), jnp.float32),
        name="pick",
        cost_estimate=cost(1 << 20, 1 << 17),
        compiler_params=GRANT,
    )(scores, places)
    return (layer_rows[None], beam_scores)


def solution(mesh):
    placed = (
        P("dp", "seq", None),
        P(),
        P(),
        P(),
        P(),
        P(),
        P("dp", None),
        P("dp", None),
        P("dp", None),
        P(),
        P("dp", "seq"),
    )
    return jax.shard_map(
        layer,
        mesh=mesh,
        in_specs=placed,
        out_specs=(P("dp", "seq", None), P("dp", "seq")),
        check_vma=False,
    )
```
